32 devices in a mesh: wave: 8 (over z, core), lev: 4 (over y, x).
Axes of the slice: x: 2, y: 2, z: 4, core: 2. Of those that a mesh axis runs over, the one named last changes fastest.
Arguments:
- spectrum: bfloat16 [4, 4, 2, 1280, 1280], P(None, 'lev', None, 'wave'), may hold values from -6 to 6
- legendre: bfloat16 [1280, 8, 1280], P('wave'), may hold values from -0.15625 to 0.15625
- order_of_slot: int32 [1280], replicated, may hold values from 0 to 1279, each once
- reduced_length: int32 [8], replicated, may hold values from 20 to 5136, as said below
- gauss_weight: float32 [8], P('wave'), may hold values from 2 to 6
- depart_row: int32 [2, 4, 4, 8, 5632], P(None, 'lev', None, 'wave'), may hold values from -1 to 1, as said below
- depart_col: int32 [2, 4, 4, 8, 5632], P(None, 'lev', None, 'wave'), may hold values from 0 to 5135, as said below
- depart_weight: float32 [2, 4, 4, 8, 5632], P(None, 'lev', None, 'wave'), may hold values from 0.05 to 0.5
Outputs:
- spectrum_out: bfloat16 [4, 4, 2, 1280, 1280], P(None, 'lev', None, 'wave')
The draws below stay inside these ranges and needn't reach their ends.
Inputs may be any that keep to these rules, and one draw needn't show every extreme that they name: `reduced_length`: each latitude j has 20 + 4 i points for a cycle i with j * 160 <= i < (j + 1) * 160; the last latitude has 5136. `depart_row`: offset of the departure latitude from the arrival latitude; a departure latitude outside the window reads zeros. `depart_col`: below the reduced length of the departure latitude (of the nearest window latitude where it lies outside the window). `order_of_slot`: A permutation of the zonal orders.
All inputs are finite; a program needn't handle non-finite values.
Results may differ from the reference program's by a relative error of at most 0.02.
Values may be sent and summed in bfloat16 or wider, within the bound.
A program may use at most 128 MiB of HBM per device.

```python
import math
import jax
import jax.numpy as jnp
from jax import lax

ORDERS = 1280
VARS = 4
STEPS = 2
STENCIL = 4
BLOCK = 512
LAT = 8
LEVELS = 4
GRID = 5632


def cycle_lengths(key):
    stride = ORDERS // LAT
    cycle_offset = jax.random.randint(jax.random.fold_in(key, 11), (LAT,), 0, stride)
    cycle_index = jnp.arange(LAT, dtype=jnp.int32) * stride + cycle_offset
    cycle_index = cycle_index.at[LAT - 1].set(ORDERS - 1)
    return (20 + 4 * cycle_index).astype(jnp.int32)


def offsets_of(key):
    array_shape = (STEPS, LEVELS, STENCIL, LAT, GRID)
    offsets = jax.random.randint(jax.random.fold_in(key, 12), array_shape, -1, 2)
    offsets = offsets.at[..., 0].set(0).at[..., 1].set(-1).at[..., 2].set(1)
    return offsets.astype(jnp.int32)


def draw_reduced_length(key, part):
    return cycle_lengths(key)


def draw_depart_row(key, part):
    return offsets_of(key)


def draw_depart_col(key, part):
    array_shape = (STEPS, LEVELS, STENCIL, LAT, GRID)
    lengths = cycle_lengths(key)
    offsets = offsets_of(key)
    target = jnp.clip(jnp.arange(LAT, dtype=jnp.int32)[:, None] + offsets, 0, LAT - 1)
    row_length = lengths[target]
    fraction = jax.random.randint(jax.random.fold_in(key, 13), array_shape, 0, 262144)
    columns = fraction * row_length // 262144
    columns = columns.at[..., 0].set(row_length[..., 0] - 1)
    return columns.astype(jnp.int32)


def steps_of(own_key, dims, split, smallest, largest):
    def one(position, blocks):
        draws = jax.random.uniform(jax.random.fold_in(jax.random.fold_in(own_key, 6), position), (blocks,), jnp.float32, smallest / len(split), largest / len(split))
        return jnp.repeat(jnp.exp(draws), dims[position] // blocks).reshape((-1,) + (1,) * (len(dims) - position - 1))

    gain = one(*split[0])
    for cut in split[1:]:
        gain = gain * one(*cut)
    return gain


def bell_draw(own_key, extent, width, reach, cuts=(), kind=jnp.bfloat16):
    level = steps_of(own_key, extent, cuts, -0.22, 0.18) if cuts else 1.0
    array = jax.random.normal(own_key, extent, jnp.float32) * width * level
    return jnp.minimum(jnp.maximum(array, -reach), reach).astype(kind)


def setup_inputs(seed: int = 0) -> dict:
    arg_keys = jax.random.split(jax.random.key(seed), 9)
    return {
        "spectrum": bell_draw(arg_keys[0], (VARS, LEVELS, 2, ORDERS, ORDERS), 1.0, 6.0, ((1, 4), (3, 8))),
        "legendre": bell_draw(arg_keys[1], (ORDERS, LAT, ORDERS), ORDERS ** -0.5, 0.15625, ((0, 8),)),
        "order_of_slot": jax.random.permutation(arg_keys[2], ORDERS).astype(jnp.int32),
        "reduced_length": draw_reduced_length(jax.random.fold_in(arg_keys[8], 71), 0),
        "gauss_weight": jnp.clip(2.0 + 4.0 * jax.random.uniform(arg_keys[4], (LAT,), jnp.float32) ** steps_of(arg_keys[4], (LAT,), ((0, 8),), -0.2, 0.2), 2.0, 6.0),
        "depart_row": draw_depart_row(jax.random.fold_in(arg_keys[8], 71), 0),
        "depart_col": draw_depart_col(jax.random.fold_in(arg_keys[8], 71), 0),
        "depart_weight": jnp.clip(0.05 + 0.45 * jax.random.uniform(arg_keys[7], (STEPS, LEVELS, STENCIL, LAT, GRID), jnp.float32) ** steps_of(arg_keys[7], (STEPS, LEVELS, STENCIL, LAT, GRID), ((1, 4), (3, 8)), -0.2, 0.2), 0.05, 0.5),
    }


full_turn = 2.0 * math.pi

def base_table(length, orders, order_limit):
    offsets = jnp.arange(BLOCK, dtype=jnp.int32)
    phases = orders[:, None] * offsets[None, :] % length
    angles = phases.astype(jnp.float32) * (jnp.float32(full_turn) / length.astype(jnp.float32))
    active = (orders < order_limit)[:, None]
    cosine = jnp.where(active, jnp.cos(angles), 0.0)
    sine_part = jnp.where(active, -jnp.sin(angles), 0.0)
    return jnp.concatenate([cosine, sine_part], axis=0).astype(jnp.bfloat16)

def block_phases(length, orders):
    starts = jnp.arange(GRID // BLOCK, dtype=jnp.int32) * BLOCK
    phases = starts[:, None] * orders[None, :] % length
    angles = phases.astype(jnp.float32) * (jnp.float32(full_turn) / length.astype(jnp.float32))
    return (jnp.cos(angles), jnp.sin(angles))

def synthesize(coeffs, length, order_limit, fourier_table, cos_phase, sin_phase):
    field_count = coeffs.shape[0]
    blocks = cos_phase.shape[0]
    real_part = coeffs[:, 0, :].astype(jnp.float32)[:, None, :]
    imag_part = coeffs[:, 1, :].astype(jnp.float32)[:, None, :]
    rot_real = real_part * cos_phase[None] - imag_part * sin_phase[None]
    rot_imag = real_part * sin_phase[None] + imag_part * cos_phase[None]
    rotated = jnp.stack([rot_real, rot_imag], axis=2).astype(jnp.bfloat16)
    rotated = rotated.reshape(field_count * blocks, -1)
    result = jnp.dot(rotated.astype(jnp.float32), fourier_table.astype(jnp.float32), preferred_element_type=jnp.float32)
    result = result.reshape(field_count, blocks * BLOCK)
    points = jnp.arange(blocks * BLOCK, dtype=jnp.int32)
    factor = 1.0 / jnp.sqrt(order_limit.astype(jnp.float32))
    return jnp.where(points[None, :] < length, result * factor, 0.0)

def analyse(newgrid, fourier_table, cos_phase, sin_phase):
    field_count = newgrid.shape[0]
    blocks = cos_phase.shape[0]
    partial_value = jnp.dot(newgrid.reshape(field_count * blocks, BLOCK).astype(jnp.float32), fourier_table.astype(jnp.float32).T, preferred_element_type=jnp.float32)
    partial_value = partial_value.reshape(field_count, blocks, 2, -1)
    part_real = partial_value[:, :, 0, :]
    part_imag = partial_value[:, :, 1, :]
    real_sum = lax.optimization_barrier(jnp.sum(part_real * cos_phase[None] + part_imag * sin_phase[None], axis=1))
    imag_sum = lax.optimization_barrier(jnp.sum(part_imag * cos_phase[None] - part_real * sin_phase[None], axis=1))
    return jnp.stack([real_sum, imag_sum], axis=1)

def reference(spectrum, legendre, order_of_slot, reduced_length, gauss_weight, depart_row, depart_col, depart_weight):
    degrees = jnp.arange(ORDERS, dtype=jnp.int32)
    masked = jnp.where(degrees[None, None, :] >= order_of_slot[:, None, None], legendre.astype(jnp.float32), 0.0)
    limits = jnp.minimum(ORDERS, (reduced_length - 1) // 2)
    latitudes = jnp.arange(LAT, dtype=jnp.int32)
    points = jnp.arange(GRID, dtype=jnp.int32)
    field_count = VARS * LEVELS
    spectral_state = spectrum

    def synth_level(level_state):
        return jnp.einsum('vcsn,sjn->jvcs', level_state.astype(jnp.float32), masked).astype(jnp.bfloat16)

    def analyse_level(level_coeffs):
        return jnp.einsum('jvcs,sjn->vcsn', level_coeffs.astype(jnp.float32), masked).astype(jnp.bfloat16)

    def grid_of(mapped):
        coeffs, length, order_limit = mapped
        fourier_table = base_table(length, order_of_slot, order_limit)
        cos_phase, sin_phase = block_phases(length, order_of_slot)
        return synthesize(coeffs, length, order_limit, fourier_table, cos_phase, sin_phase)

    def coeffs_of(mapped):
        rows_grid, length, order_limit, weight = mapped
        fourier_table = base_table(length, order_of_slot, order_limit)
        cos_phase, sin_phase = block_phases(length, order_of_slot)
        sums = analyse(rows_grid, fourier_table, cos_phase, sin_phase)
        return (sums * (weight * jnp.sqrt(2.0 / length.astype(jnp.float32)))).astype(jnp.bfloat16)

    def interp_level(mapped):
        flat_rows, row_offsets, columns, weights = mapped
        flat_index = (latitudes[None, :, None] + 1 + row_offsets) * GRID + columns
        values = flat_rows[:, flat_index.reshape(-1)].reshape(VARS, STENCIL, LAT, GRID)
        return lax.optimization_barrier(jnp.sum(values * weights[None], axis=1))
    for step_index in range(STEPS):
        fourier = lax.map(synth_level, jnp.moveaxis(spectral_state, 1, 0))
        fourier = jnp.transpose(fourier, (1, 2, 0, 3, 4)).reshape(LAT, field_count, 2, ORDERS)
        gridpoints = lax.map(grid_of, (fourier, reduced_length, limits))
        gridpoints = jnp.transpose(gridpoints.reshape(LAT, VARS, LEVELS, GRID), (2, 1, 0, 3))
        padded = jnp.pad(gridpoints, ((0, 0), (0, 0), (1, 1), (0, 0))).reshape(LEVELS, VARS, (LAT + 2) * GRID)
        interp = lax.map(interp_level, (padded, depart_row[step_index], depart_col[step_index], depart_weight[step_index]))
        tendency = interp + 0.5 * jnp.roll(interp, -1, axis=1) * jnp.tanh(jnp.roll(interp, -2, axis=1))
        newgrid = jnp.where(points[None, None, None, :] < reduced_length[None, None, :, None], tendency, 0.0).astype(jnp.bfloat16)
        newgrid = jnp.transpose(newgrid, (2, 1, 0, 3)).reshape(LAT, field_count, GRID)
        coeffs = lax.map(coeffs_of, (newgrid, reduced_length, limits, gauss_weight))
        coeffs = coeffs.reshape(LAT, VARS, LEVELS, 2, ORDERS)
        spectral_state = jnp.moveaxis(lax.map(analyse_level, jnp.moveaxis(coeffs, 2, 0)), 0, 1)
    return spectral_state
```

```python
import functools
import math

import jax
import jax.numpy as jnp
from jax import lax
from jax.experimental import pallas as pl
from jax.experimental.pallas import tpu as pltpu
from jax.sharding import PartitionSpec as P

BLOCK = 512
RADIX = 8
FULL_TURN = 2.0 * math.pi
F32 = jnp.float32
BF16 = jnp.bfloat16

VMEM_SPEC = pl.BlockSpec(memory_space=pltpu.VMEM)
SMEM_SPEC = pl.BlockSpec(memory_space=pltpu.SMEM)


def padded_blocks(grid_width):
    return -(-(grid_width // BLOCK) // 16) * 16


def phase_rows(length, orders, blocks):
    digits = jnp.arange(RADIX, dtype=jnp.int32)
    steps = [digits, digits * RADIX, digits * RADIX * RADIX]
    steps.append(jnp.arange(blocks, dtype=jnp.int32) * BLOCK)
    steps = jnp.concatenate(steps)
    phases = steps[:, None] * orders[None, :] % length
    angles = phases.astype(F32) * (jnp.float32(FULL_TURN) / length.astype(F32))
    return jnp.cos(angles), jnp.sin(angles)


def build_table(cos_ref, sin_ref, active_ref, fc_ref, fs_ref, ca_ref, sa_ref):
    active = active_ref[...]
    cos_low = cos_ref[0:RADIX, :] * active
    sin_low = sin_ref[0:RADIX, :] * active
    cos_mid = cos_ref[RADIX : 2 * RADIX, :]
    sin_mid = sin_ref[RADIX : 2 * RADIX, :]
    for a in range(RADIX):
        c = cos_ref[2 * RADIX + a : 2 * RADIX + a + 1, :]
        s = sin_ref[2 * RADIX + a : 2 * RADIX + a + 1, :]
        ca_ref[a * RADIX : (a + 1) * RADIX, :] = c * cos_mid - s * sin_mid
        sa_ref[a * RADIX : (a + 1) * RADIX, :] = s * cos_mid + c * sin_mid

    def body(i, carry):
        cos_parts, sin_parts = [], []
        for k in range(2):
            c = ca_ref[pl.ds(2 * i + k, 1), :]
            s = sa_ref[pl.ds(2 * i + k, 1), :]
            cos_parts.append(c * cos_low - s * sin_low)
            sin_parts.append(-(s * cos_low + c * sin_low))
        rows = pl.ds(pl.multiple_of(i * 2 * RADIX, 2 * RADIX), 2 * RADIX)
        fc_ref[rows, :] = jnp.concatenate(cos_parts, axis=0).astype(BF16)
        fs_ref[rows, :] = jnp.concatenate(sin_parts, axis=0).astype(BF16)
        return carry

    lax.fori_loop(0, RADIX * RADIX // 2, body, 0)


def synthesize(coeffs, cos_block, sin_block, fc_ref, fs_ref, length, scale):
    fields = coeffs.shape[0] // 2
    blocks = cos_block.shape[0]
    reals, imags = [], []
    for v in range(fields):
        real = coeffs[2 * v : 2 * v + 1]
        imag = coeffs[2 * v + 1 : 2 * v + 2]
        reals.append((real * cos_block - imag * sin_block).astype(BF16))
        imags.append((real * sin_block + imag * cos_block).astype(BF16))
    dims = (((1,), (1,)), ((), ()))
    out = lax.dot_general(
        jnp.concatenate(reals, axis=0), fc_ref[...], dims, preferred_element_type=F32
    ) + lax.dot_general(
        jnp.concatenate(imags, axis=0), fs_ref[...], dims, preferred_element_type=F32
    )
    row = lax.broadcasted_iota(jnp.int32, out.shape, 0) % blocks
    point = row * BLOCK + lax.broadcasted_iota(jnp.int32, out.shape, 1)
    return jnp.where(point < length, out * scale, 0.0)


def synth_kernel(blocks, coef_ref, cos_ref, sin_ref, fc_ref, fs_ref, len_ref, scale_ref, out_ref):
    out_ref[...] = synthesize(
        coef_ref[...].astype(F32),
        cos_ref[3 * RADIX : 3 * RADIX + blocks, :],
        sin_ref[3 * RADIX : 3 * RADIX + blocks, :],
        fc_ref,
        fs_ref,
        len_ref[0],
        scale_ref[0],
    ).astype(BF16)


def gather_block(b, k, table, row_ref, col_ref, weight_ref, fields, blocks):
    stencil = col_ref.shape[1]
    half = 256
    lanes = pl.ds(pl.multiple_of(b * BLOCK, BLOCK), BLOCK)
    iota_half = lax.broadcasted_iota(jnp.int32, (half, BLOCK), 0).astype(F32).astype(BF16)
    iota_rows = lax.broadcasted_iota(jnp.int32, (3 * blocks, BLOCK), 0)
    one = jnp.ones((), BF16)
    zero = jnp.zeros((), BF16)
    acc = [jnp.zeros((blocks, BLOCK), F32) for _ in range(fields)]
    for p in range(stencil):
        col = col_ref[k, p, :, lanes]
        row = row_ref[k, p, :, lanes]
        weight = weight_ref[k, p, :, lanes]
        point = col % BLOCK
        halves = []
        for h in range(BLOCK // half):
            local = point - h * half
            key = jnp.where((local >= 0) & (local < half), local, -1).astype(F32).astype(BF16)
            halves.append(jnp.where(iota_half == key, one, zero))
        onehot = jnp.concatenate(halves, axis=0)
        found = jnp.dot(table, onehot, preferred_element_type=F32)
        which = (row + 1) * blocks + col // BLOCK
        chosen = jnp.where(iota_rows == which, weight, 0.0)
        for r in range(3):
            sel = chosen[r * blocks : (r + 1) * blocks]
            for v in range(fields):
                start = (r * fields + v) * blocks
                acc[v] = acc[v] + found[start : start + blocks] * sel
    return [jnp.sum(a, axis=0, keepdims=True) for a in acc]


def advance(table, k, row_ref, col_ref, weight_ref, new_ref, length, fields, blocks, real_blocks):
    new_ref[...] = jnp.zeros_like(new_ref)

    def body(b, carry):
        interp = gather_block(b, k, table, row_ref, col_ref, weight_ref, fields, blocks)
        point = b * BLOCK + lax.broadcasted_iota(jnp.int32, (1, BLOCK), 1)
        for v in range(fields):
            value = interp[v] + 0.5 * interp[(v + 1) % fields] * jnp.tanh(interp[(v + 2) % fields])
            new_ref[pl.ds(v * blocks + b, 1), :] = jnp.where(point < length, value, 0.0)
        return carry

    lax.fori_loop(0, real_blocks, body, 0)


def analyse(new_ref, cos_block, sin_block, fc_ref, fs_ref, scale):
    blocks = cos_block.shape[0]
    fields = new_ref.shape[0] // blocks
    newgrid = new_ref[...].astype(BF16)
    part_real = jnp.dot(newgrid, fc_ref[...], preferred_element_type=F32)
    part_imag = jnp.dot(newgrid, fs_ref[...], preferred_element_type=F32)
    out = []
    for v in range(fields):
        pr = part_real[v * blocks : (v + 1) * blocks]
        pi = part_imag[v * blocks : (v + 1) * blocks]
        real = jnp.sum(pr * cos_block + pi * sin_block, axis=0, keepdims=True)
        imag = jnp.sum(pi * cos_block - pr * sin_block, axis=0, keepdims=True)
        out += [real * scale, imag * scale]
    return out


def grid_kernel(
    fields, blocks, real_blocks,
    table_ref, row_ref, col_ref, weight_ref, cos_ref, sin_ref, fc_ref, fs_ref, len_ref, scale_ref,
    out_ref, new_ref,
):
    advance(
        table_ref[...], 0, row_ref, col_ref, weight_ref, new_ref, len_ref[0],
        fields, blocks, real_blocks,
    )
    rows = analyse(
        new_ref,
        cos_ref[3 * RADIX : 3 * RADIX + blocks, :],
        sin_ref[3 * RADIX : 3 * RADIX + blocks, :],
        fc_ref,
        fs_ref,
        scale_ref[0],
    )
    out_ref[...] = jnp.concatenate(rows, axis=0).astype(BF16)


HALF = 256


def fill_phases(orders, length, cos_ref, sin_ref):
    limit = length.astype(F32)
    inverse = 1.0 / jnp.full(orders.shape, limit)
    turn = FULL_TURN / jnp.full(orders.shape, limit)
    digit = lax.broadcasted_iota(jnp.int32, (RADIX, orders.shape[1]), 0)
    for t in range(cos_ref.shape[0] // RADIX):
        if t < 3:
            step = digit * RADIX**t
        else:
            step = (digit + (t - 3) * RADIX) * BLOCK
        product = step * orders
        rest = product - jnp.floor(product.astype(F32) * inverse).astype(jnp.int32) * length
        rest = jnp.where(rest < 0, rest + length, rest)
        rest = jnp.where(rest >= length, rest - length, rest)
        angle = rest.astype(F32) * turn
        cos_ref[t * RADIX : (t + 1) * RADIX, :] = jnp.cos(angle)
        sin_ref[t * RADIX : (t + 1) * RADIX, :] = jnp.sin(angle)


def grid_rows(coeffs, cos_block, sin_block, fc_ref, fs_ref, length, scale):
    fields = coeffs.shape[0] // 2
    blocks = cos_block.shape[0]
    reals, imags = [], []
    for v in range(fields):
        real = coeffs[2 * v : 2 * v + 1]
        imag = coeffs[2 * v + 1 : 2 * v + 2]
        reals.append((real * cos_block - imag * sin_block).astype(BF16))
        imags.append((real * sin_block + imag * cos_block).astype(BF16))
    dims = (((1,), (1,)), ((), ()))
    out = lax.dot_general(
        fc_ref[...], jnp.concatenate(reals, axis=0), dims, preferred_element_type=F32
    ) + lax.dot_general(
        fs_ref[...], jnp.concatenate(imags, axis=0), dims, preferred_element_type=F32
    )
    out = out.T
    row = lax.broadcasted_iota(jnp.int32, out.shape, 0) % blocks
    point = row * BLOCK + lax.broadcasted_iota(jnp.int32, out.shape, 1)
    out = jnp.where(point < length, out * scale, 0.0)
    parts = []
    for v in range(fields):
        rows = out[v * blocks : (v + 1) * blocks]
        parts += [rows[:8, :HALF], rows[:8, HALF:], rows[8:12, :HALF], rows[8:12, HALF:]]
    return jnp.concatenate(parts, axis=0)


def pick_block(b, k, table, row_ref, col_ref, weight_ref, fields):
    stencil = col_ref.shape[1]
    lanes = pl.ds(pl.multiple_of(b * BLOCK, BLOCK), BLOCK)
    iota = lax.broadcasted_iota(jnp.int32, (HALF, BLOCK), 0).astype(F32).astype(BF16)
    sub = lax.broadcasted_iota(jnp.int32, (8, BLOCK), 0)
    one = jnp.ones((), BF16)
    zero = jnp.zeros((), BF16)
    acc = [jnp.zeros((8, BLOCK), F32) for _ in range(fields)]
    for p in range(stencil):
        col = col_ref[k, p, :, lanes]
        row = row_ref[k, p, :, lanes]
        weight = weight_ref[k, p, :, lanes]
        key = (col & (HALF - 1)).astype(F32).astype(BF16)
        onehot = jnp.where(iota == key, one, zero)
        found = jnp.dot(table, onehot, preferred_element_type=F32)
        big = col // BLOCK
        side = (col // HALF) & 1
        which = (row + 1) * 24 + jnp.where(big < 8, side * 8 + big, 8 + side * 4 + big)
        got = [jnp.zeros((8, BLOCK), F32) for _ in range(fields)]
        for r in range(3):
            for t in range(3):
                hit = sub == which - (r * 24 + t * 8)
                for v in range(fields):
                    start = (r * fields + v) * 24 + t * 8
                    got[v] = jnp.where(hit, found[start : start + 8], got[v])
        for v in range(fields):
            acc[v] = acc[v] + got[v] * weight
    return [jnp.sum(a, axis=0, keepdims=True) for a in acc]


def advance_fast(table, k, row_ref, col_ref, weight_ref, new_ref, length, fields, blocks, real_blocks):
    new_ref[...] = jnp.zeros_like(new_ref)

    def body(b, carry):
        interp = pick_block(b, k, table, row_ref, col_ref, weight_ref, fields)
        point = b * BLOCK + lax.broadcasted_iota(jnp.int32, (1, BLOCK), 1)
        for v in range(fields):
            value = interp[v] + 0.5 * interp[(v + 1) % fields] * jnp.tanh(interp[(v + 2) % fields])
            new_ref[pl.ds(v * blocks + b, 1), :] = jnp.where(point < length, value, 0.0)
        return carry

    lax.fori_loop(0, real_blocks, body, 0)


GROUP = 16
MESH = pl.DeviceIdType.MESH


def mask_group(g, first, orders_ref, leg_ref, rows_j):
    degree = lax.broadcasted_iota(jnp.int32, (rows_j, leg_ref.shape[2]), 1)
    for pair in range(GROUP // 2):
        rows = slice(2 * pair * rows_j, 2 * (pair + 1) * rows_j)
        both = leg_ref[g, rows, :].astype(F32)
        parts = []
        for s in range(2):
            keep = degree >= orders_ref[first + g * GROUP + 2 * pair + s]
            parts.append(jnp.where(keep, both[s * rows_j : (s + 1) * rows_j], 0.0))
        leg_ref[g, rows, :] = jnp.concatenate(parts, axis=0).astype(BF16)


def forward_group(g, fields, rows_j, spec_ref, leg_ref, four_ref, square_ref):
    masked = leg_ref[g]
    state = spec_ref[g].reshape(fields * GROUP, spec_ref.shape[3])
    both = lax.dot_general(
        masked, jnp.concatenate([state, masked], axis=0), (((1,), (1,)), ((), ())),
        preferred_element_type=F32,
    )
    size = GROUP * rows_j
    width = fields * GROUP
    row = lax.broadcasted_iota(jnp.int32, (size, width), 0) // rows_j
    col = lax.broadcasted_iota(jnp.int32, (size, width), 1) % GROUP
    prod = jnp.where(row == col, both[:, :width], 0.0)
    four_ref[g] = jnp.sum(prod.reshape(GROUP, rows_j, width), axis=0)
    row = lax.broadcasted_iota(jnp.int32, (size, size), 0)
    col = lax.broadcasted_iota(jnp.int32, (size, size), 1)
    square = jnp.where(row // rows_j == col // rows_j, both[:, width:], 0.0)
    square_ref[g] = jnp.sum(square.reshape(GROUP, rows_j, size), axis=0)


def gram_of(square_ref, gram_ref, rows_j):
    groups, _, size = square_ref.shape
    row = lax.broadcasted_iota(jnp.int32, (size, size), 0)
    col = lax.broadcasted_iota(jnp.int32, (size, size), 1)
    swap = (row // rows_j == col % GROUP) & (row % rows_j == col // GROUP)
    turned = jnp.dot(
        square_ref[...].reshape(groups * rows_j, size), jnp.where(swap, 1.0, 0.0),
        preferred_element_type=F32, precision="highest",
    )
    gram_ref[...] = jnp.zeros_like(gram_ref)
    for h in range(groups):
        rows = turned[h * rows_j : (h + 1) * rows_j]
        for j in range(rows_j):
            gram_ref[j, :, h * GROUP : (h + 1) * GROUP] = rows[:, j * GROUP : (j + 1) * GROUP]


def order_rows(first, orders_ref, width):
    sub = lax.broadcasted_iota(jnp.int32, (8, width), 0)
    parts = []
    for t in range(GROUP // 8):
        part = jnp.full((8, width), orders_ref[first + 8 * t], jnp.int32)
        for i in range(1, 8):
            part = jnp.where(sub == i, orders_ref[first + 8 * t + i], part)
        parts.append(part)
    return jnp.concatenate(parts, axis=0)


def inverse_kernel(slots, coef_ref, leg_hbm, orders_ref, out_hbm, leg_ref, out_ref, load_sem, out_sem):
    groups, size, degrees = leg_ref.shape
    fields = coef_ref.shape[1]
    rows_j = size // GROUP
    me = lax.axis_index("wave")

    def load(g):
        return pltpu.make_async_copy(leg_hbm.at[g], leg_ref.at[g], load_sem.at[g])

    def store(g):
        slot_rows = pl.ds(pl.multiple_of(g * GROUP, GROUP), GROUP)
        return pltpu.make_async_copy(out_ref.at[g], out_hbm.at[:, slot_rows, :], out_sem.at[g])

    for g in range(groups):
        load(g).start()
    last = jnp.swapaxes(coef_ref[...], 0, 1)
    row = lax.broadcasted_iota(jnp.int32, (size, fields * GROUP), 0) // rows_j
    col = lax.broadcasted_iota(jnp.int32, (size, fields * GROUP), 1) % GROUP
    own = row == col
    degree = lax.broadcasted_iota(jnp.int32, (GROUP, degrees), 1)
    for g in range(groups):
        coefs = jnp.concatenate(
            [last[v, :, g * GROUP : (g + 1) * GROUP] for v in range(fields)], axis=1
        )
        tiled = jnp.concatenate([coefs] * GROUP, axis=0)
        spread = jnp.where(own, tiled, 0.0).T.astype(BF16)
        keep = degree >= order_rows(me * slots + g * GROUP, orders_ref, 128)[:, :1]
        load(g).wait()
        out = jnp.dot(spread, leg_ref[g], preferred_element_type=F32)
        for v in range(fields):
            rows = jnp.where(keep, out[v * GROUP : (v + 1) * GROUP], 0.0)
            out_ref[g, v] = rows.astype(BF16)
        store(g).start()
    for g in range(groups):
        store(g).wait()


def steps_kernel(
    steps, count, fields, blocks, real_blocks, slots,
    spec_hbm, leg_hbm, orders_ref, row_ref, col_ref, weight_ref, order_ref, len_ref, gauss_ref,
    out_ref,
    spec_ref, leg_ref, four_ref, square_ref, vjs_ref, first_ref, gram_ref, load_sem,
    cos_ref, sin_ref, fc_ref, fs_ref, ca_ref, sa_ref, spec_send, spec_recv, grid_send, grid_recv, tab_ref, coef_ref,
    new_ref, spec_ssem, spec_rsem, grid_ssem, grid_rsem, halo_ssem, halo_rsem,
):
    rows_j = leg_ref.shape[1] // GROUP
    groups = slots // GROUP

    def loads(g):
        slot_rows = pl.ds(pl.multiple_of(g * GROUP, GROUP), GROUP)
        return (
            pltpu.make_async_copy(leg_hbm.at[g], leg_ref.at[g], load_sem.at[0, g]),
            pltpu.make_async_copy(spec_hbm.at[:, slot_rows, :], spec_ref.at[g], load_sem.at[1, g]),
        )

    for g in range(groups):
        for copy in loads(g):
            copy.start()
    tab_ref[...] = jnp.zeros_like(tab_ref)
    vjs_ref[...] = jnp.zeros_like(vjs_ref)
    grid_send[...] = jnp.zeros_like(grid_send)
    me = lax.axis_index("wave")
    peers = [lax.rem(me + d, count) for d in range(1, count)]
    barrier = pltpu.get_barrier_semaphore()
    for peer in peers:
        pl.semaphore_signal(barrier, inc=1, device_id={"wave": peer}, device_id_type=MESH)
    length = len_ref[me]
    orders = orders_ref[...].reshape(1, orders_ref.shape[0])
    limit = jnp.minimum(orders.shape[1], (length - 1) // 2)
    fill_phases(orders, length, cos_ref, sin_ref)

    def forward(g, carry):
        for copy in loads(g):
            copy.wait()
        mask_group(g, me * slots, order_ref, leg_ref, rows_j)
        forward_group(g, fields, rows_j, spec_ref, leg_ref, four_ref, square_ref)
        return carry

    lax.fori_loop(0, groups, forward, 0, unroll=2)
    for h in range(groups):
        for v in range(fields):
            vjs_ref[v, :, h * GROUP : (h + 1) * GROUP] = four_ref[
                h, :, v * GROUP : (v + 1) * GROUP
            ]
    first_ref[...] = jnp.swapaxes(vjs_ref[...], 0, 1)
    pl.semaphore_wait(barrier, count - 1)

    def exchange(send, recv, ssem, rsem):
        copies = []
        for d, peer in enumerate(peers):
            copy = pltpu.make_async_remote_copy(
                src_ref=send.at[peer], dst_ref=recv.at[me], send_sem=ssem.at[d],
                recv_sem=rsem.at[d], device_id={"wave": peer}, device_id_type=MESH,
            )
            copy.start()
            copies.append(copy)
        return copies

    copies = exchange(first_ref, spec_recv.at[0], spec_ssem.at[0], spec_rsem.at[0])
    gram_of(square_ref, gram_ref, rows_j)
    active = jnp.where(orders < limit, 1.0, 0.0)
    build_table(cos_ref, sin_ref, active, fc_ref, fs_ref, ca_ref, sa_ref)
    grid_scale = 1.0 / jnp.sqrt(jnp.full((1, BLOCK), limit.astype(F32)))
    coef_scale = gauss_ref[0] * jnp.sqrt(2.0 / jnp.full(orders.shape, length.astype(F32)))
    cos_block = cos_ref[3 * RADIX : 3 * RADIX + blocks, :]
    sin_block = sin_ref[3 * RADIX : 3 * RADIX + blocks, :]
    rows = fields // 2 * 24
    for k in range(steps):
        source = first_ref if k == 0 else spec_send.at[k - 1]
        for copy in copies:
            copy.wait()
        spec_recv[k, me] = source[me]
        for i in range(count):
            coef_ref[:, i * slots : (i + 1) * slots] = spec_recv[k, i, :, :slots]
        own = grid_rows(
            coef_ref[...], cos_block, sin_block, fc_ref, fs_ref, length, grid_scale
        )
        tab_ref[k, 1] = own.astype(BF16)
        up = pltpu.make_async_remote_copy(
            src_ref=tab_ref.at[k, 1], dst_ref=tab_ref.at[k, 0], send_sem=halo_ssem.at[k, 0],
            recv_sem=halo_rsem.at[k, 0], device_id={"wave": lax.rem(me + 1, count)},
            device_id_type=MESH,
        )
        down = pltpu.make_async_remote_copy(
            src_ref=tab_ref.at[k, 1], dst_ref=tab_ref.at[k, 2], send_sem=halo_ssem.at[k, 1],
            recv_sem=halo_rsem.at[k, 1], device_id={"wave": lax.rem(me + count - 1, count)},
            device_id_type=MESH,
        )

        @pl.when(me < count - 1)
        def _():
            up.start()

        @pl.when(me > 0)
        def _():
            down.start()
            up.wait_recv()

        @pl.when(me < count - 1)
        def _():
            down.wait_recv()

        table = tab_ref[k].reshape(3 * rows, HALF)
        advance_fast(
            table, k, row_ref, col_ref, weight_ref, new_ref, length,
            fields // 2, blocks, real_blocks,
        )

        @pl.when(me < count - 1)
        def _():
            up.wait_send()

        @pl.when(me > 0)
        def _():
            down.wait_send()

        parts = analyse(new_ref, cos_block, sin_block, fc_ref, fs_ref, coef_scale)
        for v, part in enumerate(parts):
            coef_ref[v : v + 1, :] = part
        for i in range(count):
            grid_send[k, i, :, :slots] = coef_ref[:, i * slots : (i + 1) * slots]
        copies = exchange(grid_send.at[k], grid_recv.at[k], grid_ssem.at[k], grid_rsem.at[k])
        grid_recv[k, me] = grid_send[k, me]
        for copy in copies:
            copy.wait()
        if k + 1 < steps:
            mixed = []
            for v in range(fields):
                total = None
                for j in range(count):
                    term = gram_ref[j] * grid_recv[k, j, v : v + 1, :]
                    total = term if total is None else total + term
                mixed.append(total[None])
            spec_send[k] = jnp.swapaxes(jnp.concatenate(mixed, axis=0), 0, 1)
            copies = exchange(
                spec_send.at[k], spec_recv.at[k + 1], spec_ssem.at[k + 1], spec_rsem.at[k + 1]
            )
    out_ref[...] = grid_recv[steps - 1]


def fused(spectrum, legendre, order_of_slot, reduced_length, gauss_weight, row, col, weight, count):
    slots, rows_j, degrees = legendre.shape
    fields = 2 * spectrum.shape[0]
    orders_total = order_of_slot.shape[0]
    steps, stencil, grid_width = row.shape[0], row.shape[2], row.shape[-1]
    real_blocks = grid_width // BLOCK
    blocks = padded_blocks(grid_width)
    groups = slots // GROUP
    size = GROUP * rows_j
    lanes = -(-slots // 128) * 128
    shape = (steps, count, fields, lanes)
    table_rows = fields // 2 * blocks
    coefs = pl.pallas_call(
        functools.partial(steps_kernel, steps, count, fields, blocks, real_blocks, slots),
        out_shape=jax.ShapeDtypeStruct((rows_j, fields, lanes), F32),
        in_specs=[pl.BlockSpec(memory_space=pl.ANY)] * 2 + [VMEM_SPEC] * 4 + [SMEM_SPEC] * 3,
        out_specs=VMEM_SPEC,
        scratch_shapes=[
            pltpu.VMEM((groups, fields, GROUP, degrees), BF16),
            pltpu.VMEM((groups, size, degrees), BF16),
            pltpu.VMEM((groups, rows_j, fields * GROUP), F32),
            pltpu.VMEM((groups, rows_j, size), F32),
            pltpu.VMEM((fields, rows_j, lanes), F32),
            pltpu.VMEM((rows_j, fields, lanes), F32),
            pltpu.VMEM((rows_j, rows_j, lanes), F32),
            pltpu.SemaphoreType.DMA((2, groups)),
        ]
        + [pltpu.VMEM((3 * RADIX + blocks, orders_total), F32)] * 2
        + [pltpu.VMEM((BLOCK, orders_total), BF16)] * 2
        + [pltpu.VMEM((RADIX * RADIX, orders_total), F32)] * 2
        + [pltpu.VMEM(shape, F32)] * 4
        + [
            pltpu.VMEM((steps, 3, fields // 2 * 24, HALF), BF16),
            pltpu.VMEM((fields, orders_total), F32),
            pltpu.VMEM((table_rows, BLOCK), F32),
        ]
        + [pltpu.SemaphoreType.DMA((steps, count - 1))] * 4
        + [pltpu.SemaphoreType.DMA((steps, 2))] * 2,
        compiler_params=pltpu.CompilerParams(collective_id=0, has_side_effects=True),
        name="steps",
    )(
        spectrum.reshape(fields, slots, degrees),
        legendre.reshape(groups, size, degrees),
        order_of_slot,
        row.reshape(steps, stencil, 1, grid_width),
        col.reshape(steps, stencil, 1, grid_width),
        weight.reshape(steps, stencil, 1, grid_width),
        order_of_slot, reduced_length, gauss_weight,
    )
    out = pl.pallas_call(
        functools.partial(inverse_kernel, slots),
        out_shape=jax.ShapeDtypeStruct((fields, slots, degrees), BF16),
        in_specs=[VMEM_SPEC, pl.BlockSpec(memory_space=pl.ANY), SMEM_SPEC],
        out_specs=pl.BlockSpec(memory_space=pl.ANY),
        scratch_shapes=[
            pltpu.VMEM((groups, size, degrees), BF16),
            pltpu.VMEM((groups, fields, GROUP, degrees), BF16),
            pltpu.SemaphoreType.DMA((groups,)),
            pltpu.SemaphoreType.DMA((groups,)),
        ],
        name="inverse",
    )(coefs, legendre.reshape(groups, size, degrees), order_of_slot)
    return out.reshape(spectrum.shape)


def per_device(
    spectrum,
    legendre,
    order_of_slot,
    reduced_length,
    gauss_weight,
    depart_row,
    depart_col,
    depart_weight,
):
    own_index = lax.axis_index("wave")
    count = lax.axis_size("wave")
    slot_count = legendre.shape[0]
    orders_total = order_of_slot.shape[0]
    variables, level_count = spectrum.shape[:2]
    assert level_count == 1
    steps = depart_row.shape[0]
    grid_width = depart_row.shape[-1]
    stencil = depart_row.shape[2]
    fields = variables
    real_blocks = grid_width // BLOCK
    blocks = padded_blocks(grid_width)

    fits = slot_count % GROUP == 0 and 2 * fields == 8 and real_blocks <= 12
    if fits and legendre.shape[1] == 8 and count == 8:
        return fused(
            spectrum, legendre, order_of_slot, reduced_length, gauss_weight,
            depart_row, depart_col, depart_weight, count,
        )

    length = lax.dynamic_index_in_dim(reduced_length, own_index, keepdims=False)
    own_orders = lax.dynamic_slice_in_dim(order_of_slot, own_index * slot_count, slot_count)
    degrees = jnp.arange(legendre.shape[2], dtype=jnp.int32)
    masked = jnp.where(
        degrees[None, None, :] >= own_orders[:, None, None], legendre, jnp.zeros((), BF16)
    )
    order_limit = jnp.minimum(orders_total, (length - 1) // 2)
    cos_rows, sin_rows = phase_rows(length, order_of_slot, blocks)
    active = (order_of_slot < order_limit).astype(F32)[None, :]
    fc, fs = pl.pallas_call(
        build_table,
        out_shape=[jax.ShapeDtypeStruct((BLOCK, orders_total), BF16)] * 2,
        in_specs=[VMEM_SPEC] * 3,
        out_specs=[VMEM_SPEC] * 2,
        scratch_shapes=[pltpu.VMEM((RADIX * RADIX, orders_total), F32)] * 2,
        name="table",
    )(cos_rows, sin_rows, active)
    length1 = length.reshape(1)
    grid_scale = (1.0 / jnp.sqrt(order_limit.astype(F32))).reshape(1)
    coef_scale = (gauss_weight[0] * jnp.sqrt(2.0 / length.astype(F32))).reshape(1)

    synth = pl.pallas_call(
        functools.partial(synth_kernel, blocks),
        out_shape=jax.ShapeDtypeStruct((fields * blocks, BLOCK), BF16),
        in_specs=[VMEM_SPEC] * 5 + [SMEM_SPEC] * 2,
        out_specs=VMEM_SPEC,
        name="synth",
    )
    grid_step = pl.pallas_call(
        functools.partial(grid_kernel, fields, blocks, real_blocks),
        out_shape=jax.ShapeDtypeStruct((2 * fields, orders_total), BF16),
        in_specs=[VMEM_SPEC] * 8 + [SMEM_SPEC] * 2,
        out_specs=VMEM_SPEC,
        scratch_shapes=[pltpu.VMEM((fields * blocks, BLOCK), F32)],
        name="grid_step",
    )
    spectral = spectrum.reshape(2 * fields, slot_count, -1)
    fourier = jnp.einsum("vsn,sjn->jvs", spectral, masked, preferred_element_type=F32)
    gram = jnp.einsum("sjn,skn->sjk", masked, masked, preferred_element_type=F32)
    forward = [(i, i + 1) for i in range(count - 1)]
    backward = [(i + 1, i) for i in range(count - 1)]
    for k in range(steps):
        gathered = lax.all_to_all(fourier.astype(BF16), "wave", split_axis=0, concat_axis=2, tiled=True)
        own = synth(
            gathered.reshape(2 * fields, orders_total), cos_rows, sin_rows, fc, fs, length1, grid_scale
        )
        low = lax.ppermute(own, "wave", forward)
        high = lax.ppermute(own, "wave", backward)
        coeffs = grid_step(
            jnp.concatenate([low, own, high], axis=0),
            depart_row[k].reshape(1, stencil, 1, grid_width),
            depart_col[k].reshape(1, stencil, 1, grid_width),
            depart_weight[k].reshape(1, stencil, 1, grid_width),
            cos_rows, sin_rows, fc, fs, length1, coef_scale,
        )
        returned = lax.all_to_all(
            coeffs.reshape(1, 2 * fields, orders_total), "wave", split_axis=2, concat_axis=0, tiled=True
        )
        if k + 1 < steps:
            fourier = jnp.einsum("jvs,sjk->kvs", returned.astype(F32), gram, precision="highest")
    final = jnp.einsum("jvs,sjn->vsn", returned, masked, preferred_element_type=F32).astype(BF16)
    return final.reshape(spectrum.shape)


def solution(mesh):
    placed = (
        P(None, "lev", None, "wave", None),
        P("wave", None, None),
        P(),
        P(),
        P("wave"),
        P(None, "lev", None, "wave", None),
        P(None, "lev", None, "wave", None),
        P(None, "lev", None, "wave", None),
    )
    return jax.shard_map(
        per_device,
        mesh=mesh,
        in_specs=placed,
        out_specs=P(None, "lev", None, "wave", None),
        check_vma=False,
    )
```

```python
import functools
import math

import jax
import jax.numpy as jnp
from jax import lax
from jax.experimental import pallas as pl
from jax.experimental.pallas import tpu as pltpu
from jax.sharding import PartitionSpec as P

BLOCK = 512
RADIX = 8
FULL_TURN = 2.0 * math.pi
F32 = jnp.float32
BF16 = jnp.bfloat16

VMEM_SPEC = pl.BlockSpec(memory_space=pltpu.VMEM)
SMEM_SPEC = pl.BlockSpec(memory_space=pltpu.SMEM)


def padded_blocks(grid_width):
    return -(-(grid_width // BLOCK) // 16) * 16


def phase_rows(length, orders, blocks):
    digits = jnp.arange(RADIX, dtype=jnp.int32)
    steps = [digits, digits * RADIX, digits * RADIX * RADIX]
    steps.append(jnp.arange(blocks, dtype=jnp.int32) * BLOCK)
    steps = jnp.concatenate(steps)
    phases = steps[:, None] * orders[None, :] % length
    angles = phases.astype(F32) * (jnp.float32(FULL_TURN) / length.astype(F32))
    return jnp.cos(angles), jnp.sin(angles)


def build_table(cos_ref, sin_ref, active_ref, fc_ref, fs_ref, ca_ref, sa_ref):
    active = active_ref[...]
    cos_low = cos_ref[0:RADIX, :] * active
    sin_low = sin_ref[0:RADIX, :] * active
    cos_mid = cos_ref[RADIX : 2 * RADIX, :]
    sin_mid = sin_ref[RADIX : 2 * RADIX, :]
    for a in range(RADIX):
        c = cos_ref[2 * RADIX + a : 2 * RADIX + a + 1, :]
        s = sin_ref[2 * RADIX + a : 2 * RADIX + a + 1, :]
        ca_ref[a * RADIX : (a + 1) * RADIX, :] = c * cos_mid - s * sin_mid
        sa_ref[a * RADIX : (a + 1) * RADIX, :] = s * cos_mid + c * sin_mid

    def body(i, carry):
        cos_parts, sin_parts = [], []
        for k in range(2):
            c = ca_ref[pl.ds(2 * i + k, 1), :]
            s = sa_ref[pl.ds(2 * i + k, 1), :]
            cos_parts.append(c * cos_low - s * sin_low)
            sin_parts.append(-(s * cos_low + c * sin_low))
        rows = pl.ds(pl.multiple_of(i * 2 * RADIX, 2 * RADIX), 2 * RADIX)
        fc_ref[rows, :] = jnp.concatenate(cos_parts, axis=0).astype(BF16)
        fs_ref[rows, :] = jnp.concatenate(sin_parts, axis=0).astype(BF16)
        return carry

    lax.fori_loop(0, RADIX * RADIX // 2, body, 0)


def synthesize(coeffs, cos_block, sin_block, fc_ref, fs_ref, length, scale):
    fields = coeffs.shape[0] // 2
    blocks = cos_block.shape[0]
    reals, imags = [], []
    for v in range(fields):
        real = coeffs[2 * v : 2 * v + 1]
        imag = coeffs[2 * v + 1 : 2 * v + 2]
        reals.append((real * cos_block - imag * sin_block).astype(BF16))
        imags.append((real * sin_block + imag * cos_block).astype(BF16))
    dims = (((1,), (1,)), ((), ()))
    out = lax.dot_general(
        jnp.concatenate(reals, axis=0), fc_ref[...], dims, preferred_element_type=F32
    ) + lax.dot_general(
        jnp.concatenate(imags, axis=0), fs_ref[...], dims, preferred_element_type=F32
    )
    row = lax.broadcasted_iota(jnp.int32, out.shape, 0) % blocks
    point = row * BLOCK + lax.broadcasted_iota(jnp.int32, out.shape, 1)
    return jnp.where(point < length, out * scale, 0.0)


def synth_kernel(blocks, coef_ref, cos_ref, sin_ref, fc_ref, fs_ref, len_ref, scale_ref, out_ref):
    out_ref[...] = synthesize(
        coef_ref[...].astype(F32),
        cos_ref[3 * RADIX : 3 * RADIX + blocks, :],
        sin_ref[3 * RADIX : 3 * RADIX + blocks, :],
        fc_ref,
        fs_ref,
        len_ref[0],
        scale_ref[0],
    ).astype(BF16)


def gather_block(b, k, table, row_ref, col_ref, weight_ref, fields, blocks):
    stencil = col_ref.shape[1]
    half = 256
    lanes = pl.ds(pl.multiple_of(b * BLOCK, BLOCK), BLOCK)
    iota_half = lax.broadcasted_iota(jnp.int32, (half, BLOCK), 0).astype(F32).astype(BF16)
    iota_rows = lax.broadcasted_iota(jnp.int32, (3 * blocks, BLOCK), 0)
    one = jnp.ones((), BF16)
    zero = jnp.zeros((), BF16)
    acc = [jnp.zeros((blocks, BLOCK), F32) for _ in range(fields)]
    for p in range(stencil):
        col = col_ref[k, p, :, lanes]
        row = row_ref[k, p, :, lanes]
        weight = weight_ref[k, p, :, lanes]
        point = col % BLOCK
        halves = []
        for h in range(BLOCK // half):
            local = point - h * half
            key = jnp.where((local >= 0) & (local < half), local, -1).astype(F32).astype(BF16)
            halves.append(jnp.where(iota_half == key, one, zero))
        onehot = jnp.concatenate(halves, axis=0)
        found = jnp.dot(table, onehot, preferred_element_type=F32)
        which = (row + 1) * blocks + col // BLOCK
        chosen = jnp.where(iota_rows == which, weight, 0.0)
        for r in range(3):
            sel = chosen[r * blocks : (r + 1) * blocks]
            for v in range(fields):
                start = (r * fields + v) * blocks
                acc[v] = acc[v] + found[start : start + blocks] * sel
    return [jnp.sum(a, axis=0, keepdims=True) for a in acc]


def advance(table, k, row_ref, col_ref, weight_ref, new_ref, length, fields, blocks, real_blocks):
    new_ref[...] = jnp.zeros_like(new_ref)

    def body(b, carry):
        interp = gather_block(b, k, table, row_ref, col_ref, weight_ref, fields, blocks)
        point = b * BLOCK + lax.broadcasted_iota(jnp.int32, (1, BLOCK), 1)
        for v in range(fields):
            value = interp[v] + 0.5 * interp[(v + 1) % fields] * jnp.tanh(interp[(v + 2) % fields])
            new_ref[pl.ds(v * blocks + b, 1), :] = jnp.where(point < length, value, 0.0)
        return carry

    lax.fori_loop(0, real_blocks, body, 0)


def analyse(new_ref, cos_block, sin_block, fc_ref, fs_ref, scale):
    blocks = cos_block.shape[0]
    fields = new_ref.shape[0] // blocks
    newgrid = new_ref[...].astype(BF16)
    part_real = jnp.dot(newgrid, fc_ref[...], preferred_element_type=F32)
    part_imag = jnp.dot(newgrid, fs_ref[...], preferred_element_type=F32)
    out = []
    for v in range(fields):
        pr = part_real[v * blocks : (v + 1) * blocks]
        pi = part_imag[v * blocks : (v + 1) * blocks]
        real = jnp.sum(pr * cos_block + pi * sin_block, axis=0, keepdims=True)
        imag = jnp.sum(pi * cos_block - pr * sin_block, axis=0, keepdims=True)
        out += [real * scale, imag * scale]
    return out


def grid_kernel(
    fields, blocks, real_blocks,
    table_ref, row_ref, col_ref, weight_ref, cos_ref, sin_ref, fc_ref, fs_ref, len_ref, scale_ref,
    out_ref, new_ref,
):
    advance(
        table_ref[...], 0, row_ref, col_ref, weight_ref, new_ref, len_ref[0],
        fields, blocks, real_blocks,
    )
    rows = analyse(
        new_ref,
        cos_ref[3 * RADIX : 3 * RADIX + blocks, :],
        sin_ref[3 * RADIX : 3 * RADIX + blocks, :],
        fc_ref,
        fs_ref,
        scale_ref[0],
    )
    out_ref[...] = jnp.concatenate(rows, axis=0).astype(BF16)


SPAN = 256
WIDE = 3 * SPAN
GROUP = 16
MESH = pl.DeviceIdType.MESH
HBM_SPEC = pl.BlockSpec(memory_space=pltpu.HBM)


def half_rows(lat, stride):
    return (20 + 4 * ((lat + 1) * stride - 1) + SPAN - 1) // SPAN


def unit_turns(steps, orders, length):
    product = steps * orders
    inverse = 1.0 / length
    rest = product - jnp.floor(product * inverse + 0.5) * length
    x = rest * (inverse * (0.25 * FULL_TURN))
    y = x * x
    s = x * (1.0 + y * (-1.0 / 6 + y * (1.0 / 120 + y * (-1.0 / 5040 + y * (1.0 / 362880)))))
    c = 1.0 + y * (-0.5 + y * (1.0 / 24 + y * (-1.0 / 720 + y * (1.0 / 40320))))
    s, c = 2.0 * s * c, 1.0 - 2.0 * s * s
    return 1.0 - 2.0 * s * s, 2.0 * s * c


def tables(p, orders, length, limit, cos_ref, sin_ref, fc_ref, fs_ref, ca_ref, sa_ref):
    shape = (8, orders.shape[1])
    digit = lax.broadcasted_iota(jnp.int32, shape, 0)
    digit_f = digit.astype(F32)
    length_f = jnp.full(shape, length.astype(F32))
    orders_f = jnp.broadcast_to(orders.astype(F32), shape)
    active = jnp.where(orders_f < limit.astype(F32), 1.0, 0.0)
    cos_b, sin_b = unit_turns(digit_f * SPAN, orders_f, length_f)
    mixed = jnp.where(digit < 4, digit_f * 64, (digit_f - 4.0) * (8 * SPAN))
    cos_h, sin_h = unit_turns(mixed, orders_f, length_f)
    cos_ref[p, 0:8, :] = cos_b
    sin_ref[p, 0:8, :] = sin_b
    for t in range(1, cos_ref.shape[1] // 8):
        c, s = cos_h[4 + t : 5 + t], sin_h[4 + t : 5 + t]
        cos_ref[p, 8 * t : 8 * t + 8, :] = c * cos_b - s * sin_b
        sin_ref[p, 8 * t : 8 * t + 8, :] = s * cos_b + c * sin_b
    cos_m, sin_m = unit_turns(digit_f * 8, orders_f, length_f)
    for t in range(SPAN // 64):
        c, s = cos_h[t : t + 1], sin_h[t : t + 1]
        ca_ref[8 * t : 8 * t + 8, :] = c * cos_m - s * sin_m
        sa_ref[8 * t : 8 * t + 8, :] = s * cos_m + c * sin_m
    cos_low, sin_low = unit_turns(digit_f, orders_f, length_f)
    ca_ref[SPAN // 8 : SPAN // 8 + 8, :] = cos_low * active
    sa_ref[SPAN // 8 : SPAN // 8 + 8, :] = sin_low * active

    def body(i, carry):
        cos_l = ca_ref[SPAN // 8 : SPAN // 8 + 8, :]
        sin_l = sa_ref[SPAN // 8 : SPAN // 8 + 8, :]
        cos_parts, sin_parts = [], []
        for k in range(2):
            c = ca_ref[pl.ds(2 * i + k, 1), :]
            s = sa_ref[pl.ds(2 * i + k, 1), :]
            cos_parts.append(c * cos_l - s * sin_l)
            sin_parts.append(-(s * cos_l + c * sin_l))
        rows = pl.ds(pl.multiple_of(i * 16, 16), 16)
        fc_ref[p, rows, :] = jnp.concatenate(cos_parts, axis=0).astype(BF16)
        fs_ref[p, rows, :] = jnp.concatenate(sin_parts, axis=0).astype(BF16)
        return carry

    lax.fori_loop(0, SPAN // 16, body, 0)


def grid_rows(coeffs, cos_block, sin_block, fc, fs, length, scale):
    variables = coeffs.shape[0] // 2
    blocks = cos_block.shape[0]
    reals, imags = [], []
    for v in range(variables):
        real = coeffs[2 * v : 2 * v + 1]
        imag = coeffs[2 * v + 1 : 2 * v + 2]
        reals.append((real * cos_block - imag * sin_block).astype(BF16))
        imags.append((real * sin_block + imag * cos_block).astype(BF16))
    dims = (((1,), (1,)), ((), ()))
    out = lax.dot_general(
        fc, jnp.concatenate(reals, axis=0), dims, preferred_element_type=F32
    ) + lax.dot_general(
        fs, jnp.concatenate(imags, axis=0), dims, preferred_element_type=F32
    )
    out = out.T
    row = lax.broadcasted_iota(jnp.int32, out.shape, 0) % blocks
    point = row * SPAN + lax.broadcasted_iota(jnp.int32, out.shape, 1)
    return jnp.where(point < length, out * scale, 0.0)


def pick_wide(b, k, table, rows8, row_ref, col_ref, weight_ref, variables):
    stencil = col_ref.shape[1]
    lanes = pl.ds(pl.multiple_of(b * WIDE, WIDE), WIDE)
    iota = lax.broadcasted_iota(jnp.int32, (SPAN, WIDE), 0).astype(F32).astype(BF16)
    sub = lax.broadcasted_iota(jnp.int32, (8, WIDE), 0)
    one = jnp.ones((), BF16)
    zero = jnp.zeros((), BF16)
    starts = [8 * sum(rows8[:r]) if rows8[r] else 1024 for r in range(3)]
    acc = [None] * variables
    for p in range(stencil):
        col = col_ref[k, p, :, lanes]
        row = row_ref[k, p, :, lanes]
        weight = weight_ref[k, p, :, lanes]
        key = (col & (SPAN - 1)).astype(F32).astype(BF16)
        onehot = jnp.where(iota == key, one, zero)
        found = jnp.dot(table, onehot, preferred_element_type=F32)
        base = jnp.where(row < 0, starts[0], jnp.where(row > 0, starts[2], starts[1]))
        which = base + (col // SPAN)
        got = [jnp.zeros((8, WIDE), F32) for _ in range(variables)]
        for q in range(sum(rows8)):
            hit = sub == which - 8 * q
            for v in range(variables):
                start = (q * variables + v) * 8
                got[v] = jnp.where(hit, found[start : start + 8], got[v])
        for v in range(variables):
            term = got[v] * weight
            acc[v] = term if p == 0 else acc[v] + term
    return [jnp.sum(a, axis=0, keepdims=True) for a in acc]


def gather(k, rows8, turns, own_ref, tab_ref, row_ref, col_ref, weight_ref, new_ref, variables):
    blocks = own_ref.shape[1] // variables
    parts = []
    for r in range(3):
        for t in range(rows8[r]):
            for v in range(variables):
                parts.append(own_ref[r, v * blocks + 8 * t : v * blocks + 8 * t + 8, :])
    size = 8 * len(parts)
    tab_ref[0:size, :] = jnp.concatenate(parts, axis=0).astype(BF16)

    def body(b, carry):
        interp = pick_wide(
            b, k, tab_ref[0:size, :], rows8, row_ref, col_ref, weight_ref, variables
        )
        for v in range(variables):
            for t in range(WIDE // SPAN):
                new_ref[pl.ds(v * blocks + b * (WIDE // SPAN) + t, 1), :] = interp[v][
                    :, t * SPAN : (t + 1) * SPAN
                ]
        return carry

    lax.fori_loop(0, turns, body, 0)


def new_grid(new_ref, length, variables):
    blocks = new_ref.shape[0] // variables
    interp = [new_ref[v * blocks : (v + 1) * blocks, :] for v in range(variables)]
    shape = interp[0].shape
    point = lax.broadcasted_iota(jnp.int32, shape, 0) * SPAN + lax.broadcasted_iota(jnp.int32, shape, 1)
    inside = point < length
    out = []
    for v in range(variables):
        value = interp[v] + 0.5 * interp[(v + 1) % variables] * jnp.tanh(interp[(v + 2) % variables])
        out.append(jnp.where(inside, value, 0.0))
    return jnp.concatenate(out, axis=0).astype(BF16)


def analyse_rows(newgrid, cos_block, sin_block, fc, fs, scale):
    blocks = cos_block.shape[0]
    part_real = jnp.dot(newgrid, fc, preferred_element_type=F32)
    part_imag = jnp.dot(newgrid, fs, preferred_element_type=F32)
    out = []
    for v in range(newgrid.shape[0] // blocks):
        pr = part_real[v * blocks : (v + 1) * blocks]
        pi = part_imag[v * blocks : (v + 1) * blocks]
        real = jnp.sum(pr * cos_block + pi * sin_block, axis=0, keepdims=True)
        imag = jnp.sum(pi * cos_block - pr * sin_block, axis=0, keepdims=True)
        out += [real * scale, imag * scale]
    return jnp.concatenate(out, axis=0)


def order_rows(first, orders_ref):
    sub = lax.broadcasted_iota(jnp.int32, (8, 128), 0)
    parts = []
    for t in range(GROUP // 8):
        part = jnp.full((8, 128), orders_ref[first + 8 * t], jnp.int32)
        for i in range(1, 8):
            part = jnp.where(sub == i, orders_ref[first + 8 * t + i], part)
        parts.append(part)
    return jnp.concatenate(parts, axis=0)[:, :1]


def own_slots(both, rows_j, width, inner):
    size = GROUP * rows_j
    row = lax.broadcasted_iota(jnp.int32, (size, width), 0) // rows_j
    col = lax.broadcasted_iota(jnp.int32, (size, width), 1)
    col = col % GROUP if inner else col // rows_j
    return jnp.sum(jnp.where(row == col, both, 0.0).reshape(GROUP, rows_j, width), axis=0)


def forward_group(g, first, fields, rows_j, spec_ref, leg_ref, orders_ref, four_ref):
    degrees = spec_ref.shape[3]
    degree = lax.broadcasted_iota(jnp.int32, (GROUP, degrees), 1)
    keep = jnp.where(degree >= order_rows(first + g * GROUP, orders_ref), 1.0, 0.0).astype(BF16)
    state = jnp.concatenate([spec_ref[g, v] * keep for v in range(fields)], axis=0)
    both = lax.dot_general(
        leg_ref[g], state, (((1,), (1,)), ((), ())), preferred_element_type=F32
    )
    four_ref[g] = own_slots(both, rows_j, fields * GROUP, True)


def gram_group(g, first, rows_j, leg_ref, orders_ref, square_ref):
    degrees = leg_ref.shape[2]
    degree = lax.broadcasted_iota(jnp.int32, (2 * rows_j, degrees), 1)
    sub = lax.broadcasted_iota(jnp.int32, (2 * rows_j, 128), 0)
    parts = []
    for pair in range(GROUP // 2):
        slot = first + g * GROUP + 2 * pair
        order = jnp.where(sub < rows_j, orders_ref[slot], orders_ref[slot + 1])[:, :1]
        keep = jnp.where(degree >= order, 1.0, 0.0).astype(BF16)
        parts.append(leg_ref[g, 2 * pair * rows_j : 2 * (pair + 1) * rows_j, :] * keep)
    both = lax.dot_general(
        leg_ref[g], jnp.concatenate(parts, axis=0), (((1,), (1,)), ((), ())),
        preferred_element_type=F32,
    )
    square_ref[g] = own_slots(both, rows_j, GROUP * rows_j, False)


def gram_of(square_ref, gram_ref, rows_j):
    groups, _, size = square_ref.shape
    row = lax.broadcasted_iota(jnp.int32, (size, size), 0)
    col = lax.broadcasted_iota(jnp.int32, (size, size), 1)
    swap = (row // rows_j == col % GROUP) & (row % rows_j == col // GROUP)
    turned = jnp.dot(
        square_ref[...].reshape(groups * rows_j, size), jnp.where(swap, 1.0, 0.0),
        preferred_element_type=F32, precision="highest",
    )
    for h in range(groups):
        rows = turned[h * rows_j : (h + 1) * rows_j]
        for j in range(rows_j):
            gram_ref[j, :, h * GROUP : (h + 1) * GROUP] = rows[:, j * GROUP : (j + 1) * GROUP]


def steps_kernel(
    steps, count, fields, slots, stride,
    spec_hbm, leg_hbm, orders_ref, row_hbm, col_hbm, weight_hbm, order_ref, len_ref, gauss_ref,
    out_ref,
    spec_ref, leg_ref, row_ref, col_ref, weight_ref,
    four_ref, square_ref, vjs_ref, gram_ref, pack_ref,
    cos_ref, sin_ref, fc_ref, fs_ref, ca_ref, sa_ref,
    coef_ref, mine_ref, mix_ref, own_ref, tab_ref, new_ref,
    a_send, a_recv, g_send, g_recv, all_send, all_recv, b_send, b_recv,
    load_sem, point_sem, a_ssem, a_rsem, g_ssem, g_rsem, all_ssem, all_rsem, b_ssem, b_rsem,
):
    rows_j = leg_ref.shape[1] // GROUP
    groups = slots // GROUP
    variables = fields // 2
    total = orders_ref.shape[0]
    blocks = cos_ref.shape[1]
    cut = 3 * slots

    def loads(g):
        slot_rows = pl.ds(pl.multiple_of(g * GROUP, GROUP), GROUP)
        return (
            pltpu.make_async_copy(leg_hbm.at[g], leg_ref.at[g], load_sem.at[0, g]),
            pltpu.make_async_copy(spec_hbm.at[:, slot_rows, :], spec_ref.at[g], load_sem.at[1, g]),
        )

    points = [
        pltpu.make_async_copy(row_hbm, row_ref, point_sem.at[0]),
        pltpu.make_async_copy(col_hbm, col_ref, point_sem.at[1]),
        pltpu.make_async_copy(weight_hbm, weight_ref, point_sem.at[2]),
    ]
    me = lax.axis_index("wave")
    peers = [lax.rem(me + d, count) for d in range(1, count)]
    barrier = pltpu.get_barrier_semaphore()
    for peer in peers:
        pl.semaphore_signal(barrier, inc=1, device_id={"wave": peer}, device_id_type=MESH)
    for g in range(groups):
        for copy in loads(g):
            copy.start()
    for copy in points:
        copy.start()
    vjs_ref[...] = jnp.zeros_like(vjs_ref)
    gram_ref[...] = jnp.zeros_like(gram_ref)
    pack_ref[...] = jnp.zeros_like(pack_ref)
    new_ref[...] = jnp.zeros_like(new_ref)
    coef_ref[...] = jnp.zeros_like(coef_ref)
    mine_ref[...] = jnp.zeros_like(mine_ref)
    orders = orders_ref[...].reshape(1, total)
    lats = [jnp.clip(me + r - 1, 0, count - 1) for r in range(3)]
    lengths = [len_ref[lat] for lat in lats]
    limits = [jnp.minimum(total, (length - 1) // 2) for length in lengths]
    first = me * slots

    for r in range(3):
        tables(
            r, orders, lengths[r], limits[r], cos_ref, sin_ref, fc_ref, fs_ref, ca_ref, sa_ref
        )

    def forward(g, carry):
        for copy in loads(g):
            copy.wait()
        forward_group(g, first, fields, rows_j, spec_ref, leg_ref, order_ref, four_ref)
        return carry

    lax.fori_loop(0, groups, forward, 0, unroll=2)
    for h in range(groups):
        for v in range(fields):
            vjs_ref[v, :, h * GROUP : (h + 1) * GROUP] = four_ref[
                h, :, v * GROUP : (v + 1) * GROUP
            ]

    def pack(source, send):
        for p in range(count):
            for r in range(3):
                pack_ref[p, :, r * slots : (r + 1) * slots] = source[
                    min(max(p + r - 1, 0), count - 1)
                ][:, :slots]
        for p in range(count):
            send(p)

    def send_first(p):
        half = pack_ref.shape[2] // 2
        a_send[p] = jnp.concatenate(
            [pack_ref[p, :, :half], pack_ref[p, :, half:]], axis=0
        ).astype(BF16)

    def send_gram(p):
        g_send[p] = pack_ref[p]

    def exchange(send, recv, ssem, rsem):
        copies = []
        for d, peer in enumerate(peers):
            copy = pltpu.make_async_remote_copy(
                src_ref=send(peer), dst_ref=recv.at[me], send_sem=ssem.at[d],
                recv_sem=rsem.at[d], device_id={"wave": peer}, device_id_type=MESH,
            )
            copy.start()
            copies.append(copy)
        return copies

    pack(jnp.swapaxes(vjs_ref[...], 0, 1), send_first)
    pl.semaphore_wait(barrier, count - 1)
    copies = exchange(lambda peer: a_send.at[peer], a_recv, a_ssem, a_rsem)
    a_recv[me] = a_send[me]

    def gram(g, carry):
        gram_group(g, first, rows_j, leg_ref, order_ref, square_ref)
        return carry

    lax.fori_loop(0, groups, gram, 0, unroll=2)
    gram_of(square_ref, gram_ref, rows_j)
    pack(gram_ref[...], send_gram)
    for copy in copies:
        copy.wait()
    gram_copies = exchange(lambda peer: g_send.at[peer], g_recv, g_ssem, g_rsem)
    g_recv[me] = g_send[me]
    for copy in points:
        copy.wait()
    for i in range(count):
        half = a_recv.shape[2]
        both = a_recv[i].astype(F32)
        both = jnp.concatenate([both[:fields], both[fields:]], axis=1)
        for r in range(3):
            coef_ref[r, :, i * slots : (i + 1) * slots] = both[:, r * slots : (r + 1) * slots]

    shape = (1, total)
    coef_scale = gauss_ref[0] * jnp.sqrt(2.0 / jnp.full(shape, lengths[1].astype(F32)))
    inside = [jnp.where(me > 0, 1.0, 0.0), 1.0, jnp.where(me < count - 1, 1.0, 0.0)]
    scales = [
        inside[r] / jnp.sqrt(jnp.full((1, SPAN), limits[r].astype(F32))) for r in range(3)
    ]
    turns = (half_rows(me, stride) + WIDE // SPAN - 1) // (WIDE // SPAN)
    most = [(half_rows(count - 4 + r, stride) + 7) // 8 for r in range(1, 4)]
    for k in range(steps):
        for r in range(3):
            own_ref[r] = grid_rows(
                coef_ref[r], cos_ref[r], sin_ref[r], fc_ref[r], fs_ref[r], lengths[r], scales[r]
            )
        args = (own_ref, tab_ref, row_ref, col_ref, weight_ref, new_ref, variables)

        @pl.when(me < count - 1)
        def _():
            gather(k, [most[0], most[1], most[2]], turns, *args)

        @pl.when(me == count - 1)
        def _():
            gather(k, [most[1], most[2], 0], turns, *args)

        mine = analyse_rows(
            new_grid(new_ref, lengths[1], variables),
            cos_ref[1], sin_ref[1], fc_ref[1], fs_ref[1], coef_scale,
        )
        if k + 1 < steps:
            half = total // 2
            all_send[k] = jnp.concatenate([mine[:, :half], mine[:, half:]], axis=0).astype(BF16)
            copies = exchange(
                lambda peer: all_send.at[k], all_recv.at[k], all_ssem.at[k], all_rsem.at[k]
            )
            all_recv[k, me] = all_send[k]
            if k == 0:
                for copy in gram_copies:
                    copy.wait()
                for i in range(count):
                    for r in range(3):
                        mix_ref[r, :, i * slots : (i + 1) * slots] = g_recv[
                            i, :, r * slots : (r + 1) * slots
                        ]
            for copy in copies:
                copy.wait()
            sums = [None] * 3
            for j in range(count):
                both = all_recv[k, j].astype(F32)
                both = jnp.concatenate([both[:fields], both[fields:]], axis=1)
                for r in range(3):
                    term = mix_ref[r, j : j + 1, :] * both
                    sums[r] = term if j == 0 else sums[r] + term
            for r in range(3):
                coef_ref[r] = sums[r]
        else:
            mine_ref[:, :total] = mine
            for i in range(count):
                b_send[i] = jnp.concatenate(
                    [
                        mine_ref[:, i * slots : i * slots + 128],
                        mine_ref[:, i * slots + 128 : i * slots + 256],
                    ],
                    axis=0,
                ).astype(BF16)
            copies = exchange(lambda peer: b_send.at[peer], b_recv, b_ssem, b_rsem)
            b_recv[me] = b_send[me]
            for copy in copies:
                copy.wait()
    out_ref[...] = b_recv[...]


def inverse_kernel(slots, coef_ref, leg_ref, orders_ref, out_hbm, out_ref, out_sem):
    groups, size, degrees = leg_ref.shape
    rows_j = size // GROUP
    fields = coef_ref.shape[1] // 2
    me = lax.axis_index("wave")

    def store(g):
        slot_rows = pl.ds(pl.multiple_of(g * GROUP, GROUP), GROUP)
        return pltpu.make_async_copy(out_ref.at[g], out_hbm.at[:, slot_rows, :], out_sem.at[g])

    last = jnp.swapaxes(coef_ref[...].astype(F32), 0, 1)
    row = lax.broadcasted_iota(jnp.int32, (size, fields * GROUP), 0) // rows_j
    col = lax.broadcasted_iota(jnp.int32, (size, fields * GROUP), 1) % GROUP
    own = row == col
    degree = lax.broadcasted_iota(jnp.int32, (GROUP, degrees), 1)
    for g in range(groups):
        half, lane = divmod(g * GROUP, 128)
        coefs = jnp.concatenate(
            [last[half * fields + v, :, lane : lane + GROUP] for v in range(fields)], axis=1
        )
        tiled = jnp.concatenate([coefs] * GROUP, axis=0)
        spread = jnp.where(own, tiled, 0.0).T.astype(BF16)
        keep = degree >= order_rows(me * slots + g * GROUP, orders_ref)
        out = jnp.dot(spread, leg_ref[g], preferred_element_type=F32)
        for v in range(fields):
            rows = jnp.where(keep, out[v * GROUP : (v + 1) * GROUP], 0.0)
            out_ref[g, v] = rows.astype(BF16)
        store(g).start()
    for g in range(groups):
        store(g).wait()


def fused(spectrum, legendre, order_of_slot, reduced_length, gauss_weight, row, col, weight, count):
    slots, rows_j, degrees = legendre.shape
    fields = 2 * spectrum.shape[0]
    total = order_of_slot.shape[0]
    steps, stencil, grid_width = row.shape[0], row.shape[2], row.shape[-1]
    blocks = -(-(grid_width // SPAN) // 8) * 8
    stride = total // count
    groups = slots // GROUP
    size = GROUP * rows_j
    lanes = -(-slots // 128) * 128
    packed = -(-3 * slots // 256) * 256
    rows_v = fields // 2 * blocks
    half = total // 2
    points = (steps, stencil, 1, grid_width)
    coefs = pl.pallas_call(
        functools.partial(steps_kernel, steps, count, fields, slots, stride),
        out_shape=pltpu.VMEM((count, 2 * fields, 128), BF16),
        in_specs=[HBM_SPEC] * 2 + [VMEM_SPEC] + [HBM_SPEC] * 3 + [SMEM_SPEC] * 3,
        out_specs=VMEM_SPEC,
        scratch_shapes=[
            pltpu.VMEM((groups, fields, GROUP, degrees), BF16),
            pltpu.VMEM((groups, size, degrees), BF16),
            pltpu.VMEM(points, jnp.int32),
            pltpu.VMEM(points, jnp.int32),
            pltpu.VMEM(points, F32),
            pltpu.VMEM((groups, rows_j, fields * GROUP), F32),
            pltpu.VMEM((groups, rows_j, size), F32),
            pltpu.VMEM((fields, rows_j, lanes), F32),
            pltpu.VMEM((rows_j, rows_j, lanes), F32),
            pltpu.VMEM((count, fields, packed), F32),
            pltpu.VMEM((3, blocks, total), F32),
            pltpu.VMEM((3, blocks, total), F32),
            pltpu.VMEM((3, SPAN, total), BF16),
            pltpu.VMEM((3, SPAN, total), BF16),
            pltpu.VMEM((SPAN // 8 + 8, total), F32),
            pltpu.VMEM((SPAN // 8 + 8, total), F32),
            pltpu.VMEM((3, fields, total), F32),
            pltpu.VMEM((fields, total + 128), F32),
            pltpu.VMEM((3, rows_j, total), F32),
            pltpu.VMEM((3, rows_v, SPAN), F32),
            pltpu.VMEM((3 * rows_v, SPAN), BF16),
            pltpu.VMEM((rows_v, SPAN), F32),
            pltpu.VMEM((count, 2 * fields, packed // 2), BF16),
            pltpu.VMEM((count, 2 * fields, packed // 2), BF16),
            pltpu.VMEM((count, rows_j, packed), F32),
            pltpu.VMEM((count, rows_j, packed), F32),
            pltpu.VMEM((steps, 2 * fields, half), BF16),
            pltpu.VMEM((steps, count, 2 * fields, half), BF16),
            pltpu.VMEM((count, 2 * fields, 128), BF16),
            pltpu.VMEM((count, 2 * fields, 128), BF16),
            pltpu.SemaphoreType.DMA((2, groups)),
            pltpu.SemaphoreType.DMA((3,)),
        ]
        + [pltpu.SemaphoreType.DMA((count - 1,))] * 4
        + [pltpu.SemaphoreType.DMA((steps, count - 1))] * 2
        + [pltpu.SemaphoreType.DMA((count - 1,))] * 2,
        compiler_params=pltpu.CompilerParams(
            collective_id=0, has_side_effects=True, vmem_limit_bytes=56 * 2**20
        ),
        name="steps",
    )(
        spectrum.reshape(fields, slots, degrees),
        legendre.reshape(groups, size, degrees),
        order_of_slot,
        row.reshape(points), col.reshape(points), weight.reshape(points),
        order_of_slot, reduced_length, gauss_weight,
    )
    out = pl.pallas_call(
        functools.partial(inverse_kernel, slots),
        out_shape=jax.ShapeDtypeStruct((fields, slots, degrees), BF16),
        in_specs=[VMEM_SPEC, VMEM_SPEC, SMEM_SPEC],
        out_specs=pl.BlockSpec(memory_space=pl.ANY),
        scratch_shapes=[
            pltpu.VMEM((groups, fields, GROUP, degrees), BF16),
            pltpu.SemaphoreType.DMA((groups,)),
        ],
        compiler_params=pltpu.CompilerParams(vmem_limit_bytes=24 * 2**20),
        name="inverse",
    )(coefs, legendre.reshape(groups, size, degrees), order_of_slot)
    return out.reshape(spectrum.shape)


def per_device(
    spectrum,
    legendre,
    order_of_slot,
    reduced_length,
    gauss_weight,
    depart_row,
    depart_col,
    depart_weight,
):
    own_index = lax.axis_index("wave")
    count = lax.axis_size("wave")
    slot_count = legendre.shape[0]
    orders_total = order_of_slot.shape[0]
    variables, level_count = spectrum.shape[:2]
    assert level_count == 1
    steps = depart_row.shape[0]
    grid_width = depart_row.shape[-1]
    stencil = depart_row.shape[2]
    fields = variables
    real_blocks = grid_width // BLOCK
    blocks = padded_blocks(grid_width)

    stride = orders_total // count
    longest = half_rows(count - 1, stride)
    fits = (
        slot_count % GROUP == 0 and 128 < slot_count <= 256 and 2 * fields == 8
        and legendre.shape[1] == 8 and count == 8 and stride == slot_count
        and orders_total % 256 == 0 and orders_total * grid_width < 2**24
        and grid_width % SPAN == 0 and grid_width // SPAN <= 24
        and -(-longest // 3) * WIDE <= grid_width
    )
    if fits:
        return fused(
            spectrum, legendre, order_of_slot, reduced_length, gauss_weight,
            depart_row, depart_col, depart_weight, count,
        )

    length = lax.dynamic_index_in_dim(reduced_length, own_index, keepdims=False)
    own_orders = lax.dynamic_slice_in_dim(order_of_slot, own_index * slot_count, slot_count)
    degrees = jnp.arange(legendre.shape[2], dtype=jnp.int32)
    masked = jnp.where(
        degrees[None, None, :] >= own_orders[:, None, None], legendre, jnp.zeros((), BF16)
    )
    order_limit = jnp.minimum(orders_total, (length - 1) // 2)
    cos_rows, sin_rows = phase_rows(length, order_of_slot, blocks)
    active = (order_of_slot < order_limit).astype(F32)[None, :]
    fc, fs = pl.pallas_call(
        build_table,
        out_shape=[jax.ShapeDtypeStruct((BLOCK, orders_total), BF16)] * 2,
        in_specs=[VMEM_SPEC] * 3,
        out_specs=[VMEM_SPEC] * 2,
        scratch_shapes=[pltpu.VMEM((RADIX * RADIX, orders_total), F32)] * 2,
        name="table",
    )(cos_rows, sin_rows, active)
    length1 = length.reshape(1)
    grid_scale = (1.0 / jnp.sqrt(order_limit.astype(F32))).reshape(1)
    coef_scale = (gauss_weight[0] * jnp.sqrt(2.0 / length.astype(F32))).reshape(1)

    synth = pl.pallas_call(
        functools.partial(synth_kernel, blocks),
        out_shape=jax.ShapeDtypeStruct((fields * blocks, BLOCK), BF16),
        in_specs=[VMEM_SPEC] * 5 + [SMEM_SPEC] * 2,
        out_specs=VMEM_SPEC,
        name="synth",
    )
    grid_step = pl.pallas_call(
        functools.partial(grid_kernel, fields, blocks, real_blocks),
        out_shape=jax.ShapeDtypeStruct((2 * fields, orders_total), BF16),
        in_specs=[VMEM_SPEC] * 8 + [SMEM_SPEC] * 2,
        out_specs=VMEM_SPEC,
        scratch_shapes=[pltpu.VMEM((fields * blocks, BLOCK), F32)],
        name="grid_step",
    )
    spectral = spectrum.reshape(2 * fields, slot_count, -1)
    fourier = jnp.einsum("vsn,sjn->jvs", spectral, masked, preferred_element_type=F32)
    gram = jnp.einsum("sjn,skn->sjk", masked, masked, preferred_element_type=F32)
    forward = [(i, i + 1) for i in range(count - 1)]
    backward = [(i + 1, i) for i in range(count - 1)]
    for k in range(steps):
        gathered = lax.all_to_all(fourier.astype(BF16), "wave", split_axis=0, concat_axis=2, tiled=True)
        own = synth(
            gathered.reshape(2 * fields, orders_total), cos_rows, sin_rows, fc, fs, length1, grid_scale
        )
        low = lax.ppermute(own, "wave", forward)
        high = lax.ppermute(own, "wave", backward)
        coeffs = grid_step(
            jnp.concatenate([low, own, high], axis=0),
            depart_row[k].reshape(1, stencil, 1, grid_width),
            depart_col[k].reshape(1, stencil, 1, grid_width),
            depart_weight[k].reshape(1, stencil, 1, grid_width),
            cos_rows, sin_rows, fc, fs, length1, coef_scale,
        )
        returned = lax.all_to_all(
            coeffs.reshape(1, 2 * fields, orders_total), "wave", split_axis=2, concat_axis=0, tiled=True
        )
        if k + 1 < steps:
            fourier = jnp.einsum("jvs,sjk->kvs", returned.astype(F32), gram, precision="highest")
    final = jnp.einsum("jvs,sjn->vsn", returned, masked, preferred_element_type=F32).astype(BF16)
    return final.reshape(spectrum.shape)


def solution(mesh):
    placed = (
        P(None, "lev", None, "wave", None),
        P("wave", None, None),
        P(),
        P(),
        P("wave"),
        P(None, "lev", None, "wave", None),
        P(None, "lev", None, "wave", None),
        P(None, "lev", None, "wave", None),
    )
    return jax.shard_map(
        per_device,
        mesh=mesh,
        in_specs=placed,
        out_specs=P(None, "lev", None, "wave", None),
        check_vma=False,
    )
```

```python
import functools
import math

import jax
import jax.numpy as jnp
from jax import lax
from jax.experimental import pallas as pl
from jax.experimental.pallas import tpu as pltpu
from jax.sharding import PartitionSpec as P

BLOCK = 512
RADIX = 8
FULL_TURN = 2.0 * math.pi
F32 = jnp.float32
BF16 = jnp.bfloat16

VMEM_SPEC = pl.BlockSpec(memory_space=pltpu.VMEM)
SMEM_SPEC = pl.BlockSpec(memory_space=pltpu.SMEM)


def padded_blocks(grid_width):
    return -(-(grid_width // BLOCK) // 16) * 16


def phase_rows(length, orders, blocks):
    digits = jnp.arange(RADIX, dtype=jnp.int32)
    steps = [digits, digits * RADIX, digits * RADIX * RADIX]
    steps.append(jnp.arange(blocks, dtype=jnp.int32) * BLOCK)
    steps = jnp.concatenate(steps)
    phases = steps[:, None] * orders[None, :] % length
    angles = phases.astype(F32) * (jnp.float32(FULL_TURN) / length.astype(F32))
    return jnp.cos(angles), jnp.sin(angles)


def build_table(cos_ref, sin_ref, active_ref, fc_ref, fs_ref, ca_ref, sa_ref):
    active = active_ref[...]
    cos_low = cos_ref[0:RADIX, :] * active
    sin_low = sin_ref[0:RADIX, :] * active
    cos_mid = cos_ref[RADIX : 2 * RADIX, :]
    sin_mid = sin_ref[RADIX : 2 * RADIX, :]
    for a in range(RADIX):
        c = cos_ref[2 * RADIX + a : 2 * RADIX + a + 1, :]
        s = sin_ref[2 * RADIX + a : 2 * RADIX + a + 1, :]
        ca_ref[a * RADIX : (a + 1) * RADIX, :] = c * cos_mid - s * sin_mid
        sa_ref[a * RADIX : (a + 1) * RADIX, :] = s * cos_mid + c * sin_mid

    def body(i, carry):
        cos_parts, sin_parts = [], []
        for k in range(2):
            c = ca_ref[pl.ds(2 * i + k, 1), :]
            s = sa_ref[pl.ds(2 * i + k, 1), :]
            cos_parts.append(c * cos_low - s * sin_low)
            sin_parts.append(-(s * cos_low + c * sin_low))
        rows = pl.ds(pl.multiple_of(i * 2 * RADIX, 2 * RADIX), 2 * RADIX)
        fc_ref[rows, :] = jnp.concatenate(cos_parts, axis=0).astype(BF16)
        fs_ref[rows, :] = jnp.concatenate(sin_parts, axis=0).astype(BF16)
        return carry

    lax.fori_loop(0, RADIX * RADIX // 2, body, 0)


def synthesize(coeffs, cos_block, sin_block, fc_ref, fs_ref, length, scale):
    fields = coeffs.shape[0] // 2
    blocks = cos_block.shape[0]
    reals, imags = [], []
    for v in range(fields):
        real = coeffs[2 * v : 2 * v + 1]
        imag = coeffs[2 * v + 1 : 2 * v + 2]
        reals.append((real * cos_block - imag * sin_block).astype(BF16))
        imags.append((real * sin_block + imag * cos_block).astype(BF16))
    dims = (((1,), (1,)), ((), ()))
    out = lax.dot_general(
        jnp.concatenate(reals, axis=0), fc_ref[...], dims, preferred_element_type=F32
    ) + lax.dot_general(
        jnp.concatenate(imags, axis=0), fs_ref[...], dims, preferred_element_type=F32
    )
    row = lax.broadcasted_iota(jnp.int32, out.shape, 0) % blocks
    point = row * BLOCK + lax.broadcasted_iota(jnp.int32, out.shape, 1)
    return jnp.where(point < length, out * scale, 0.0)


def synth_kernel(blocks, coef_ref, cos_ref, sin_ref, fc_ref, fs_ref, len_ref, scale_ref, out_ref):
    out_ref[...] = synthesize(
        coef_ref[...].astype(F32),
        cos_ref[3 * RADIX : 3 * RADIX + blocks, :],
        sin_ref[3 * RADIX : 3 * RADIX + blocks, :],
        fc_ref,
        fs_ref,
        len_ref[0],
        scale_ref[0],
    ).astype(BF16)


def gather_block(b, k, table, row_ref, col_ref, weight_ref, fields, blocks):
    stencil = col_ref.shape[1]
    half = 256
    lanes = pl.ds(pl.multiple_of(b * BLOCK, BLOCK), BLOCK)
    iota_half = lax.broadcasted_iota(jnp.int32, (half, BLOCK), 0).astype(F32).astype(BF16)
    iota_rows = lax.broadcasted_iota(jnp.int32, (3 * blocks, BLOCK), 0)
    one = jnp.ones((), BF16)
    zero = jnp.zeros((), BF16)
    acc = [jnp.zeros((blocks, BLOCK), F32) for _ in range(fields)]
    for p in range(stencil):
        col = col_ref[k, p, :, lanes]
        row = row_ref[k, p, :, lanes]
        weight = weight_ref[k, p, :, lanes]
        point = col % BLOCK
        halves = []
        for h in range(BLOCK // half):
            local = point - h * half
            key = jnp.where((local >= 0) & (local < half), local, -1).astype(F32).astype(BF16)
            halves.append(jnp.where(iota_half == key, one, zero))
        onehot = jnp.concatenate(halves, axis=0)
        found = jnp.dot(table, onehot, preferred_element_type=F32)
        which = (row + 1) * blocks + col // BLOCK
        chosen = jnp.where(iota_rows == which, weight, 0.0)
        for r in range(3):
            sel = chosen[r * blocks : (r + 1) * blocks]
            for v in range(fields):
                start = (r * fields + v) * blocks
                acc[v] = acc[v] + found[start : start + blocks] * sel
    return [jnp.sum(a, axis=0, keepdims=True) for a in acc]


def advance(table, k, row_ref, col_ref, weight_ref, new_ref, length, fields, blocks, real_blocks):
    new_ref[...] = jnp.zeros_like(new_ref)

    def body(b, carry):
        interp = gather_block(b, k, table, row_ref, col_ref, weight_ref, fields, blocks)
        point = b * BLOCK + lax.broadcasted_iota(jnp.int32, (1, BLOCK), 1)
        for v in range(fields):
            value = interp[v] + 0.5 * interp[(v + 1) % fields] * jnp.tanh(interp[(v + 2) % fields])
            new_ref[pl.ds(v * blocks + b, 1), :] = jnp.where(point < length, value, 0.0)
        return carry

    lax.fori_loop(0, real_blocks, body, 0)


def analyse(new_ref, cos_block, sin_block, fc_ref, fs_ref, scale):
    blocks = cos_block.shape[0]
    fields = new_ref.shape[0] // blocks
    newgrid = new_ref[...].astype(BF16)
    part_real = jnp.dot(newgrid, fc_ref[...], preferred_element_type=F32)
    part_imag = jnp.dot(newgrid, fs_ref[...], preferred_element_type=F32)
    out = []
    for v in range(fields):
        pr = part_real[v * blocks : (v + 1) * blocks]
        pi = part_imag[v * blocks : (v + 1) * blocks]
        real = jnp.sum(pr * cos_block + pi * sin_block, axis=0, keepdims=True)
        imag = jnp.sum(pi * cos_block - pr * sin_block, axis=0, keepdims=True)
        out += [real * scale, imag * scale]
    return out


def grid_kernel(
    fields, blocks, real_blocks,
    table_ref, row_ref, col_ref, weight_ref, cos_ref, sin_ref, fc_ref, fs_ref, len_ref, scale_ref,
    out_ref, new_ref,
):
    advance(
        table_ref[...], 0, row_ref, col_ref, weight_ref, new_ref, len_ref[0],
        fields, blocks, real_blocks,
    )
    rows = analyse(
        new_ref,
        cos_ref[3 * RADIX : 3 * RADIX + blocks, :],
        sin_ref[3 * RADIX : 3 * RADIX + blocks, :],
        fc_ref,
        fs_ref,
        scale_ref[0],
    )
    out_ref[...] = jnp.concatenate(rows, axis=0).astype(BF16)


SPAN = 256
WIDE = 3 * SPAN
GROUP = 16
MESH = pl.DeviceIdType.MESH
HBM_SPEC = pl.BlockSpec(memory_space=pltpu.HBM)


def half_rows(lat, stride):
    return (20 + 4 * ((lat + 1) * stride - 1) + SPAN - 1) // SPAN


def unit_turns(steps, orders, length):
    product = steps * orders
    inverse = 1.0 / length
    rest = product - jnp.floor(product * inverse + 0.5) * length
    x = rest * (inverse * (0.25 * FULL_TURN))
    y = x * x
    s = x * (1.0 + y * (-1.0 / 6 + y * (1.0 / 120 + y * (-1.0 / 5040 + y * (1.0 / 362880)))))
    c = 1.0 + y * (-0.5 + y * (1.0 / 24 + y * (-1.0 / 720 + y * (1.0 / 40320))))
    s, c = 2.0 * s * c, 1.0 - 2.0 * s * s
    return 1.0 - 2.0 * s * s, 2.0 * s * c


def tables(p, orders, length, limit, cos_ref, sin_ref, fc_ref, fs_ref, ca_ref, sa_ref):
    shape = (8, orders.shape[1])
    digit = lax.broadcasted_iota(jnp.int32, shape, 0)
    digit_f = digit.astype(F32)
    length_f = jnp.full(shape, length.astype(F32))
    orders_f = jnp.broadcast_to(orders.astype(F32), shape)
    active = jnp.where(orders_f < limit.astype(F32), 1.0, 0.0)
    cos_b, sin_b = unit_turns(digit_f * SPAN, orders_f, length_f)
    mixed = jnp.where(digit < 4, digit_f * 64, (digit_f - 4.0) * (8 * SPAN))
    cos_h, sin_h = unit_turns(mixed, orders_f, length_f)
    cos_ref[p, 0:8, :] = cos_b
    sin_ref[p, 0:8, :] = sin_b
    for t in range(1, cos_ref.shape[1] // 8):
        c, s = cos_h[4 + t : 5 + t], sin_h[4 + t : 5 + t]
        cos_ref[p, 8 * t : 8 * t + 8, :] = c * cos_b - s * sin_b
        sin_ref[p, 8 * t : 8 * t + 8, :] = s * cos_b + c * sin_b
    cos_m, sin_m = unit_turns(digit_f * 8, orders_f, length_f)
    for t in range(SPAN // 64):
        c, s = cos_h[t : t + 1], sin_h[t : t + 1]
        ca_ref[8 * t : 8 * t + 8, :] = c * cos_m - s * sin_m
        sa_ref[8 * t : 8 * t + 8, :] = s * cos_m + c * sin_m
    cos_low, sin_low = unit_turns(digit_f, orders_f, length_f)
    ca_ref[SPAN // 8 : SPAN // 8 + 8, :] = cos_low * active
    sa_ref[SPAN // 8 : SPAN // 8 + 8, :] = sin_low * active

    def body(i, carry):
        cos_l = ca_ref[SPAN // 8 : SPAN // 8 + 8, :]
        sin_l = sa_ref[SPAN // 8 : SPAN // 8 + 8, :]
        cos_parts, sin_parts = [], []
        for k in range(2):
            c = ca_ref[pl.ds(2 * i + k, 1), :]
            s = sa_ref[pl.ds(2 * i + k, 1), :]
            cos_parts.append(c * cos_l - s * sin_l)
            sin_parts.append(-(s * cos_l + c * sin_l))
        rows = pl.ds(pl.multiple_of(i * 16, 16), 16)
        fc_ref[p, rows, :] = jnp.concatenate(cos_parts, axis=0).astype(BF16)
        fs_ref[p, rows, :] = jnp.concatenate(sin_parts, axis=0).astype(BF16)
        return carry

    lax.fori_loop(0, SPAN // 16, body, 0)


def grid_rows(coeffs, cos_block, sin_block, fc, fs, length, scale):
    variables = coeffs.shape[0] // 2
    blocks = cos_block.shape[0]
    reals, imags = [], []
    for v in range(variables):
        real = coeffs[2 * v : 2 * v + 1]
        imag = coeffs[2 * v + 1 : 2 * v + 2]
        reals.append((real * cos_block - imag * sin_block).astype(BF16))
        imags.append((real * sin_block + imag * cos_block).astype(BF16))
    dims = (((1,), (1,)), ((), ()))
    out = lax.dot_general(
        fc, jnp.concatenate(reals, axis=0), dims, preferred_element_type=F32
    ) + lax.dot_general(
        fs, jnp.concatenate(imags, axis=0), dims, preferred_element_type=F32
    )
    out = out.T
    row = lax.broadcasted_iota(jnp.int32, out.shape, 0) % blocks
    point = row * SPAN + lax.broadcasted_iota(jnp.int32, out.shape, 1)
    return jnp.where(point < length, out * scale, 0.0)


def pick_wide(b, k, table, most, row_ref, col_ref, weight_ref, variables):
    stencil = col_ref.shape[1]
    lanes = pl.ds(pl.multiple_of(b * WIDE, WIDE), WIDE)
    iota = lax.broadcasted_iota(jnp.int32, (SPAN, WIDE), 0).astype(F32).astype(BF16)
    sub = lax.broadcasted_iota(jnp.int32, (8, WIDE), 0)
    one = jnp.ones((), BF16)
    zero = jnp.zeros((), BF16)
    starts = [sum(most[:r]) if most[r] else 1024 for r in range(3)]
    acc = [None] * variables
    for p in range(stencil):
        col = col_ref[k, p, :, lanes]
        row = row_ref[k, p, :, lanes]
        weight = weight_ref[k, p, :, lanes]
        key = (col & (SPAN - 1)).astype(F32).astype(BF16)
        onehot = jnp.where(iota == key, one, zero)
        found = jnp.dot(table, onehot, preferred_element_type=F32)
        base = jnp.where(row < 0, starts[0], jnp.where(row > 0, starts[2], starts[1]))
        which = base + (col // SPAN)
        got = [jnp.zeros((8, WIDE), F32) for _ in range(variables)]
        for q in range(table.shape[0] // (8 * variables)):
            hit = sub == which - 8 * q
            for v in range(variables):
                start = (q * variables + v) * 8
                got[v] = jnp.where(hit, found[start : start + 8], got[v])
        for v in range(variables):
            term = got[v] * weight
            acc[v] = term if p == 0 else acc[v] + term
    return [jnp.sum(a, axis=0, keepdims=True) for a in acc]


def gather(k, most, turns, own_ref, tab_ref, row_ref, col_ref, weight_ref, new_ref, variables):
    blocks = own_ref.shape[1] // variables
    fill = -sum(most) % 8
    groups = (sum(most) + fill) // 8
    lists = []
    for v in range(variables):
        rows = [own_ref[r, v * blocks : v * blocks + most[r], :] for r in range(3) if most[r]]
        if fill:
            rows.append(jnp.zeros((fill, SPAN), F32))
        lists.append(jnp.concatenate(rows, axis=0))
    parts = [lists[v][8 * t : 8 * t + 8] for t in range(groups) for v in range(variables)]
    size = 8 * len(parts)
    tab_ref[0:size, :] = jnp.concatenate(parts, axis=0).astype(BF16)

    def body(b, carry):
        interp = pick_wide(
            b, k, tab_ref[0:size, :], most, row_ref, col_ref, weight_ref, variables
        )
        for v in range(variables):
            for t in range(WIDE // SPAN):
                new_ref[pl.ds(v * blocks + b * (WIDE // SPAN) + t, 1), :] = interp[v][
                    :, t * SPAN : (t + 1) * SPAN
                ]
        return carry

    lax.fori_loop(0, turns, body, 0)


def new_grid(new_ref, length, variables):
    blocks = new_ref.shape[0] // variables
    interp = [new_ref[v * blocks : (v + 1) * blocks, :] for v in range(variables)]
    shape = interp[0].shape
    point = lax.broadcasted_iota(jnp.int32, shape, 0) * SPAN + lax.broadcasted_iota(jnp.int32, shape, 1)
    inside = point < length
    out = []
    for v in range(variables):
        value = interp[v] + 0.5 * interp[(v + 1) % variables] * jnp.tanh(interp[(v + 2) % variables])
        out.append(jnp.where(inside, value, 0.0))
    return jnp.concatenate(out, axis=0).astype(BF16)


def analyse_rows(newgrid, cos_block, sin_block, fc, fs, scale):
    blocks = cos_block.shape[0]
    part_real = jnp.dot(newgrid, fc, preferred_element_type=F32)
    part_imag = jnp.dot(newgrid, fs, preferred_element_type=F32)
    out = []
    for v in range(newgrid.shape[0] // blocks):
        pr = part_real[v * blocks : (v + 1) * blocks]
        pi = part_imag[v * blocks : (v + 1) * blocks]
        real = jnp.sum(pr * cos_block + pi * sin_block, axis=0, keepdims=True)
        imag = jnp.sum(pi * cos_block - pr * sin_block, axis=0, keepdims=True)
        out += [real * scale, imag * scale]
    return jnp.concatenate(out, axis=0)


def order_rows(first, orders_ref):
    sub = lax.broadcasted_iota(jnp.int32, (8, 128), 0)
    parts = []
    for t in range(GROUP // 8):
        part = jnp.full((8, 128), orders_ref[first + 8 * t], jnp.int32)
        for i in range(1, 8):
            part = jnp.where(sub == i, orders_ref[first + 8 * t + i], part)
        parts.append(part)
    return jnp.concatenate(parts, axis=0)[:, :1]


def own_slots(both, rows_j, width, inner):
    size = GROUP * rows_j
    row = lax.broadcasted_iota(jnp.int32, (size, width), 0) // rows_j
    col = lax.broadcasted_iota(jnp.int32, (size, width), 1)
    col = col % GROUP if inner else col // rows_j
    return jnp.sum(jnp.where(row == col, both, 0.0).reshape(GROUP, rows_j, width), axis=0)


def forward_group(g, first, fields, rows_j, spec_ref, leg_ref, orders_ref, four_ref):
    degrees = spec_ref.shape[3]
    degree = lax.broadcasted_iota(jnp.int32, (GROUP, degrees), 1)
    keep = jnp.where(degree >= order_rows(first + g * GROUP, orders_ref), 1.0, 0.0).astype(BF16)
    state = jnp.concatenate([spec_ref[g, v] * keep for v in range(fields)], axis=0)
    both = lax.dot_general(
        leg_ref[g], state, (((1,), (1,)), ((), ())), preferred_element_type=F32
    )
    four_ref[g] = own_slots(both, rows_j, fields * GROUP, True)


def gram_group(g, first, rows_j, leg_ref, orders_ref, square_ref):
    degrees = leg_ref.shape[2]
    degree = lax.broadcasted_iota(jnp.int32, (2 * rows_j, degrees), 1)
    sub = lax.broadcasted_iota(jnp.int32, (2 * rows_j, 128), 0)
    parts = []
    for pair in range(GROUP // 2):
        slot = first + g * GROUP + 2 * pair
        order = jnp.where(sub < rows_j, orders_ref[slot], orders_ref[slot + 1])[:, :1]
        keep = jnp.where(degree >= order, 1.0, 0.0).astype(BF16)
        parts.append(leg_ref[g, 2 * pair * rows_j : 2 * (pair + 1) * rows_j, :] * keep)
    both = lax.dot_general(
        leg_ref[g], jnp.concatenate(parts, axis=0), (((1,), (1,)), ((), ())),
        preferred_element_type=F32,
    )
    square_ref[g] = own_slots(both, rows_j, GROUP * rows_j, False)


def gram_of(square_ref, gram_ref, rows_j):
    groups, _, size = square_ref.shape
    row = lax.broadcasted_iota(jnp.int32, (size, size), 0)
    col = lax.broadcasted_iota(jnp.int32, (size, size), 1)
    swap = (row // rows_j == col % GROUP) & (row % rows_j == col // GROUP)
    turned = jnp.dot(
        square_ref[...].reshape(groups * rows_j, size), jnp.where(swap, 1.0, 0.0),
        preferred_element_type=F32, precision="highest",
    )
    for h in range(groups):
        rows = turned[h * rows_j : (h + 1) * rows_j]
        for j in range(rows_j):
            gram_ref[j, :, h * GROUP : (h + 1) * GROUP] = rows[:, j * GROUP : (j + 1) * GROUP]


def steps_kernel(
    steps, count, fields, slots, stride,
    spec_hbm, leg_hbm, orders_ref, row_hbm, col_hbm, weight_hbm, order_ref, len_ref, gauss_ref,
    out_ref,
    spec_ref, leg_ref, row_ref, col_ref, weight_ref,
    four_ref, square_ref, vjs_ref, gram_ref, pack_ref,
    cos_ref, sin_ref, fc_ref, fs_ref, ca_ref, sa_ref,
    coef_ref, mine_ref, mix_ref, own_ref, tab_ref, new_ref,
    a_send, a_recv, g_send, g_recv, all_send, all_recv, b_send, b_recv,
    load_sem, point_sem, a_ssem, a_rsem, g_ssem, g_rsem, all_ssem, all_rsem, b_ssem, b_rsem,
):
    rows_j = leg_ref.shape[1] // GROUP
    groups = slots // GROUP
    variables = fields // 2
    total = orders_ref.shape[0]
    blocks = cos_ref.shape[1]
    cut = 3 * slots

    def loads(g):
        slot_rows = pl.ds(pl.multiple_of(g * GROUP, GROUP), GROUP)
        return (
            pltpu.make_async_copy(leg_hbm.at[g], leg_ref.at[g], load_sem.at[0, g]),
            pltpu.make_async_copy(spec_hbm.at[:, slot_rows, :], spec_ref.at[g], load_sem.at[1, g]),
        )

    points = [
        pltpu.make_async_copy(row_hbm, row_ref, point_sem.at[0]),
        pltpu.make_async_copy(col_hbm, col_ref, point_sem.at[1]),
        pltpu.make_async_copy(weight_hbm, weight_ref, point_sem.at[2]),
    ]
    me = lax.axis_index("wave")
    peers = [lax.rem(me + d, count) for d in range(1, count)]
    barrier = pltpu.get_barrier_semaphore()
    for peer in peers:
        pl.semaphore_signal(barrier, inc=1, device_id={"wave": peer}, device_id_type=MESH)
    for g in range(groups):
        for copy in loads(g):
            copy.start()
    for copy in points:
        copy.start()
    vjs_ref[...] = jnp.zeros_like(vjs_ref)
    gram_ref[...] = jnp.zeros_like(gram_ref)
    pack_ref[...] = jnp.zeros_like(pack_ref)
    new_ref[...] = jnp.zeros_like(new_ref)
    coef_ref[...] = jnp.zeros_like(coef_ref)
    mine_ref[...] = jnp.zeros_like(mine_ref)
    orders = orders_ref[...].reshape(1, total)
    lats = [jnp.clip(me + r - 1, 0, count - 1) for r in range(3)]
    lengths = [len_ref[lat] for lat in lats]
    limits = [jnp.minimum(total, (length - 1) // 2) for length in lengths]
    first = me * slots

    for r in range(3):
        tables(
            r, orders, lengths[r], limits[r], cos_ref, sin_ref, fc_ref, fs_ref, ca_ref, sa_ref
        )

    for g in range(groups):
        for copy in loads(g):
            copy.wait()
    for g in range(groups):
        forward_group(g, first, fields, rows_j, spec_ref, leg_ref, order_ref, four_ref)
    for h in range(groups):
        for v in range(fields):
            vjs_ref[v, :, h * GROUP : (h + 1) * GROUP] = four_ref[
                h, :, v * GROUP : (v + 1) * GROUP
            ]

    def pack(source, send):
        for p in range(count):
            for r in range(3):
                pack_ref[p, :, r * slots : (r + 1) * slots] = source[
                    min(max(p + r - 1, 0), count - 1)
                ][:, :slots]
        for p in range(count):
            send(p)

    def send_first(p):
        half = pack_ref.shape[2] // 2
        a_send[p] = jnp.concatenate(
            [pack_ref[p, :, :half], pack_ref[p, :, half:]], axis=0
        ).astype(BF16)

    def send_gram(p):
        g_send[p] = pack_ref[p]

    def exchange(send, recv, ssem, rsem):
        copies = []
        for d, peer in enumerate(peers):
            copy = pltpu.make_async_remote_copy(
                src_ref=send(peer), dst_ref=recv.at[me], send_sem=ssem.at[d],
                recv_sem=rsem.at[d], device_id={"wave": peer}, device_id_type=MESH,
            )
            copy.start()
            copies.append(copy)
        return copies

    pack(jnp.swapaxes(vjs_ref[...], 0, 1), send_first)
    pl.semaphore_wait(barrier, count - 1)
    copies = exchange(lambda peer: a_send.at[peer], a_recv, a_ssem, a_rsem)
    a_recv[me] = a_send[me]

    def gram(g, carry):
        gram_group(g, first, rows_j, leg_ref, order_ref, square_ref)
        return carry

    lax.fori_loop(0, groups, gram, 0, unroll=2)
    gram_of(square_ref, gram_ref, rows_j)
    pack(gram_ref[...], send_gram)
    for copy in copies:
        copy.wait()
    gram_copies = exchange(lambda peer: g_send.at[peer], g_recv, g_ssem, g_rsem)
    g_recv[me] = g_send[me]
    for copy in points:
        copy.wait()
    for i in range(count):
        half = a_recv.shape[2]
        both = a_recv[i].astype(F32)
        both = jnp.concatenate([both[:fields], both[fields:]], axis=1)
        for r in range(3):
            coef_ref[r, :, i * slots : (i + 1) * slots] = both[:, r * slots : (r + 1) * slots]

    shape = (1, total)
    coef_scale = gauss_ref[0] * jnp.sqrt(2.0 / jnp.full(shape, lengths[1].astype(F32)))
    inside = [jnp.where(me > 0, 1.0, 0.0), 1.0, jnp.where(me < count - 1, 1.0, 0.0)]
    scales = [
        inside[r] / jnp.sqrt(jnp.full((1, SPAN), limits[r].astype(F32))) for r in range(3)
    ]
    turns = (half_rows(me, stride) + WIDE // SPAN - 1) // (WIDE // SPAN)
    most = [half_rows(count - 4 + r, stride) for r in range(1, 4)]
    for k in range(steps):
        for r in range(3):
            own_ref[r] = grid_rows(
                coef_ref[r], cos_ref[r], sin_ref[r], fc_ref[r], fs_ref[r], lengths[r], scales[r]
            )
        args = (own_ref, tab_ref, row_ref, col_ref, weight_ref, new_ref, variables)

        @pl.when(me < count - 1)
        def _():
            gather(k, [most[0], most[1], most[2]], turns, *args)

        @pl.when(me == count - 1)
        def _():
            gather(k, [most[1], most[2], 0], turns, *args)

        mine = analyse_rows(
            new_grid(new_ref, lengths[1], variables),
            cos_ref[1], sin_ref[1], fc_ref[1], fs_ref[1], coef_scale,
        )
        if k + 1 < steps:
            half = total // 2
            all_send[k] = jnp.concatenate([mine[:, :half], mine[:, half:]], axis=0).astype(BF16)
            copies = exchange(
                lambda peer: all_send.at[k], all_recv.at[k], all_ssem.at[k], all_rsem.at[k]
            )
            all_recv[k, me] = all_send[k]
            if k == 0:
                for copy in gram_copies:
                    copy.wait()
                for i in range(count):
                    for r in range(3):
                        mix_ref[r, :, i * slots : (i + 1) * slots] = g_recv[
                            i, :, r * slots : (r + 1) * slots
                        ]
            for copy in copies:
                copy.wait()
            sums = [None] * 3
            for j in range(count):
                both = all_recv[k, j].astype(F32)
                both = jnp.concatenate([both[:fields], both[fields:]], axis=1)
                for r in range(3):
                    term = mix_ref[r, j : j + 1, :] * both
                    sums[r] = term if j == 0 else sums[r] + term
            for r in range(3):
                coef_ref[r] = sums[r]
        else:
            mine_ref[:, :total] = mine
            for i in range(count):
                b_send[i] = jnp.concatenate(
                    [
                        mine_ref[:, i * slots : i * slots + 128],
                        mine_ref[:, i * slots + 128 : i * slots + 256],
                    ],
                    axis=0,
                ).astype(BF16)
            copies = exchange(lambda peer: b_send.at[peer], b_recv, b_ssem, b_rsem)
            b_recv[me] = b_send[me]
            for copy in copies:
                copy.wait()
    out_ref[...] = b_recv[...]


def inverse_kernel(slots, coef_ref, leg_ref, orders_ref, out_hbm, out_ref, out_sem):
    groups, size, degrees = leg_ref.shape
    rows_j = size // GROUP
    fields = coef_ref.shape[1] // 2
    me = lax.axis_index("wave")

    def store(g):
        slot_rows = pl.ds(pl.multiple_of(g * GROUP, GROUP), GROUP)
        return pltpu.make_async_copy(out_ref.at[g], out_hbm.at[:, slot_rows, :], out_sem.at[g])

    last = jnp.swapaxes(coef_ref[...].astype(F32), 0, 1)
    row = lax.broadcasted_iota(jnp.int32, (size, fields * GROUP), 0) // rows_j
    col = lax.broadcasted_iota(jnp.int32, (size, fields * GROUP), 1) % GROUP
    own = row == col
    degree = lax.broadcasted_iota(jnp.int32, (GROUP, degrees), 1)
    for g in range(groups):
        half, lane = divmod(g * GROUP, 128)
        coefs = jnp.concatenate(
            [last[half * fields + v, :, lane : lane + GROUP] for v in range(fields)], axis=1
        )
        tiled = jnp.concatenate([coefs] * GROUP, axis=0)
        spread = jnp.where(own, tiled, 0.0).T.astype(BF16)
        keep = degree >= order_rows(me * slots + g * GROUP, orders_ref)
        out = jnp.dot(spread, leg_ref[g], preferred_element_type=F32)
        for v in range(fields):
            rows = jnp.where(keep, out[v * GROUP : (v + 1) * GROUP], 0.0)
            out_ref[g, v] = rows.astype(BF16)
        store(g).start()
    for g in range(groups):
        store(g).wait()


def fused(spectrum, legendre, order_of_slot, reduced_length, gauss_weight, row, col, weight, count):
    slots, rows_j, degrees = legendre.shape
    fields = 2 * spectrum.shape[0]
    total = order_of_slot.shape[0]
    steps, stencil, grid_width = row.shape[0], row.shape[2], row.shape[-1]
    blocks = -(-(grid_width // SPAN) // 8) * 8
    stride = total // count
    groups = slots // GROUP
    size = GROUP * rows_j
    lanes = -(-slots // 128) * 128
    packed = -(-3 * slots // 256) * 256
    rows_v = fields // 2 * blocks
    half = total // 2
    points = (steps, stencil, 1, grid_width)
    coefs = pl.pallas_call(
        functools.partial(steps_kernel, steps, count, fields, slots, stride),
        out_shape=pltpu.VMEM((count, 2 * fields, 128), BF16),
        in_specs=[HBM_SPEC] * 2 + [VMEM_SPEC] + [HBM_SPEC] * 3 + [SMEM_SPEC] * 3,
        out_specs=VMEM_SPEC,
        scratch_shapes=[
            pltpu.VMEM((groups, fields, GROUP, degrees), BF16),
            pltpu.VMEM((groups, size, degrees), BF16),
            pltpu.VMEM(points, jnp.int32),
            pltpu.VMEM(points, jnp.int32),
            pltpu.VMEM(points, F32),
            pltpu.VMEM((groups, rows_j, fields * GROUP), F32),
            pltpu.VMEM((groups, rows_j, size), F32),
            pltpu.VMEM((fields, rows_j, lanes), F32),
            pltpu.VMEM((rows_j, rows_j, lanes), F32),
            pltpu.VMEM((count, fields, packed), F32),
            pltpu.VMEM((3, blocks, total), F32),
            pltpu.VMEM((3, blocks, total), F32),
            pltpu.VMEM((3, SPAN, total), BF16),
            pltpu.VMEM((3, SPAN, total), BF16),
            pltpu.VMEM((SPAN // 8 + 8, total), F32),
            pltpu.VMEM((SPAN // 8 + 8, total), F32),
            pltpu.VMEM((3, fields, total), F32),
            pltpu.VMEM((fields, total + 128), F32),
            pltpu.VMEM((3, rows_j, total), F32),
            pltpu.VMEM((3, rows_v, SPAN), F32),
            pltpu.VMEM((3 * rows_v, SPAN), BF16),
            pltpu.VMEM((rows_v, SPAN), F32),
            pltpu.VMEM((count, 2 * fields, packed // 2), BF16),
            pltpu.VMEM((count, 2 * fields, packed // 2), BF16),
            pltpu.VMEM((count, rows_j, packed), F32),
            pltpu.VMEM((count, rows_j, packed), F32),
            pltpu.VMEM((steps, 2 * fields, half), BF16),
            pltpu.VMEM((steps, count, 2 * fields, half), BF16),
            pltpu.VMEM((count, 2 * fields, 128), BF16),
            pltpu.VMEM((count, 2 * fields, 128), BF16),
            pltpu.SemaphoreType.DMA((2, groups)),
            pltpu.SemaphoreType.DMA((3,)),
        ]
        + [pltpu.SemaphoreType.DMA((count - 1,))] * 4
        + [pltpu.SemaphoreType.DMA((steps, count - 1))] * 2
        + [pltpu.SemaphoreType.DMA((count - 1,))] * 2,
        compiler_params=pltpu.CompilerParams(
            collective_id=0, has_side_effects=True, vmem_limit_bytes=56 * 2**20
        ),
        name="steps",
    )(
        spectrum.reshape(fields, slots, degrees),
        legendre.reshape(groups, size, degrees),
        order_of_slot,
        row.reshape(points), col.reshape(points), weight.reshape(points),
        order_of_slot, reduced_length, gauss_weight,
    )
    out = pl.pallas_call(
        functools.partial(inverse_kernel, slots),
        out_shape=jax.ShapeDtypeStruct((fields, slots, degrees), BF16),
        in_specs=[VMEM_SPEC, VMEM_SPEC, SMEM_SPEC],
        out_specs=pl.BlockSpec(memory_space=pl.ANY),
        scratch_shapes=[
            pltpu.VMEM((groups, fields, GROUP, degrees), BF16),
            pltpu.SemaphoreType.DMA((groups,)),
        ],
        compiler_params=pltpu.CompilerParams(vmem_limit_bytes=24 * 2**20),
        name="inverse",
    )(coefs, legendre.reshape(groups, size, degrees), order_of_slot)
    return out.reshape(spectrum.shape)


def per_device(
    spectrum,
    legendre,
    order_of_slot,
    reduced_length,
    gauss_weight,
    depart_row,
    depart_col,
    depart_weight,
):
    own_index = lax.axis_index("wave")
    count = lax.axis_size("wave")
    slot_count = legendre.shape[0]
    orders_total = order_of_slot.shape[0]
    variables, level_count = spectrum.shape[:2]
    assert level_count == 1
    steps = depart_row.shape[0]
    grid_width = depart_row.shape[-1]
    stencil = depart_row.shape[2]
    fields = variables
    real_blocks = grid_width // BLOCK
    blocks = padded_blocks(grid_width)

    stride = orders_total // count
    longest = half_rows(count - 1, stride)
    fits = (
        slot_count % GROUP == 0 and 128 < slot_count <= 256 and 2 * fields == 8
        and legendre.shape[1] == 8 and count == 8 and stride == slot_count
        and orders_total % 256 == 0 and orders_total * grid_width < 2**24
        and grid_width % SPAN == 0 and grid_width // SPAN <= 24
        and -(-longest // 3) * WIDE <= grid_width
    )
    if fits:
        return fused(
            spectrum, legendre, order_of_slot, reduced_length, gauss_weight,
            depart_row, depart_col, depart_weight, count,
        )

    length = lax.dynamic_index_in_dim(reduced_length, own_index, keepdims=False)
    own_orders = lax.dynamic_slice_in_dim(order_of_slot, own_index * slot_count, slot_count)
    degrees = jnp.arange(legendre.shape[2], dtype=jnp.int32)
    masked = jnp.where(
        degrees[None, None, :] >= own_orders[:, None, None], legendre, jnp.zeros((), BF16)
    )
    order_limit = jnp.minimum(orders_total, (length - 1) // 2)
    cos_rows, sin_rows = phase_rows(length, order_of_slot, blocks)
    active = (order_of_slot < order_limit).astype(F32)[None, :]
    fc, fs = pl.pallas_call(
        build_table,
        out_shape=[jax.ShapeDtypeStruct((BLOCK, orders_total), BF16)] * 2,
        in_specs=[VMEM_SPEC] * 3,
        out_specs=[VMEM_SPEC] * 2,
        scratch_shapes=[pltpu.VMEM((RADIX * RADIX, orders_total), F32)] * 2,
        name="table",
    )(cos_rows, sin_rows, active)
    length1 = length.reshape(1)
    grid_scale = (1.0 / jnp.sqrt(order_limit.astype(F32))).reshape(1)
    coef_scale = (gauss_weight[0] * jnp.sqrt(2.0 / length.astype(F32))).reshape(1)

    synth = pl.pallas_call(
        functools.partial(synth_kernel, blocks),
        out_shape=jax.ShapeDtypeStruct((fields * blocks, BLOCK), BF16),
        in_specs=[VMEM_SPEC] * 5 + [SMEM_SPEC] * 2,
        out_specs=VMEM_SPEC,
        name="synth",
    )
    grid_step = pl.pallas_call(
        functools.partial(grid_kernel, fields, blocks, real_blocks),
        out_shape=jax.ShapeDtypeStruct((2 * fields, orders_total), BF16),
        in_specs=[VMEM_SPEC] * 8 + [SMEM_SPEC] * 2,
        out_specs=VMEM_SPEC,
        scratch_shapes=[pltpu.VMEM((fields * blocks, BLOCK), F32)],
        name="grid_step",
    )
    spectral = spectrum.reshape(2 * fields, slot_count, -1)
    fourier = jnp.einsum("vsn,sjn->jvs", spectral, masked, preferred_element_type=F32)
    gram = jnp.einsum("sjn,skn->sjk", masked, masked, preferred_element_type=F32)
    forward = [(i, i + 1) for i in range(count - 1)]
    backward = [(i + 1, i) for i in range(count - 1)]
    for k in range(steps):
        gathered = lax.all_to_all(fourier.astype(BF16), "wave", split_axis=0, concat_axis=2, tiled=True)
        own = synth(
            gathered.reshape(2 * fields, orders_total), cos_rows, sin_rows, fc, fs, length1, grid_scale
        )
        low = lax.ppermute(own, "wave", forward)
        high = lax.ppermute(own, "wave", backward)
        coeffs = grid_step(
            jnp.concatenate([low, own, high], axis=0),
            depart_row[k].reshape(1, stencil, 1, grid_width),
            depart_col[k].reshape(1, stencil, 1, grid_width),
            depart_weight[k].reshape(1, stencil, 1, grid_width),
            cos_rows, sin_rows, fc, fs, length1, coef_scale,
        )
        returned = lax.all_to_all(
            coeffs.reshape(1, 2 * fields, orders_total), "wave", split_axis=2, concat_axis=0, tiled=True
        )
        if k + 1 < steps:
            fourier = jnp.einsum("jvs,sjk->kvs", returned.astype(F32), gram, precision="highest")
    final = jnp.einsum("jvs,sjn->vsn", returned, masked, preferred_element_type=F32).astype(BF16)
    return final.reshape(spectrum.shape)


def solution(mesh):
    placed = (
        P(None, "lev", None, "wave", None),
        P("wave", None, None),
        P(),
        P(),
        P("wave"),
        P(None, "lev", None, "wave", None),
        P(None, "lev", None, "wave", None),
        P(None, "lev", None, "wave", None),
    )
    return jax.shard_map(
        per_device,
        mesh=mesh,
        in_specs=placed,
        out_specs=P(None, "lev", None, "wave", None),
        check_vma=False,
    )
```

```python
import functools
import math

import jax
import jax.numpy as jnp
from jax import lax
from jax.experimental import pallas as pl
from jax.experimental.pallas import tpu as pltpu
from jax.sharding import PartitionSpec as P

BLOCK = 512
RADIX = 8
FULL_TURN = 2.0 * math.pi
F32 = jnp.float32
BF16 = jnp.bfloat16

VMEM_SPEC = pl.BlockSpec(memory_space=pltpu.VMEM)
SMEM_SPEC = pl.BlockSpec(memory_space=pltpu.SMEM)


def padded_blocks(grid_width):
    return -(-(grid_width // BLOCK) // 16) * 16


def phase_rows(length, orders, blocks):
    digits = jnp.arange(RADIX, dtype=jnp.int32)
    steps = [digits, digits * RADIX, digits * RADIX * RADIX]
    steps.append(jnp.arange(blocks, dtype=jnp.int32) * BLOCK)
    steps = jnp.concatenate(steps)
    phases = steps[:, None] * orders[None, :] % length
    angles = phases.astype(F32) * (jnp.float32(FULL_TURN) / length.astype(F32))
    return jnp.cos(angles), jnp.sin(angles)


def build_table(cos_ref, sin_ref, active_ref, fc_ref, fs_ref, ca_ref, sa_ref):
    active = active_ref[...]
    cos_low = cos_ref[0:RADIX, :] * active
    sin_low = sin_ref[0:RADIX, :] * active
    cos_mid = cos_ref[RADIX : 2 * RADIX, :]
    sin_mid = sin_ref[RADIX : 2 * RADIX, :]
    for a in range(RADIX):
        c = cos_ref[2 * RADIX + a : 2 * RADIX + a + 1, :]
        s = sin_ref[2 * RADIX + a : 2 * RADIX + a + 1, :]
        ca_ref[a * RADIX : (a + 1) * RADIX, :] = c * cos_mid - s * sin_mid
        sa_ref[a * RADIX : (a + 1) * RADIX, :] = s * cos_mid + c * sin_mid

    def body(i, carry):
        cos_parts, sin_parts = [], []
        for k in range(2):
            c = ca_ref[pl.ds(2 * i + k, 1), :]
            s = sa_ref[pl.ds(2 * i + k, 1), :]
            cos_parts.append(c * cos_low - s * sin_low)
            sin_parts.append(-(s * cos_low + c * sin_low))
        rows = pl.ds(pl.multiple_of(i * 2 * RADIX, 2 * RADIX), 2 * RADIX)
        fc_ref[rows, :] = jnp.concatenate(cos_parts, axis=0).astype(BF16)
        fs_ref[rows, :] = jnp.concatenate(sin_parts, axis=0).astype(BF16)
        return carry

    lax.fori_loop(0, RADIX * RADIX // 2, body, 0)


def synthesize(coeffs, cos_block, sin_block, fc_ref, fs_ref, length, scale):
    fields = coeffs.shape[0] // 2
    blocks = cos_block.shape[0]
    reals, imags = [], []
    for v in range(fields):
        real = coeffs[2 * v : 2 * v + 1]
        imag = coeffs[2 * v + 1 : 2 * v + 2]
        reals.append((real * cos_block - imag * sin_block).astype(BF16))
        imags.append((real * sin_block + imag * cos_block).astype(BF16))
    dims = (((1,), (1,)), ((), ()))
    out = lax.dot_general(
        jnp.concatenate(reals, axis=0), fc_ref[...], dims, preferred_element_type=F32
    ) + lax.dot_general(
        jnp.concatenate(imags, axis=0), fs_ref[...], dims, preferred_element_type=F32
    )
    row = lax.broadcasted_iota(jnp.int32, out.shape, 0) % blocks
    point = row * BLOCK + lax.broadcasted_iota(jnp.int32, out.shape, 1)
    return jnp.where(point < length, out * scale, 0.0)


def synth_kernel(blocks, coef_ref, cos_ref, sin_ref, fc_ref, fs_ref, len_ref, scale_ref, out_ref):
    out_ref[...] = synthesize(
        coef_ref[...].astype(F32),
        cos_ref[3 * RADIX : 3 * RADIX + blocks, :],
        sin_ref[3 * RADIX : 3 * RADIX + blocks, :],
        fc_ref,
        fs_ref,
        len_ref[0],
        scale_ref[0],
    ).astype(BF16)


def gather_block(b, k, table, row_ref, col_ref, weight_ref, fields, blocks):
    stencil = col_ref.shape[1]
    half = 256
    lanes = pl.ds(pl.multiple_of(b * BLOCK, BLOCK), BLOCK)
    iota_half = lax.broadcasted_iota(jnp.int32, (half, BLOCK), 0).astype(F32).astype(BF16)
    iota_rows = lax.broadcasted_iota(jnp.int32, (3 * blocks, BLOCK), 0)
    one = jnp.ones((), BF16)
    zero = jnp.zeros((), BF16)
    acc = [jnp.zeros((blocks, BLOCK), F32) for _ in range(fields)]
    for p in range(stencil):
        col = col_ref[k, p, :, lanes]
        row = row_ref[k, p, :, lanes]
        weight = weight_ref[k, p, :, lanes]
        point = col % BLOCK
        halves = []
        for h in range(BLOCK // half):
            local = point - h * half
            key = jnp.where((local >= 0) & (local < half), local, -1).astype(F32).astype(BF16)
            halves.append(jnp.where(iota_half == key, one, zero))
        onehot = jnp.concatenate(halves, axis=0)
        found = jnp.dot(table, onehot, preferred_element_type=F32)
        which = (row + 1) * blocks + col // BLOCK
        chosen = jnp.where(iota_rows == which, weight, 0.0)
        for r in range(3):
            sel = chosen[r * blocks : (r + 1) * blocks]
            for v in range(fields):
                start = (r * fields + v) * blocks
                acc[v] = acc[v] + found[start : start + blocks] * sel
    return [jnp.sum(a, axis=0, keepdims=True) for a in acc]


def advance(table, k, row_ref, col_ref, weight_ref, new_ref, length, fields, blocks, real_blocks):
    new_ref[...] = jnp.zeros_like(new_ref)

    def body(b, carry):
        interp = gather_block(b, k, table, row_ref, col_ref, weight_ref, fields, blocks)
        point = b * BLOCK + lax.broadcasted_iota(jnp.int32, (1, BLOCK), 1)
        for v in range(fields):
            value = interp[v] + 0.5 * interp[(v + 1) % fields] * jnp.tanh(interp[(v + 2) % fields])
            new_ref[pl.ds(v * blocks + b, 1), :] = jnp.where(point < length, value, 0.0)
        return carry

    lax.fori_loop(0, real_blocks, body, 0)


def analyse(new_ref, cos_block, sin_block, fc_ref, fs_ref, scale):
    blocks = cos_block.shape[0]
    fields = new_ref.shape[0] // blocks
    newgrid = new_ref[...].astype(BF16)
    part_real = jnp.dot(newgrid, fc_ref[...], preferred_element_type=F32)
    part_imag = jnp.dot(newgrid, fs_ref[...], preferred_element_type=F32)
    out = []
    for v in range(fields):
        pr = part_real[v * blocks : (v + 1) * blocks]
        pi = part_imag[v * blocks : (v + 1) * blocks]
        real = jnp.sum(pr * cos_block + pi * sin_block, axis=0, keepdims=True)
        imag = jnp.sum(pi * cos_block - pr * sin_block, axis=0, keepdims=True)
        out += [real * scale, imag * scale]
    return out


def grid_kernel(
    fields, blocks, real_blocks,
    table_ref, row_ref, col_ref, weight_ref, cos_ref, sin_ref, fc_ref, fs_ref, len_ref, scale_ref,
    out_ref, new_ref,
):
    advance(
        table_ref[...], 0, row_ref, col_ref, weight_ref, new_ref, len_ref[0],
        fields, blocks, real_blocks,
    )
    rows = analyse(
        new_ref,
        cos_ref[3 * RADIX : 3 * RADIX + blocks, :],
        sin_ref[3 * RADIX : 3 * RADIX + blocks, :],
        fc_ref,
        fs_ref,
        scale_ref[0],
    )
    out_ref[...] = jnp.concatenate(rows, axis=0).astype(BF16)


SPAN = 256
WIDE = 3 * SPAN
CHUNK = 1280
GROUP = 16
MESH = pl.DeviceIdType.MESH
HBM_SPEC = pl.BlockSpec(memory_space=pltpu.HBM)


def half_rows(lat, stride):
    return (20 + 4 * ((lat + 1) * stride - 1) + SPAN - 1) // SPAN


def unit_turns(steps, orders, length):
    product = steps * orders
    inverse = 1.0 / length
    rest = product - jnp.floor(product * inverse + 0.5) * length
    x = rest * (inverse * (0.25 * FULL_TURN))
    y = x * x
    s = x * (1.0 + y * (-1.0 / 6 + y * (1.0 / 120 + y * (-1.0 / 5040 + y * (1.0 / 362880)))))
    c = 1.0 + y * (-0.5 + y * (1.0 / 24 + y * (-1.0 / 720 + y * (1.0 / 40320))))
    s, c = 2.0 * s * c, 1.0 - 2.0 * s * s
    return 1.0 - 2.0 * s * s, 2.0 * s * c


def tables(p, orders, length, limit, cos_ref, sin_ref, fc_ref, fs_ref, ca_ref, sa_ref):
    shape = (8, orders.shape[1])
    digit = lax.broadcasted_iota(jnp.int32, shape, 0)
    digit_f = digit.astype(F32)
    length_f = jnp.full(shape, length.astype(F32))
    orders_f = jnp.broadcast_to(orders.astype(F32), shape)
    active = jnp.where(orders_f < limit.astype(F32), 1.0, 0.0)
    cos_b, sin_b = unit_turns(digit_f * SPAN, orders_f, length_f)
    mixed = jnp.where(digit < 4, digit_f * 64, (digit_f - 4.0) * (8 * SPAN))
    cos_h, sin_h = unit_turns(mixed, orders_f, length_f)
    cos_ref[p, 0:8, :] = cos_b
    sin_ref[p, 0:8, :] = sin_b
    for t in range(1, cos_ref.shape[1] // 8):
        c, s = cos_h[4 + t : 5 + t], sin_h[4 + t : 5 + t]
        cos_ref[p, 8 * t : 8 * t + 8, :] = c * cos_b - s * sin_b
        sin_ref[p, 8 * t : 8 * t + 8, :] = s * cos_b + c * sin_b
    cos_m, sin_m = unit_turns(digit_f * 8, orders_f, length_f)
    for t in range(SPAN // 64):
        c, s = cos_h[t : t + 1], sin_h[t : t + 1]
        ca_ref[8 * t : 8 * t + 8, :] = c * cos_m - s * sin_m
        sa_ref[8 * t : 8 * t + 8, :] = s * cos_m + c * sin_m
    cos_low, sin_low = unit_turns(digit_f, orders_f, length_f)
    ca_ref[SPAN // 8 : SPAN // 8 + 8, :] = cos_low * active
    sa_ref[SPAN // 8 : SPAN // 8 + 8, :] = sin_low * active

    def body(i, carry):
        cos_l = ca_ref[SPAN // 8 : SPAN // 8 + 8, :]
        sin_l = sa_ref[SPAN // 8 : SPAN // 8 + 8, :]
        cos_parts, sin_parts = [], []
        for k in range(2):
            c = ca_ref[pl.ds(2 * i + k, 1), :]
            s = sa_ref[pl.ds(2 * i + k, 1), :]
            cos_parts.append(c * cos_l - s * sin_l)
            sin_parts.append(-(s * cos_l + c * sin_l))
        rows = pl.ds(pl.multiple_of(i * 16, 16), 16)
        fc_ref[p, rows, :] = jnp.concatenate(cos_parts, axis=0).astype(BF16)
        fs_ref[p, rows, :] = jnp.concatenate(sin_parts, axis=0).astype(BF16)
        return carry

    lax.fori_loop(0, SPAN // 16, body, 0)


def grid_part(coeffs, cos_block, sin_block, fc, fs):
    variables = coeffs.shape[0] // 2
    reals, imags = [], []
    for v in range(variables):
        real = coeffs[2 * v : 2 * v + 1]
        imag = coeffs[2 * v + 1 : 2 * v + 2]
        reals.append((real * cos_block - imag * sin_block).astype(BF16))
        imags.append((real * sin_block + imag * cos_block).astype(BF16))
    dims = (((1,), (1,)), ((), ()))
    return lax.dot_general(
        fc, jnp.concatenate(reals, axis=0), dims, preferred_element_type=F32
    ) + lax.dot_general(
        fs, jnp.concatenate(imags, axis=0), dims, preferred_element_type=F32
    )


def grid_rows(part, blocks, length, scale):
    out = part.T
    row = lax.broadcasted_iota(jnp.int32, out.shape, 0) % blocks
    point = row * SPAN + lax.broadcasted_iota(jnp.int32, out.shape, 1)
    return jnp.where(point < length, out * scale, 0.0)


def pick_wide(b, k, table, most, row_ref, col_ref, weight_ref, variables):
    stencil = col_ref.shape[1]
    lanes = pl.ds(pl.multiple_of(b * WIDE, WIDE), WIDE)
    iota = lax.broadcasted_iota(jnp.int32, (SPAN, WIDE), 0).astype(F32).astype(BF16)
    sub = lax.broadcasted_iota(jnp.int32, (8, WIDE), 0)
    one = jnp.ones((), BF16)
    zero = jnp.zeros((), BF16)
    starts = [sum(most[:r]) if most[r] else 1024 for r in range(3)]
    acc = [None] * variables
    for p in range(stencil):
        col = col_ref[k, p, :, lanes]
        row = row_ref[k, p, :, lanes]
        weight = weight_ref[k, p, :, lanes]
        key = (col & (SPAN - 1)).astype(F32).astype(BF16)
        onehot = jnp.where(iota == key, one, zero)
        found = jnp.dot(table, onehot, preferred_element_type=F32)
        base = jnp.where(row < 0, starts[0], jnp.where(row > 0, starts[2], starts[1]))
        which = base + (col // SPAN)
        got = [jnp.zeros((8, WIDE), F32) for _ in range(variables)]
        for q in range(table.shape[0] // (8 * variables)):
            hit = sub == which - 8 * q
            for v in range(variables):
                start = (q * variables + v) * 8
                got[v] = jnp.where(hit, found[start : start + 8], got[v])
        for v in range(variables):
            term = got[v] * weight
            acc[v] = term if p == 0 else acc[v] + term
    return [jnp.sum(a, axis=0, keepdims=True) for a in acc]


def gather(k, most, turns, own_ref, tab_ref, row_ref, col_ref, weight_ref, new_ref, variables):
    blocks = own_ref.shape[1] // variables
    fill = -sum(most) % 8
    groups = (sum(most) + fill) // 8
    lists = []
    for v in range(variables):
        rows = [own_ref[r, v * blocks : v * blocks + most[r], :] for r in range(3) if most[r]]
        if fill:
            rows.append(jnp.zeros((fill, SPAN), F32))
        lists.append(jnp.concatenate(rows, axis=0))
    parts = [lists[v][8 * t : 8 * t + 8] for t in range(groups) for v in range(variables)]
    size = 8 * len(parts)
    tab_ref[0:size, :] = jnp.concatenate(parts, axis=0).astype(BF16)

    def body(b, carry):
        interp = pick_wide(
            b, k, tab_ref[0:size, :], most, row_ref, col_ref, weight_ref, variables
        )
        for v in range(variables):
            for t in range(WIDE // SPAN):
                new_ref[pl.ds(v * blocks + b * (WIDE // SPAN) + t, 1), :] = interp[v][
                    :, t * SPAN : (t + 1) * SPAN
                ]
        return carry

    lax.fori_loop(0, turns, body, 0)


def new_grid(new_ref, length, variables):
    blocks = new_ref.shape[0] // variables
    interp = [new_ref[v * blocks : (v + 1) * blocks, :] for v in range(variables)]
    shape = interp[0].shape
    point = lax.broadcasted_iota(jnp.int32, shape, 0) * SPAN + lax.broadcasted_iota(jnp.int32, shape, 1)
    inside = point < length
    out = []
    for v in range(variables):
        value = interp[v] + 0.5 * interp[(v + 1) % variables] * jnp.tanh(interp[(v + 2) % variables])
        out.append(jnp.where(inside, value, 0.0))
    return jnp.concatenate(out, axis=0).astype(BF16)


def analyse_rows(newgrid, cos_block, sin_block, fc, fs, scale):
    blocks = cos_block.shape[0]
    part_real = jnp.dot(newgrid, fc, preferred_element_type=F32)
    part_imag = jnp.dot(newgrid, fs, preferred_element_type=F32)
    out = []
    for v in range(newgrid.shape[0] // blocks):
        pr = part_real[v * blocks : (v + 1) * blocks]
        pi = part_imag[v * blocks : (v + 1) * blocks]
        real = jnp.sum(pr * cos_block + pi * sin_block, axis=0, keepdims=True)
        imag = jnp.sum(pi * cos_block - pr * sin_block, axis=0, keepdims=True)
        out += [real * scale, imag * scale]
    return jnp.concatenate(out, axis=0)


def order_rows(first, orders_ref):
    sub = lax.broadcasted_iota(jnp.int32, (8, 128), 0)
    parts = []
    for t in range(GROUP // 8):
        part = jnp.full((8, 128), orders_ref[first + 8 * t], jnp.int32)
        for i in range(1, 8):
            part = jnp.where(sub == i, orders_ref[first + 8 * t + i], part)
        parts.append(part)
    return jnp.concatenate(parts, axis=0)[:, :1]


def own_slots(both, rows_j, width, inner):
    size = GROUP * rows_j
    row = lax.broadcasted_iota(jnp.int32, (size, width), 0) // rows_j
    col = lax.broadcasted_iota(jnp.int32, (size, width), 1)
    col = col % GROUP if inner else col // rows_j
    return jnp.sum(jnp.where(row == col, both, 0.0).reshape(GROUP, rows_j, width), axis=0)


def forward_group(g, first, fields, rows_j, spec_ref, leg_ref, orders_ref, four_ref):
    degrees = spec_ref.shape[3]
    degree = lax.broadcasted_iota(jnp.int32, (GROUP, degrees), 1)
    keep = jnp.where(degree >= order_rows(first + g * GROUP, orders_ref), 1.0, 0.0).astype(BF16)
    state = jnp.concatenate([spec_ref[g, v] * keep for v in range(fields)], axis=0)
    both = lax.dot_general(
        leg_ref[g], state, (((1,), (1,)), ((), ())), preferred_element_type=F32
    )
    four_ref[g] = own_slots(both, rows_j, fields * GROUP, True)


def gram_group(g, first, rows_j, leg_ref, orders_ref, square_ref, masked_ref):
    degrees = leg_ref.shape[2]
    degree = lax.broadcasted_iota(jnp.int32, (2 * rows_j, degrees), 1)
    sub = lax.broadcasted_iota(jnp.int32, (2 * rows_j, 128), 0)
    parts = []
    for pair in range(GROUP // 2):
        slot = first + g * GROUP + 2 * pair
        order = jnp.where(sub < rows_j, orders_ref[slot], orders_ref[slot + 1])[:, :1]
        keep = jnp.where(degree >= order, 1.0, 0.0).astype(BF16)
        parts.append(leg_ref[g, 2 * pair * rows_j : 2 * (pair + 1) * rows_j, :] * keep)
    masked = jnp.concatenate(parts, axis=0)
    masked_ref[g] = masked
    both = lax.dot_general(
        leg_ref[g], masked, (((1,), (1,)), ((), ())), preferred_element_type=F32
    )
    square_ref[g] = own_slots(both, rows_j, GROUP * rows_j, False)


def gram_of(square_ref, gram_ref, rows_j):
    groups, _, size = square_ref.shape
    row = lax.broadcasted_iota(jnp.int32, (size, size), 0)
    col = lax.broadcasted_iota(jnp.int32, (size, size), 1)
    swap = (row // rows_j == col % GROUP) & (row % rows_j == col // GROUP)
    turned = jnp.dot(
        square_ref[...].reshape(groups * rows_j, size), jnp.where(swap, 1.0, 0.0),
        preferred_element_type=F32, precision="highest",
    )
    for h in range(groups):
        rows = turned[h * rows_j : (h + 1) * rows_j]
        for j in range(rows_j):
            gram_ref[j, :, h * GROUP : (h + 1) * GROUP] = rows[:, j * GROUP : (j + 1) * GROUP]


def steps_kernel(
    steps, count, fields, slots, stride,
    spec_hbm, leg_hbm, row_hbm, col_hbm, weight_hbm, order_hbm, len_hbm, gauss_hbm,
    out_ref, masked_ref,
    orders_ref, order_ref, len_ref, gauss_ref, small_sem,
    spec_ref, leg_ref, row_ref, col_ref, weight_ref,
    four_ref, square_ref, vjs_ref, gram_ref, pack_ref,
    cos_ref, sin_ref, fc_ref, fs_ref, ca_ref, sa_ref,
    coef_ref, mine_ref, mix_ref, part_ref, own_ref, tab_ref, new_ref,
    a_send, a_recv, g_send, g_recv, all_send, all_recv, b_send, b_recv,
    load_sem, point_sem, a_ssem, a_rsem, g_ssem, g_rsem, all_ssem, all_rsem, b_ssem, b_rsem,
):
    rows_j = leg_ref.shape[1] // GROUP
    groups = slots // GROUP
    variables = fields // 2
    total = orders_ref.shape[0]
    blocks = cos_ref.shape[1]
    cut = 3 * slots

    def loads(g):
        slot_rows = pl.ds(pl.multiple_of(g * GROUP, GROUP), GROUP)
        return (
            pltpu.make_async_copy(leg_hbm.at[g], leg_ref.at[g], load_sem.at[0, g]),
            pltpu.make_async_copy(spec_hbm.at[:, slot_rows, :], spec_ref.at[g], load_sem.at[1, g]),
        )

    points = [
        pltpu.make_async_copy(row_hbm, row_ref, point_sem.at[0]),
        pltpu.make_async_copy(col_hbm, col_ref, point_sem.at[1]),
        pltpu.make_async_copy(weight_hbm, weight_ref, point_sem.at[2]),
    ]
    me = lax.axis_index("wave")
    upper = me // (count // 2)
    peers = []
    for i in range(count - 1):
        rising = i + (i - me + count) // count
        falling = count - 1 - i - (i + 1 + me) // count
        peers.append(upper * rising + (1 - upper) * falling)
    barrier = pltpu.get_barrier_semaphore()
    for peer in peers:
        pl.semaphore_signal(barrier, inc=1, device_id={"wave": peer}, device_id_type=MESH)
    small = [
        pltpu.make_async_copy(order_hbm, orders_ref, small_sem.at[0]),
        pltpu.make_async_copy(order_hbm, order_ref, small_sem.at[1]),
        pltpu.make_async_copy(len_hbm, len_ref, small_sem.at[2]),
        pltpu.make_async_copy(gauss_hbm, gauss_ref, small_sem.at[3]),
    ]
    for copy in small:
        copy.start()
    for copy in small:
        copy.wait()
    for g in range(groups):
        for copy in loads(g):
            copy.start()
    for copy in points:
        copy.start()
    vjs_ref[...] = jnp.zeros_like(vjs_ref)
    gram_ref[...] = jnp.zeros_like(gram_ref)
    pack_ref[...] = jnp.zeros_like(pack_ref)
    new_ref[...] = jnp.zeros_like(new_ref)
    coef_ref[...] = jnp.zeros_like(coef_ref)
    mine_ref[...] = jnp.zeros_like(mine_ref)
    orders = orders_ref[...].reshape(1, total)
    lats = [jnp.clip(me + r - 1, 0, count - 1) for r in range(3)]
    lengths = [len_ref[lat] for lat in lats]
    limits = [jnp.minimum(total, (length - 1) // 2) for length in lengths]
    first = me * slots

    for r in range(3):
        tables(
            r, orders, lengths[r], limits[r], cos_ref, sin_ref, fc_ref, fs_ref, ca_ref, sa_ref
        )

    for g in range(groups):
        for copy in loads(g):
            copy.wait()
    for g in range(groups):
        forward_group(g, first, fields, rows_j, spec_ref, leg_ref, order_ref, four_ref)
    for h in range(groups):
        for v in range(fields):
            vjs_ref[v, :, h * GROUP : (h + 1) * GROUP] = four_ref[
                h, :, v * GROUP : (v + 1) * GROUP
            ]

    def pack(source, send):
        for p in range(count):
            for r in range(3):
                pack_ref[p, :, r * slots : (r + 1) * slots] = source[
                    min(max(p + r - 1, 0), count - 1)
                ][:, :slots]
        for p in range(count):
            send(p)

    def send_first(p):
        half = pack_ref.shape[2] // 2
        a_send[p] = jnp.concatenate(
            [pack_ref[p, :, :half], pack_ref[p, :, half:]], axis=0
        ).astype(BF16)

    def send_gram(p):
        g_send[p] = pack_ref[p]

    def exchange(send, recv, ssem, rsem):
        copies = []
        for peer in peers:
            d = lax.rem(peer - me + count, count) - 1
            copy = pltpu.make_async_remote_copy(
                src_ref=send(peer), dst_ref=recv.at[me], send_sem=ssem.at[d],
                recv_sem=rsem.at[d], device_id={"wave": peer}, device_id_type=MESH,
            )
            copy.start()
            copies.append(copy)
        return copies

    pack(jnp.swapaxes(vjs_ref[...], 0, 1), send_first)
    pl.semaphore_wait(barrier, count - 1)
    copies = exchange(lambda peer: a_send.at[peer], a_recv, a_ssem, a_rsem)
    a_recv[me] = a_send[me]

    def gram(g, carry):
        gram_group(g, first, rows_j, leg_ref, order_ref, square_ref, masked_ref)
        return carry

    lax.fori_loop(0, groups, gram, 0, unroll=2)
    gram_of(square_ref, gram_ref, rows_j)
    pack(gram_ref[...], send_gram)
    for copy in copies:
        copy.wait()
    gram_copies = exchange(lambda peer: g_send.at[peer], g_recv, g_ssem, g_rsem)
    g_recv[me] = g_send[me]
    for copy in points:
        copy.wait()
    for i in range(count):
        half = a_recv.shape[2]
        both = a_recv[i].astype(F32)
        both = jnp.concatenate([both[:fields], both[fields:]], axis=1)
        for r in range(3):
            coef_ref[r, :, i * slots : (i + 1) * slots] = both[:, r * slots : (r + 1) * slots]

    shape = (1, total)
    coef_scale = gauss_ref[0] * jnp.sqrt(2.0 / jnp.full(shape, lengths[1].astype(F32)))
    inside = [jnp.where(me > 0, 1.0, 0.0), 1.0, jnp.where(me < count - 1, 1.0, 0.0)]
    scales = [
        inside[r] / jnp.sqrt(jnp.full((1, SPAN), limits[r].astype(F32))) for r in range(3)
    ]
    turns = (half_rows(me, stride) + WIDE // SPAN - 1) // (WIDE // SPAN)
    most = [half_rows(count - 4 + r, stride) for r in range(1, 4)]
    ranges, start = [], 0
    while start < total:
        ranges.append((start, min(start + CHUNK, total)))
        start += CHUNK

    def part_of(r, coeffs, a, b):
        return grid_part(
            coeffs, cos_ref[r, :, a:b], sin_ref[r, :, a:b], fc_ref[r, :, a:b], fs_ref[r, :, a:b]
        )

    for r in range(3):
        own_ref[r] = grid_rows(
            part_of(r, coef_ref[r], 0, total), blocks, lengths[r], scales[r]
        )
    for k in range(steps):
        args = (own_ref, tab_ref, row_ref, col_ref, weight_ref, new_ref, variables)

        @pl.when(me < count - 1)
        def _():
            gather(k, [most[0], most[1], most[2]], turns, *args)

        @pl.when(me == count - 1)
        def _():
            gather(k, [most[1], most[2], 0], turns, *args)

        fresh = new_grid(new_ref, lengths[1], variables)
        if k + 1 < steps:
            pending = []
            for c, (a, b) in enumerate(ranges):
                mine = analyse_rows(
                    fresh, cos_ref[1, :, a:b], sin_ref[1, :, a:b], fc_ref[1, :, a:b],
                    fs_ref[1, :, a:b], coef_scale[:, a:b],
                )
                half = (b - a) // 2
                lanes = slice(a // 2, b // 2)
                all_send[k, :, lanes] = jnp.concatenate(
                    [mine[:, :half], mine[:, half:]], axis=0
                ).astype(BF16)
                pending.append(
                    exchange(
                        lambda peer: all_send.at[k, :, lanes], all_recv.at[k, :, :, lanes],
                        all_ssem.at[k, c], all_rsem.at[k, c],
                    )
                )
                all_recv[k, me, :, lanes] = all_send[k, :, lanes]
            if k == 0:
                for copy in gram_copies:
                    copy.wait()
                for i in range(count):
                    for r in range(3):
                        mix_ref[r, :, i * slots : (i + 1) * slots] = g_recv[
                            i, :, r * slots : (r + 1) * slots
                        ]
            for c, (a, b) in enumerate(ranges):
                for copy in pending[c]:
                    copy.wait()
                sums = [None] * 3
                for j in range(count):
                    both = all_recv[k, j, :, a // 2 : b // 2].astype(F32)
                    both = jnp.concatenate([both[:fields], both[fields:]], axis=1)
                    for r in range(3):
                        term = mix_ref[r, j : j + 1, a:b] * both
                        sums[r] = term if j == 0 else sums[r] + term
                for r in range(3):
                    share = part_of(r, sums[r], a, b)
                    if c + 1 < len(ranges):
                        part_ref[r] = share if c == 0 else part_ref[r] + share
                    else:
                        own_ref[r] = grid_rows(
                            share if c == 0 else part_ref[r] + share,
                            blocks, lengths[r], scales[r],
                        )
        else:
            mine_ref[:, :total] = analyse_rows(
                fresh, cos_ref[1], sin_ref[1], fc_ref[1], fs_ref[1], coef_scale
            )
            for i in range(count):
                b_send[i] = jnp.concatenate(
                    [
                        mine_ref[:, i * slots : i * slots + 128],
                        mine_ref[:, i * slots + 128 : i * slots + 256],
                    ],
                    axis=0,
                ).astype(BF16)
            copies = exchange(lambda peer: b_send.at[peer], b_recv, b_ssem, b_rsem)
            b_recv[me] = b_send[me]
            for copy in copies:
                copy.wait()
    out_ref[...] = b_recv[...]


def inverse_kernel(coef_ref, leg_ref, out_hbm, out_ref, out_sem):
    groups, size, _ = leg_ref.shape
    rows_j = size // GROUP
    fields = coef_ref.shape[1] // 2

    def store(g):
        slot_rows = pl.ds(pl.multiple_of(g * GROUP, GROUP), GROUP)
        return pltpu.make_async_copy(out_ref.at[g], out_hbm.at[:, slot_rows, :], out_sem.at[g])

    last = jnp.swapaxes(coef_ref[...].astype(F32), 0, 1)
    row = lax.broadcasted_iota(jnp.int32, (size, fields * GROUP), 0) // rows_j
    col = lax.broadcasted_iota(jnp.int32, (size, fields * GROUP), 1) % GROUP
    own = row == col
    for g in range(groups):
        half, lane = divmod(g * GROUP, 128)
        coefs = jnp.concatenate(
            [last[half * fields + v, :, lane : lane + GROUP] for v in range(fields)], axis=1
        )
        tiled = jnp.concatenate([coefs] * GROUP, axis=0)
        spread = jnp.where(own, tiled, 0.0).T.astype(BF16)
        out = jnp.dot(spread, leg_ref[g], preferred_element_type=F32).astype(BF16)
        out_ref[g] = out.reshape(out_ref.shape[1:])
        store(g).start()
    for g in range(groups):
        store(g).wait()


def fused(spectrum, legendre, order_of_slot, reduced_length, gauss_weight, row, col, weight, count):
    slots, rows_j, degrees = legendre.shape
    fields = 2 * spectrum.shape[0]
    total = order_of_slot.shape[0]
    steps, stencil, grid_width = row.shape[0], row.shape[2], row.shape[-1]
    blocks = -(-(grid_width // SPAN) // 8) * 8
    stride = total // count
    groups = slots // GROUP
    size = GROUP * rows_j
    lanes = -(-slots // 128) * 128
    packed = -(-3 * slots // 256) * 256
    rows_v = fields // 2 * blocks
    half = total // 2
    points = (steps, stencil, 1, grid_width)
    coefs, masked = pl.pallas_call(
        functools.partial(steps_kernel, steps, count, fields, slots, stride),
        out_shape=[
            pltpu.VMEM((count, 2 * fields, 128), BF16),
            pltpu.VMEM((groups, size, degrees), BF16),
        ],
        in_specs=[HBM_SPEC] * 8,
        out_specs=[VMEM_SPEC] * 2,
        scratch_shapes=[
            pltpu.VMEM((total,), jnp.int32),
            pltpu.SMEM((total,), jnp.int32),
            pltpu.SMEM(reduced_length.shape, jnp.int32),
            pltpu.SMEM(gauss_weight.shape, F32),
            pltpu.SemaphoreType.DMA((4,)),
            pltpu.VMEM((groups, fields, GROUP, degrees), BF16),
            pltpu.VMEM((groups, size, degrees), BF16),
            pltpu.VMEM(points, jnp.int32),
            pltpu.VMEM(points, jnp.int32),
            pltpu.VMEM(points, F32),
            pltpu.VMEM((groups, rows_j, fields * GROUP), F32),
            pltpu.VMEM((groups, rows_j, size), F32),
            pltpu.VMEM((fields, rows_j, lanes), F32),
            pltpu.VMEM((rows_j, rows_j, lanes), F32),
            pltpu.VMEM((count, fields, packed), F32),
            pltpu.VMEM((3, blocks, total), F32),
            pltpu.VMEM((3, blocks, total), F32),
            pltpu.VMEM((3, SPAN, total), BF16),
            pltpu.VMEM((3, SPAN, total), BF16),
            pltpu.VMEM((SPAN // 8 + 8, total), F32),
            pltpu.VMEM((SPAN // 8 + 8, total), F32),
            pltpu.VMEM((3, fields, total), F32),
            pltpu.VMEM((fields, total + 128), F32),
            pltpu.VMEM((3, rows_j, total), F32),
            pltpu.VMEM((3, SPAN, rows_v), F32),
            pltpu.VMEM((3, rows_v, SPAN), F32),
            pltpu.VMEM((3 * rows_v, SPAN), BF16),
            pltpu.VMEM((rows_v, SPAN), F32),
            pltpu.VMEM((count, 2 * fields, packed // 2), BF16),
            pltpu.VMEM((count, 2 * fields, packed // 2), BF16),
            pltpu.VMEM((count, rows_j, packed), F32),
            pltpu.VMEM((count, rows_j, packed), F32),
            pltpu.VMEM((steps, 2 * fields, half), BF16),
            pltpu.VMEM((steps, count, 2 * fields, half), BF16),
            pltpu.VMEM((count, 2 * fields, 128), BF16),
            pltpu.VMEM((count, 2 * fields, 128), BF16),
            pltpu.SemaphoreType.DMA((2, groups)),
            pltpu.SemaphoreType.DMA((3,)),
        ]
        + [pltpu.SemaphoreType.DMA((count - 1,))] * 4
        + [pltpu.SemaphoreType.DMA((steps, -(-total // CHUNK), count - 1))] * 2
        + [pltpu.SemaphoreType.DMA((count - 1,))] * 2,
        compiler_params=pltpu.CompilerParams(
            collective_id=0, has_side_effects=True, vmem_limit_bytes=58 * 2**20
        ),
        name="steps",
    )(
        spectrum.reshape(fields, slots, degrees),
        legendre.reshape(groups, size, degrees),
        row.reshape(points), col.reshape(points), weight.reshape(points),
        order_of_slot, reduced_length, gauss_weight,
    )
    out = pl.pallas_call(
        inverse_kernel,
        out_shape=jax.ShapeDtypeStruct((fields, slots, degrees), BF16),
        in_specs=[VMEM_SPEC, VMEM_SPEC],
        out_specs=pl.BlockSpec(memory_space=pl.ANY),
        scratch_shapes=[
            pltpu.VMEM((groups, fields, GROUP, degrees), BF16),
            pltpu.SemaphoreType.DMA((groups,)),
        ],
        compiler_params=pltpu.CompilerParams(vmem_limit_bytes=24 * 2**20),
        name="inverse",
    )(coefs, masked)
    return out.reshape(spectrum.shape)


def per_device(
    spectrum,
    legendre,
    order_of_slot,
    reduced_length,
    gauss_weight,
    depart_row,
    depart_col,
    depart_weight,
):
    own_index = lax.axis_index("wave")
    count = lax.axis_size("wave")
    slot_count = legendre.shape[0]
    orders_total = order_of_slot.shape[0]
    variables, level_count = spectrum.shape[:2]
    assert level_count == 1
    steps = depart_row.shape[0]
    grid_width = depart_row.shape[-1]
    stencil = depart_row.shape[2]
    fields = variables
    real_blocks = grid_width // BLOCK
    blocks = padded_blocks(grid_width)

    stride = orders_total // count
    longest = half_rows(count - 1, stride)
    fits = (
        slot_count % GROUP == 0 and 128 < slot_count <= 256 and 2 * fields == 8
        and legendre.shape[1] == 8 and count == 8 and stride == slot_count
        and orders_total % 256 == 0 and orders_total * grid_width < 2**24
        and grid_width % SPAN == 0 and grid_width // SPAN <= 24
        and -(-longest // 3) * WIDE <= grid_width
    )
    if fits:
        return fused(
            spectrum, legendre, order_of_slot, reduced_length, gauss_weight,
            depart_row, depart_col, depart_weight, count,
        )

    length = lax.dynamic_index_in_dim(reduced_length, own_index, keepdims=False)
    own_orders = lax.dynamic_slice_in_dim(order_of_slot, own_index * slot_count, slot_count)
    degrees = jnp.arange(legendre.shape[2], dtype=jnp.int32)
    masked = jnp.where(
        degrees[None, None, :] >= own_orders[:, None, None], legendre, jnp.zeros((), BF16)
    )
    order_limit = jnp.minimum(orders_total, (length - 1) // 2)
    cos_rows, sin_rows = phase_rows(length, order_of_slot, blocks)
    active = (order_of_slot < order_limit).astype(F32)[None, :]
    fc, fs = pl.pallas_call(
        build_table,
        out_shape=[jax.ShapeDtypeStruct((BLOCK, orders_total), BF16)] * 2,
        in_specs=[VMEM_SPEC] * 3,
        out_specs=[VMEM_SPEC] * 2,
        scratch_shapes=[pltpu.VMEM((RADIX * RADIX, orders_total), F32)] * 2,
        name="table",
    )(cos_rows, sin_rows, active)
    length1 = length.reshape(1)
    grid_scale = (1.0 / jnp.sqrt(order_limit.astype(F32))).reshape(1)
    coef_scale = (gauss_weight[0] * jnp.sqrt(2.0 / length.astype(F32))).reshape(1)

    synth = pl.pallas_call(
        functools.partial(synth_kernel, blocks),
        out_shape=jax.ShapeDtypeStruct((fields * blocks, BLOCK), BF16),
        in_specs=[VMEM_SPEC] * 5 + [SMEM_SPEC] * 2,
        out_specs=VMEM_SPEC,
        name="synth",
    )
    grid_step = pl.pallas_call(
        functools.partial(grid_kernel, fields, blocks, real_blocks),
        out_shape=jax.ShapeDtypeStruct((2 * fields, orders_total), BF16),
        in_specs=[VMEM_SPEC] * 8 + [SMEM_SPEC] * 2,
        out_specs=VMEM_SPEC,
        scratch_shapes=[pltpu.VMEM((fields * blocks, BLOCK), F32)],
        name="grid_step",
    )
    spectral = spectrum.reshape(2 * fields, slot_count, -1)
    fourier = jnp.einsum("vsn,sjn->jvs", spectral, masked, preferred_element_type=F32)
    gram = jnp.einsum("sjn,skn->sjk", masked, masked, preferred_element_type=F32)
    forward = [(i, i + 1) for i in range(count - 1)]
    backward = [(i + 1, i) for i in range(count - 1)]
    for k in range(steps):
        gathered = lax.all_to_all(fourier.astype(BF16), "wave", split_axis=0, concat_axis=2, tiled=True)
        own = synth(
            gathered.reshape(2 * fields, orders_total), cos_rows, sin_rows, fc, fs, length1, grid_scale
        )
        low = lax.ppermute(own, "wave", forward)
        high = lax.ppermute(own, "wave", backward)
        coeffs = grid_step(
            jnp.concatenate([low, own, high], axis=0),
            depart_row[k].reshape(1, stencil, 1, grid_width),
            depart_col[k].reshape(1, stencil, 1, grid_width),
            depart_weight[k].reshape(1, stencil, 1, grid_width),
            cos_rows, sin_rows, fc, fs, length1, coef_scale,
        )
        returned = lax.all_to_all(
            coeffs.reshape(1, 2 * fields, orders_total), "wave", split_axis=2, concat_axis=0, tiled=True
        )
        if k + 1 < steps:
            fourier = jnp.einsum("jvs,sjk->kvs", returned.astype(F32), gram, precision="highest")
    final = jnp.einsum("jvs,sjn->vsn", returned, masked, preferred_element_type=F32).astype(BF16)
    return final.reshape(spectrum.shape)


def solution(mesh):
    placed = (
        P(None, "lev", None, "wave", None),
        P("wave", None, None),
        P(),
        P(),
        P("wave"),
        P(None, "lev", None, "wave", None),
        P(None, "lev", None, "wave", None),
        P(None, "lev", None, "wave", None),
    )
    return jax.shard_map(
        per_device,
        mesh=mesh,
        in_specs=placed,
        out_specs=P(None, "lev", None, "wave", None),
        check_vma=False,
    )
```

```python
import functools
import math

import jax
import jax.numpy as jnp
from jax import lax
from jax.experimental import pallas as pl
from jax.experimental.pallas import tpu as pltpu
from jax.sharding import PartitionSpec as P

BLOCK = 512
RADIX = 8
FULL_TURN = 2.0 * math.pi
F32 = jnp.float32
BF16 = jnp.bfloat16

VMEM_SPEC = pl.BlockSpec(memory_space=pltpu.VMEM)
SMEM_SPEC = pl.BlockSpec(memory_space=pltpu.SMEM)


def padded_blocks(grid_width):
    return -(-(grid_width // BLOCK) // 16) * 16


def phase_rows(length, orders, blocks):
    digits = jnp.arange(RADIX, dtype=jnp.int32)
    steps = [digits, digits * RADIX, digits * RADIX * RADIX]
    steps.append(jnp.arange(blocks, dtype=jnp.int32) * BLOCK)
    steps = jnp.concatenate(steps)
    phases = steps[:, None] * orders[None, :] % length
    angles = phases.astype(F32) * (jnp.float32(FULL_TURN) / length.astype(F32))
    return jnp.cos(angles), jnp.sin(angles)


def build_table(cos_ref, sin_ref, active_ref, fc_ref, fs_ref, ca_ref, sa_ref):
    active = active_ref[...]
    cos_low = cos_ref[0:RADIX, :] * active
    sin_low = sin_ref[0:RADIX, :] * active
    cos_mid = cos_ref[RADIX : 2 * RADIX, :]
    sin_mid = sin_ref[RADIX : 2 * RADIX, :]
    for a in range(RADIX):
        c = cos_ref[2 * RADIX + a : 2 * RADIX + a + 1, :]
        s = sin_ref[2 * RADIX + a : 2 * RADIX + a + 1, :]
        ca_ref[a * RADIX : (a + 1) * RADIX, :] = c * cos_mid - s * sin_mid
        sa_ref[a * RADIX : (a + 1) * RADIX, :] = s * cos_mid + c * sin_mid

    def body(i, carry):
        cos_parts, sin_parts = [], []
        for k in range(2):
            c = ca_ref[pl.ds(2 * i + k, 1), :]
            s = sa_ref[pl.ds(2 * i + k, 1), :]
            cos_parts.append(c * cos_low - s * sin_low)
            sin_parts.append(-(s * cos_low + c * sin_low))
        rows = pl.ds(pl.multiple_of(i * 2 * RADIX, 2 * RADIX), 2 * RADIX)
        fc_ref[rows, :] = jnp.concatenate(cos_parts, axis=0).astype(BF16)
        fs_ref[rows, :] = jnp.concatenate(sin_parts, axis=0).astype(BF16)
        return carry

    lax.fori_loop(0, RADIX * RADIX // 2, body, 0)


def synthesize(coeffs, cos_block, sin_block, fc_ref, fs_ref, length, scale):
    fields = coeffs.shape[0] // 2
    blocks = cos_block.shape[0]
    reals, imags = [], []
    for v in range(fields):
        real = coeffs[2 * v : 2 * v + 1]
        imag = coeffs[2 * v + 1 : 2 * v + 2]
        reals.append((real * cos_block - imag * sin_block).astype(BF16))
        imags.append((real * sin_block + imag * cos_block).astype(BF16))
    dims = (((1,), (1,)), ((), ()))
    out = lax.dot_general(
        jnp.concatenate(reals, axis=0), fc_ref[...], dims, preferred_element_type=F32
    ) + lax.dot_general(
        jnp.concatenate(imags, axis=0), fs_ref[...], dims, preferred_element_type=F32
    )
    row = lax.broadcasted_iota(jnp.int32, out.shape, 0) % blocks
    point = row * BLOCK + lax.broadcasted_iota(jnp.int32, out.shape, 1)
    return jnp.where(point < length, out * scale, 0.0)


def synth_kernel(blocks, coef_ref, cos_ref, sin_ref, fc_ref, fs_ref, len_ref, scale_ref, out_ref):
    out_ref[...] = synthesize(
        coef_ref[...].astype(F32),
        cos_ref[3 * RADIX : 3 * RADIX + blocks, :],
        sin_ref[3 * RADIX : 3 * RADIX + blocks, :],
        fc_ref,
        fs_ref,
        len_ref[0],
        scale_ref[0],
    ).astype(BF16)


def gather_block(b, k, table, row_ref, col_ref, weight_ref, fields, blocks):
    stencil = col_ref.shape[1]
    half = 256
    lanes = pl.ds(pl.multiple_of(b * BLOCK, BLOCK), BLOCK)
    iota_half = lax.broadcasted_iota(jnp.int32, (half, BLOCK), 0).astype(F32).astype(BF16)
    iota_rows = lax.broadcasted_iota(jnp.int32, (3 * blocks, BLOCK), 0)
    one = jnp.ones((), BF16)
    zero = jnp.zeros((), BF16)
    acc = [jnp.zeros((blocks, BLOCK), F32) for _ in range(fields)]
    for p in range(stencil):
        col = col_ref[k, p, :, lanes]
        row = row_ref[k, p, :, lanes]
        weight = weight_ref[k, p, :, lanes]
        point = col % BLOCK
        halves = []
        for h in range(BLOCK // half):
            local = point - h * half
            key = jnp.where((local >= 0) & (local < half), local, -1).astype(F32).astype(BF16)
            halves.append(jnp.where(iota_half == key, one, zero))
        onehot = jnp.concatenate(halves, axis=0)
        found = jnp.dot(table, onehot, preferred_element_type=F32)
        which = (row + 1) * blocks + col // BLOCK
        chosen = jnp.where(iota_rows == which, weight, 0.0)
        for r in range(3):
            sel = chosen[r * blocks : (r + 1) * blocks]
            for v in range(fields):
                start = (r * fields + v) * blocks
                acc[v] = acc[v] + found[start : start + blocks] * sel
    return [jnp.sum(a, axis=0, keepdims=True) for a in acc]


def advance(table, k, row_ref, col_ref, weight_ref, new_ref, length, fields, blocks, real_blocks):
    new_ref[...] = jnp.zeros_like(new_ref)

    def body(b, carry):
        interp = gather_block(b, k, table, row_ref, col_ref, weight_ref, fields, blocks)
        point = b * BLOCK + lax.broadcasted_iota(jnp.int32, (1, BLOCK), 1)
        for v in range(fields):
            value = interp[v] + 0.5 * interp[(v + 1) % fields] * jnp.tanh(interp[(v + 2) % fields])
            new_ref[pl.ds(v * blocks + b, 1), :] = jnp.where(point < length, value, 0.0)
        return carry

    lax.fori_loop(0, real_blocks, body, 0)


def analyse(new_ref, cos_block, sin_block, fc_ref, fs_ref, scale):
    blocks = cos_block.shape[0]
    fields = new_ref.shape[0] // blocks
    newgrid = new_ref[...].astype(BF16)
    part_real = jnp.dot(newgrid, fc_ref[...], preferred_element_type=F32)
    part_imag = jnp.dot(newgrid, fs_ref[...], preferred_element_type=F32)
    out = []
    for v in range(fields):
        pr = part_real[v * blocks : (v + 1) * blocks]
        pi = part_imag[v * blocks : (v + 1) * blocks]
        real = jnp.sum(pr * cos_block + pi * sin_block, axis=0, keepdims=True)
        imag = jnp.sum(pi * cos_block - pr * sin_block, axis=0, keepdims=True)
        out += [real * scale, imag * scale]
    return out


def grid_kernel(
    fields, blocks, real_blocks,
    table_ref, row_ref, col_ref, weight_ref, cos_ref, sin_ref, fc_ref, fs_ref, len_ref, scale_ref,
    out_ref, new_ref,
):
    advance(
        table_ref[...], 0, row_ref, col_ref, weight_ref, new_ref, len_ref[0],
        fields, blocks, real_blocks,
    )
    rows = analyse(
        new_ref,
        cos_ref[3 * RADIX : 3 * RADIX + blocks, :],
        sin_ref[3 * RADIX : 3 * RADIX + blocks, :],
        fc_ref,
        fs_ref,
        scale_ref[0],
    )
    out_ref[...] = jnp.concatenate(rows, axis=0).astype(BF16)


SPAN = 256
WIDE = 7 * SPAN
GROUP = 16
MESH = pl.DeviceIdType.MESH
HBM_SPEC = pl.BlockSpec(memory_space=pltpu.HBM)


def half_rows(lat, stride):
    return (20 + 4 * ((lat + 1) * stride - 1) + SPAN - 1) // SPAN


def unit_turns(steps, orders, length):
    product = steps * orders
    inverse = 1.0 / length
    rest = product - jnp.floor(product * inverse + 0.5) * length
    x = rest * (inverse * (0.25 * FULL_TURN))
    y = x * x
    s = x * (1.0 + y * (-1.0 / 6 + y * (1.0 / 120 + y * (-1.0 / 5040 + y * (1.0 / 362880)))))
    c = 1.0 + y * (-0.5 + y * (1.0 / 24 + y * (-1.0 / 720 + y * (1.0 / 40320))))
    s, c = 2.0 * s * c, 1.0 - 2.0 * s * s
    return 1.0 - 2.0 * s * s, 2.0 * s * c


def tables(p, orders, length, limit, cos_ref, sin_ref, fc_ref, fs_ref, ca_ref, sa_ref):
    shape = (8, orders.shape[1])
    digit = lax.broadcasted_iota(jnp.int32, shape, 0)
    digit_f = digit.astype(F32)
    length_f = jnp.full(shape, length.astype(F32))
    orders_f = jnp.broadcast_to(orders.astype(F32), shape)
    active = jnp.where(orders_f < limit.astype(F32), 1.0, 0.0)
    cos_b, sin_b = unit_turns(digit_f * SPAN, orders_f, length_f)
    mixed = jnp.where(digit < 4, digit_f * 64, (digit_f - 4.0) * (8 * SPAN))
    cos_h, sin_h = unit_turns(mixed, orders_f, length_f)
    cos_ref[p, 0:8, :] = cos_b
    sin_ref[p, 0:8, :] = sin_b
    for t in range(1, cos_ref.shape[1] // 8):
        c, s = cos_h[4 + t : 5 + t], sin_h[4 + t : 5 + t]
        cos_ref[p, 8 * t : 8 * t + 8, :] = c * cos_b - s * sin_b
        sin_ref[p, 8 * t : 8 * t + 8, :] = s * cos_b + c * sin_b
    cos_m, sin_m = unit_turns(digit_f * 8, orders_f, length_f)
    for t in range(SPAN // 64):
        c, s = cos_h[t : t + 1], sin_h[t : t + 1]
        ca_ref[8 * t : 8 * t + 8, :] = c * cos_m - s * sin_m
        sa_ref[8 * t : 8 * t + 8, :] = s * cos_m + c * sin_m
    cos_low, sin_low = unit_turns(digit_f, orders_f, length_f)
    ca_ref[SPAN // 8 : SPAN // 8 + 8, :] = cos_low * active
    sa_ref[SPAN // 8 : SPAN // 8 + 8, :] = sin_low * active

    def body(i, carry):
        cos_l = ca_ref[SPAN // 8 : SPAN // 8 + 8, :]
        sin_l = sa_ref[SPAN // 8 : SPAN // 8 + 8, :]
        cos_parts, sin_parts = [], []
        for k in range(2):
            c = ca_ref[pl.ds(2 * i + k, 1), :]
            s = sa_ref[pl.ds(2 * i + k, 1), :]
            cos_parts.append(c * cos_l - s * sin_l)
            sin_parts.append(-(s * cos_l + c * sin_l))
        rows = pl.ds(pl.multiple_of(i * 16, 16), 16)
        fc_ref[p, rows, :] = jnp.concatenate(cos_parts, axis=0).astype(BF16)
        fs_ref[p, rows, :] = jnp.concatenate(sin_parts, axis=0).astype(BF16)
        return carry

    lax.fori_loop(0, SPAN // 16, body, 0)


def grid_part(coeffs, cos_block, sin_block, fc, fs):
    variables = coeffs.shape[0] // 2
    reals, imags = [], []
    for v in range(variables):
        real = coeffs[2 * v : 2 * v + 1]
        imag = coeffs[2 * v + 1 : 2 * v + 2]
        reals.append((real * cos_block - imag * sin_block).astype(BF16))
        imags.append((real * sin_block + imag * cos_block).astype(BF16))
    dims = (((1,), (1,)), ((), ()))
    return lax.dot_general(
        fc, jnp.concatenate(reals, axis=0), dims, preferred_element_type=F32
    ) + lax.dot_general(
        fs, jnp.concatenate(imags, axis=0), dims, preferred_element_type=F32
    )


def grid_rows(part, blocks, length, scale):
    out = part.T
    row = lax.broadcasted_iota(jnp.int32, out.shape, 0) % blocks
    point = row * SPAN + lax.broadcasted_iota(jnp.int32, out.shape, 1)
    return jnp.where(point < length, out * scale, 0.0)


def pick_wide(b, k, table, most, row_ref, col_ref, weight_ref, variables):
    stencil = col_ref.shape[1]
    lanes = pl.ds(pl.multiple_of(b * WIDE, WIDE), WIDE)
    iota = lax.broadcasted_iota(jnp.int32, (SPAN, WIDE), 0).astype(F32).astype(BF16)
    sub = lax.broadcasted_iota(jnp.int32, (8, WIDE), 0)
    one = jnp.ones((), BF16)
    zero = jnp.zeros((), BF16)
    starts = [sum(most[:r]) if most[r] else 1024 for r in range(3)]
    acc = [None] * variables
    for p in range(stencil):
        col = col_ref[k, p, :, lanes]
        row = row_ref[k, p, :, lanes]
        weight = weight_ref[k, p, :, lanes]
        key = (col & (SPAN - 1)).astype(F32).astype(BF16)
        onehot = jnp.where(iota == key, one, zero)
        found = jnp.dot(table, onehot, preferred_element_type=F32)
        base = jnp.where(row < 0, starts[0], jnp.where(row > 0, starts[2], starts[1]))
        which = base + (col // SPAN)
        got = [jnp.zeros((8, WIDE), F32) for _ in range(variables)]
        for q in range(table.shape[0] // (8 * variables)):
            hit = sub == which - 8 * q
            for v in range(variables):
                start = (q * variables + v) * 8
                got[v] = jnp.where(hit, found[start : start + 8], got[v])
        for v in range(variables):
            term = got[v] * weight
            acc[v] = term if p == 0 else acc[v] + term
    return [jnp.sum(a, axis=0, keepdims=True) for a in acc]


def gather(k, most, turns, own_ref, tab_ref, row_ref, col_ref, weight_ref, new_ref, variables):
    blocks = own_ref.shape[1] // variables
    fill = -sum(most) % 8
    groups = (sum(most) + fill) // 8
    lists = []
    for v in range(variables):
        rows = [own_ref[r, v * blocks : v * blocks + most[r], :] for r in range(3) if most[r]]
        if fill:
            rows.append(jnp.zeros((fill, SPAN), F32))
        lists.append(jnp.concatenate(rows, axis=0))
    parts = [lists[v][8 * t : 8 * t + 8] for t in range(groups) for v in range(variables)]
    size = 8 * len(parts)
    tab_ref[0:size, :] = jnp.concatenate(parts, axis=0).astype(BF16)

    def body(b, carry):
        interp = pick_wide(
            b, k, tab_ref[0:size, :], most, row_ref, col_ref, weight_ref, variables
        )
        for v in range(variables):
            for t in range(WIDE // SPAN):
                new_ref[pl.ds(v * blocks + b * (WIDE // SPAN) + t, 1), :] = interp[v][
                    :, t * SPAN : (t + 1) * SPAN
                ]
        return carry

    lax.fori_loop(0, turns, body, 0)


def new_grid(new_ref, length, variables):
    blocks = new_ref.shape[0] // variables
    interp = [new_ref[v * blocks : (v + 1) * blocks, :] for v in range(variables)]
    shape = interp[0].shape
    point = lax.broadcasted_iota(jnp.int32, shape, 0) * SPAN + lax.broadcasted_iota(jnp.int32, shape, 1)
    inside = point < length
    out = []
    for v in range(variables):
        value = interp[v] + 0.5 * interp[(v + 1) % variables] * jnp.tanh(interp[(v + 2) % variables])
        out.append(jnp.where(inside, value, 0.0))
    return jnp.concatenate(out, axis=0).astype(BF16)


def analyse_rows(newgrid, cos_block, sin_block, fc, fs, scale):
    blocks = cos_block.shape[0]
    part_real = jnp.dot(newgrid, fc, preferred_element_type=F32)
    part_imag = jnp.dot(newgrid, fs, preferred_element_type=F32)
    out = []
    for v in range(newgrid.shape[0] // blocks):
        pr = part_real[v * blocks : (v + 1) * blocks]
        pi = part_imag[v * blocks : (v + 1) * blocks]
        real = jnp.sum(pr * cos_block + pi * sin_block, axis=0, keepdims=True)
        imag = jnp.sum(pi * cos_block - pr * sin_block, axis=0, keepdims=True)
        out += [real * scale, imag * scale]
    return jnp.concatenate(out, axis=0)


def order_rows(first, orders_ref):
    sub = lax.broadcasted_iota(jnp.int32, (8, 128), 0)
    parts = []
    for t in range(GROUP // 8):
        part = jnp.full((8, 128), orders_ref[first + 8 * t], jnp.int32)
        for i in range(1, 8):
            part = jnp.where(sub == i, orders_ref[first + 8 * t + i], part)
        parts.append(part)
    return jnp.concatenate(parts, axis=0)[:, :1]


def own_slots(both, rows_j, width, inner):
    size = GROUP * rows_j
    row = lax.broadcasted_iota(jnp.int32, (size, width), 0) // rows_j
    col = lax.broadcasted_iota(jnp.int32, (size, width), 1)
    col = col % GROUP if inner else col // rows_j
    return jnp.sum(jnp.where(row == col, both, 0.0).reshape(GROUP, rows_j, width), axis=0)


def forward_group(g, first, fields, rows_j, spec_ref, leg_ref, orders_ref, four_ref):
    degrees = spec_ref.shape[3]
    degree = lax.broadcasted_iota(jnp.int32, (GROUP, degrees), 1)
    keep = jnp.where(degree >= order_rows(first + g * GROUP, orders_ref), 1.0, 0.0).astype(BF16)
    state = jnp.concatenate([spec_ref[g, v] * keep for v in range(fields)], axis=0)
    both = lax.dot_general(
        leg_ref[g], state, (((1,), (1,)), ((), ())), preferred_element_type=F32
    )
    four_ref[g] = own_slots(both, rows_j, fields * GROUP, True)


def gram_group(g, first, rows_j, leg_ref, orders_ref, square_ref, masked_ref):
    degrees = leg_ref.shape[2]
    degree = lax.broadcasted_iota(jnp.int32, (2 * rows_j, degrees), 1)
    sub = lax.broadcasted_iota(jnp.int32, (2 * rows_j, 128), 0)
    parts = []
    for pair in range(GROUP // 2):
        slot = first + g * GROUP + 2 * pair
        order = jnp.where(sub < rows_j, orders_ref[slot], orders_ref[slot + 1])[:, :1]
        keep = jnp.where(degree >= order, 1.0, 0.0).astype(BF16)
        parts.append(leg_ref[g, 2 * pair * rows_j : 2 * (pair + 1) * rows_j, :] * keep)
    masked = jnp.concatenate(parts, axis=0)
    masked_ref[g] = masked
    both = lax.dot_general(
        leg_ref[g], masked, (((1,), (1,)), ((), ())), preferred_element_type=F32
    )
    square_ref[g] = own_slots(both, rows_j, GROUP * rows_j, False)


def gram_of(square_ref, gram_ref, rows_j):
    groups, _, size = square_ref.shape
    row = lax.broadcasted_iota(jnp.int32, (size, size), 0)
    col = lax.broadcasted_iota(jnp.int32, (size, size), 1)
    swap = (row // rows_j == col % GROUP) & (row % rows_j == col // GROUP)
    turned = jnp.dot(
        square_ref[...].reshape(groups * rows_j, size), jnp.where(swap, 1.0, 0.0),
        preferred_element_type=F32, precision="highest",
    )
    for h in range(groups):
        rows = turned[h * rows_j : (h + 1) * rows_j]
        for j in range(rows_j):
            gram_ref[j, :, h * GROUP : (h + 1) * GROUP] = rows[:, j * GROUP : (j + 1) * GROUP]


def steps_kernel(
    steps, count, fields, slots, stride,
    spec_hbm, leg_hbm, row_hbm, col_hbm, weight_hbm, order_hbm, len_hbm, gauss_hbm,
    out_ref, masked_ref,
    orders_ref, order_ref, len_ref, gauss_ref, small_sem,
    spec_ref, leg_ref, row_ref, col_ref, weight_ref,
    four_ref, square_ref, vjs_ref, gram_ref, pack_ref,
    cos_ref, sin_ref, fc_ref, fs_ref, ca_ref, sa_ref,
    coef_ref, mine_ref, mix_ref, own_ref, tab_ref, new_ref,
    a_send, a_recv, g_send, g_recv, all_send, all_recv, b_send, b_recv,
    load_sem, point_sem, a_ssem, a_rsem, g_ssem, g_rsem, all_ssem, all_rsem, b_ssem, b_rsem,
):
    rows_j = leg_ref.shape[1] // GROUP
    groups = slots // GROUP
    variables = fields // 2
    total = orders_ref.shape[0]
    blocks = cos_ref.shape[1]
    cut = 3 * slots

    def loads(g):
        slot_rows = pl.ds(pl.multiple_of(g * GROUP, GROUP), GROUP)
        return (
            pltpu.make_async_copy(leg_hbm.at[g], leg_ref.at[g], load_sem.at[0, g]),
            pltpu.make_async_copy(spec_hbm.at[:, slot_rows, :], spec_ref.at[g], load_sem.at[1, g]),
        )

    points = [
        pltpu.make_async_copy(row_hbm, row_ref, point_sem.at[0]),
        pltpu.make_async_copy(col_hbm, col_ref, point_sem.at[1]),
        pltpu.make_async_copy(weight_hbm, weight_ref, point_sem.at[2]),
    ]
    me = lax.axis_index("wave")
    upper = me // (count // 2)
    peers = []
    for i in range(count - 1):
        rising = i + (i - me + count) // count
        falling = count - 1 - i - (i + 1 + me) // count
        peers.append(upper * rising + (1 - upper) * falling)
    core, place, chips = lax.rem(me, 2), me // 2, count // 2
    mate = me + 1 - 2 * core
    others = []
    for i in range(chips - 1):
        rising = i + (i - place + chips) // chips
        falling = chips - 1 - i - (i + 1 + place) // chips
        others.append(upper * rising + (1 - upper) * falling)
    barrier = pltpu.get_barrier_semaphore()
    for peer in peers:
        pl.semaphore_signal(barrier, inc=1, device_id={"wave": peer}, device_id_type=MESH)
    small = [
        pltpu.make_async_copy(order_hbm, orders_ref, small_sem.at[0]),
        pltpu.make_async_copy(order_hbm, order_ref, small_sem.at[1]),
        pltpu.make_async_copy(len_hbm, len_ref, small_sem.at[2]),
        pltpu.make_async_copy(gauss_hbm, gauss_ref, small_sem.at[3]),
    ]
    for copy in small:
        copy.start()
    for copy in small:
        copy.wait()
    for g in range(groups):
        for copy in loads(g):
            copy.start()
    for copy in points:
        copy.start()
    vjs_ref[...] = jnp.zeros_like(vjs_ref)
    gram_ref[...] = jnp.zeros_like(gram_ref)
    pack_ref[...] = jnp.zeros_like(pack_ref)
    new_ref[...] = jnp.zeros_like(new_ref)
    coef_ref[...] = jnp.zeros_like(coef_ref)
    mine_ref[...] = jnp.zeros_like(mine_ref)
    orders = orders_ref[...].reshape(1, total)
    lats = [jnp.clip(me + r - 1, 0, count - 1) for r in range(3)]
    lengths = [len_ref[lat] for lat in lats]
    limits = [jnp.minimum(total, (length - 1) // 2) for length in lengths]
    first = me * slots

    for r in range(3):
        tables(
            r, orders, lengths[r], limits[r], cos_ref, sin_ref, fc_ref, fs_ref, ca_ref, sa_ref
        )

    for g in range(groups):
        for copy in loads(g):
            copy.wait()
    for g in range(groups):
        forward_group(g, first, fields, rows_j, spec_ref, leg_ref, order_ref, four_ref)
    for h in range(groups):
        for v in range(fields):
            vjs_ref[v, :, h * GROUP : (h + 1) * GROUP] = four_ref[
                h, :, v * GROUP : (v + 1) * GROUP
            ]

    def pack(source, send):
        for p in range(count):
            for r in range(3):
                pack_ref[p, :, r * slots : (r + 1) * slots] = source[
                    min(max(p + r - 1, 0), count - 1)
                ][:, :slots]
        for p in range(count):
            send(p)

    def send_first(p):
        half = pack_ref.shape[2] // 2
        a_send[p] = jnp.concatenate(
            [pack_ref[p, :, :half], pack_ref[p, :, half:]], axis=0
        ).astype(BF16)

    def send_gram(p):
        g_send[p] = pack_ref[p]

    def exchange(send, recv, ssem, rsem):
        copies = []
        for peer in peers:
            d = lax.rem(peer - me + count, count) - 1
            copy = pltpu.make_async_remote_copy(
                src_ref=send(peer), dst_ref=recv.at[me], send_sem=ssem.at[d],
                recv_sem=rsem.at[d], device_id={"wave": peer}, device_id_type=MESH,
            )
            copy.start()
            copies.append(copy)
        return copies

    pack(jnp.swapaxes(vjs_ref[...], 0, 1), send_first)
    pl.semaphore_wait(barrier, count - 1)
    copies = exchange(lambda peer: a_send.at[peer], a_recv, a_ssem, a_rsem)
    a_recv[me] = a_send[me]

    def gram(g, carry):
        gram_group(g, first, rows_j, leg_ref, order_ref, square_ref, masked_ref)
        return carry

    lax.fori_loop(0, groups, gram, 0, unroll=2)
    gram_of(square_ref, gram_ref, rows_j)
    pack(gram_ref[...], send_gram)
    for copy in copies:
        copy.wait()
    gram_copies = exchange(lambda peer: g_send.at[peer], g_recv, g_ssem, g_rsem)
    g_recv[me] = g_send[me]
    for copy in points:
        copy.wait()
    for i in range(count):
        half = a_recv.shape[2]
        both = a_recv[i].astype(F32)
        both = jnp.concatenate([both[:fields], both[fields:]], axis=1)
        for r in range(3):
            coef_ref[r, :, i * slots : (i + 1) * slots] = both[:, r * slots : (r + 1) * slots]

    shape = (1, total)
    coef_scale = gauss_ref[0] * jnp.sqrt(2.0 / jnp.full(shape, lengths[1].astype(F32)))
    inside = [jnp.where(me > 0, 1.0, 0.0), 1.0, jnp.where(me < count - 1, 1.0, 0.0)]
    scales = [
        inside[r] / jnp.sqrt(jnp.full((1, SPAN), limits[r].astype(F32))) for r in range(3)
    ]
    turns = (half_rows(me, stride) + WIDE // SPAN - 1) // (WIDE // SPAN)
    most = [half_rows(count - 4 + r, stride) for r in range(1, 4)]
    def part_of(r, coeffs):
        return grid_part(coeffs, cos_ref[r], sin_ref[r], fc_ref[r], fs_ref[r])

    for r in range(3):
        own_ref[r] = grid_rows(
            part_of(r, coef_ref[r]), blocks, lengths[r], scales[r]
        )
    for k in range(steps):
        args = (own_ref, tab_ref, row_ref, col_ref, weight_ref, new_ref, variables)

        @pl.when(me < count - 1)
        def _():
            gather(k, [most[0], most[1], most[2]], turns, *args)

        @pl.when(me == count - 1)
        def _():
            gather(k, [most[1], most[2], 0], turns, *args)

        fresh = new_grid(new_ref, lengths[1], variables)
        if k + 1 < steps:
            mine = analyse_rows(
                fresh, cos_ref[1], sin_ref[1], fc_ref[1], fs_ref[1], coef_scale
            )
            half = total // 2
            all_send[k] = jnp.concatenate([mine[:, :half], mine[:, half:]], axis=0).astype(BF16)

            def hand(source, lat, slot, peer):
                return pltpu.make_async_remote_copy(
                    src_ref=source, dst_ref=all_recv.at[k, lat], send_sem=all_ssem.at[k, slot],
                    recv_sem=all_rsem.at[k, lat], device_id={"wave": peer}, device_id_type=MESH,
                )

            sent = [
                hand(all_send.at[k], me, i, chip * 2 + core) for i, chip in enumerate(others)
            ]
            sent.append(hand(all_send.at[k], me, len(others), mate))
            for copy in sent:
                copy.start()
            if k == 0:
                for copy in gram_copies:
                    copy.wait()
                for i in range(count):
                    for r in range(3):
                        mix_ref[r, :, i * slots : (i + 1) * slots] = g_recv[
                            i, :, r * slots : (r + 1) * slots
                        ]

            def mixed(lat, both, sums):
                both = both.astype(F32)
                both = jnp.concatenate([both[:fields], both[fields:]], axis=1)
                terms = [mix_ref[r, pl.ds(lat, 1), :] * both for r in range(3)]
                return terms if sums is None else [x + y for x, y in zip(sums, terms)]

            near = [chip * 2 + core for chip in reversed(others)]
            for i, lat in enumerate(near):
                hand(all_send.at[k], lat, 0, mate).wait_recv()
                copy = hand(all_recv.at[k, lat], lat, len(others) + 1 + i, mate)
                copy.start()
                sent.append(copy)
            sums = mixed(me, all_send[k], None)
            for lat in near:
                sums = mixed(lat, all_recv[k, lat], sums)
            for lat in [mate] + [chip * 2 + 1 - core for chip in reversed(others)]:
                hand(all_send.at[k], lat, 0, mate).wait_recv()
                sums = mixed(lat, all_recv[k, lat], sums)
            for r in range(3):
                own_ref[r] = grid_rows(
                    part_of(r, sums[r]), blocks, lengths[r], scales[r]
                )
            for copy in sent:
                copy.wait_send()
        else:
            mine_ref[:, :total] = analyse_rows(
                fresh, cos_ref[1], sin_ref[1], fc_ref[1], fs_ref[1], coef_scale
            )
            for i in range(count):
                b_send[i] = jnp.concatenate(
                    [
                        mine_ref[:, i * slots : i * slots + 128],
                        mine_ref[:, i * slots + 128 : i * slots + 256],
                    ],
                    axis=0,
                ).astype(BF16)
            copies = exchange(lambda peer: b_send.at[peer], b_recv, b_ssem, b_rsem)
            b_recv[me] = b_send[me]
            for copy in copies:
                copy.wait()
    out_ref[...] = b_recv[...]


def inverse_kernel(coef_ref, leg_ref, out_hbm, out_ref, out_sem):
    groups, size, _ = leg_ref.shape
    rows_j = size // GROUP
    fields = coef_ref.shape[1] // 2

    def store(g):
        slot_rows = pl.ds(pl.multiple_of(g * GROUP, GROUP), GROUP)
        return pltpu.make_async_copy(out_ref.at[g], out_hbm.at[:, slot_rows, :], out_sem.at[g])

    last = jnp.swapaxes(coef_ref[...].astype(F32), 0, 1)
    row = lax.broadcasted_iota(jnp.int32, (size, fields * GROUP), 0) // rows_j
    col = lax.broadcasted_iota(jnp.int32, (size, fields * GROUP), 1) % GROUP
    own = row == col
    for g in range(groups):
        half, lane = divmod(g * GROUP, 128)
        coefs = jnp.concatenate(
            [last[half * fields + v, :, lane : lane + GROUP] for v in range(fields)], axis=1
        )
        tiled = jnp.concatenate([coefs] * GROUP, axis=0)
        spread = jnp.where(own, tiled, 0.0).T.astype(BF16)
        out = jnp.dot(spread, leg_ref[g], preferred_element_type=F32).astype(BF16)
        out_ref[g] = out.reshape(out_ref.shape[1:])
        store(g).start()
    for g in range(groups):
        store(g).wait()


def fused(spectrum, legendre, order_of_slot, reduced_length, gauss_weight, row, col, weight, count):
    slots, rows_j, degrees = legendre.shape
    fields = 2 * spectrum.shape[0]
    total = order_of_slot.shape[0]
    steps, stencil, grid_width = row.shape[0], row.shape[2], row.shape[-1]
    blocks = -(-(grid_width // SPAN) // 8) * 8
    stride = total // count
    groups = slots // GROUP
    size = GROUP * rows_j
    lanes = -(-slots // 128) * 128
    packed = -(-3 * slots // 256) * 256
    rows_v = fields // 2 * blocks
    half = total // 2
    points = (steps, stencil, 1, grid_width)
    coefs, masked = pl.pallas_call(
        functools.partial(steps_kernel, steps, count, fields, slots, stride),
        out_shape=[
            pltpu.VMEM((count, 2 * fields, 128), BF16),
            pltpu.VMEM((groups, size, degrees), BF16),
        ],
        in_specs=[HBM_SPEC] * 8,
        out_specs=[VMEM_SPEC] * 2,
        scratch_shapes=[
            pltpu.VMEM((total,), jnp.int32),
            pltpu.SMEM((total,), jnp.int32),
            pltpu.SMEM(reduced_length.shape, jnp.int32),
            pltpu.SMEM(gauss_weight.shape, F32),
            pltpu.SemaphoreType.DMA((4,)),
            pltpu.VMEM((groups, fields, GROUP, degrees), BF16),
            pltpu.VMEM((groups, size, degrees), BF16),
            pltpu.VMEM(points, jnp.int32),
            pltpu.VMEM(points, jnp.int32),
            pltpu.VMEM(points, F32),
            pltpu.VMEM((groups, rows_j, fields * GROUP), F32),
            pltpu.VMEM((groups, rows_j, size), F32),
            pltpu.VMEM((fields, rows_j, lanes), F32),
            pltpu.VMEM((rows_j, rows_j, lanes), F32),
            pltpu.VMEM((count, fields, packed), F32),
            pltpu.VMEM((3, blocks, total), F32),
            pltpu.VMEM((3, blocks, total), F32),
            pltpu.VMEM((3, SPAN, total), BF16),
            pltpu.VMEM((3, SPAN, total), BF16),
            pltpu.VMEM((SPAN // 8 + 8, total), F32),
            pltpu.VMEM((SPAN // 8 + 8, total), F32),
            pltpu.VMEM((3, fields, total), F32),
            pltpu.VMEM((fields, total + 128), F32),
            pltpu.VMEM((3, rows_j, total), F32),
            pltpu.VMEM((3, rows_v, SPAN), F32),
            pltpu.VMEM((3 * rows_v, SPAN), BF16),
            pltpu.VMEM((rows_v, SPAN), F32),
            pltpu.VMEM((count, 2 * fields, packed // 2), BF16),
            pltpu.VMEM((count, 2 * fields, packed // 2), BF16),
            pltpu.VMEM((count, rows_j, packed), F32),
            pltpu.VMEM((count, rows_j, packed), F32),
            pltpu.VMEM((steps, 2 * fields, half), BF16),
            pltpu.VMEM((steps, count, 2 * fields, half), BF16),
            pltpu.VMEM((count, 2 * fields, 128), BF16),
            pltpu.VMEM((count, 2 * fields, 128), BF16),
            pltpu.SemaphoreType.DMA((2, groups)),
            pltpu.SemaphoreType.DMA((3,)),
        ]
        + [pltpu.SemaphoreType.DMA((count - 1,))] * 4
        + [pltpu.SemaphoreType.DMA((steps, count))] * 2
        + [pltpu.SemaphoreType.DMA((count - 1,))] * 2,
        compiler_params=pltpu.CompilerParams(
            collective_id=0, has_side_effects=True, vmem_limit_bytes=58 * 2**20
        ),
        name="steps",
    )(
        spectrum.reshape(fields, slots, degrees),
        legendre.reshape(groups, size, degrees),
        row.reshape(points), col.reshape(points), weight.reshape(points),
        order_of_slot, reduced_length, gauss_weight,
    )
    out = pl.pallas_call(
        inverse_kernel,
        out_shape=jax.ShapeDtypeStruct((fields, slots, degrees), BF16),
        in_specs=[VMEM_SPEC, VMEM_SPEC],
        out_specs=pl.BlockSpec(memory_space=pl.ANY),
        scratch_shapes=[
            pltpu.VMEM((groups, fields, GROUP, degrees), BF16),
            pltpu.SemaphoreType.DMA((groups,)),
        ],
        compiler_params=pltpu.CompilerParams(vmem_limit_bytes=24 * 2**20),
        name="inverse",
    )(coefs, masked)
    return out.reshape(spectrum.shape)


def per_device(
    spectrum,
    legendre,
    order_of_slot,
    reduced_length,
    gauss_weight,
    depart_row,
    depart_col,
    depart_weight,
):
    own_index = lax.axis_index("wave")
    count = lax.axis_size("wave")
    slot_count = legendre.shape[0]
    orders_total = order_of_slot.shape[0]
    variables, level_count = spectrum.shape[:2]
    assert level_count == 1
    steps = depart_row.shape[0]
    grid_width = depart_row.shape[-1]
    stencil = depart_row.shape[2]
    fields = variables
    real_blocks = grid_width // BLOCK
    blocks = padded_blocks(grid_width)

    stride = orders_total // count
    longest = half_rows(count - 1, stride)
    fits = (
        slot_count % GROUP == 0 and 128 < slot_count <= 256 and 2 * fields == 8
        and legendre.shape[1] == 8 and count == 8 and stride == slot_count
        and orders_total % 256 == 0 and orders_total * grid_width < 2**24
        and grid_width % SPAN == 0 and grid_width // SPAN <= 24
        and -(-longest // (WIDE // SPAN)) * WIDE <= grid_width
    )
    if fits:
        return fused(
            spectrum, legendre, order_of_slot, reduced_length, gauss_weight,
            depart_row, depart_col, depart_weight, count,
        )

    length = lax.dynamic_index_in_dim(reduced_length, own_index, keepdims=False)
    own_orders = lax.dynamic_slice_in_dim(order_of_slot, own_index * slot_count, slot_count)
    degrees = jnp.arange(legendre.shape[2], dtype=jnp.int32)
    masked = jnp.where(
        degrees[None, None, :] >= own_orders[:, None, None], legendre, jnp.zeros((), BF16)
    )
    order_limit = jnp.minimum(orders_total, (length - 1) // 2)
    cos_rows, sin_rows = phase_rows(length, order_of_slot, blocks)
    active = (order_of_slot < order_limit).astype(F32)[None, :]
    fc, fs = pl.pallas_call(
        build_table,
        out_shape=[jax.ShapeDtypeStruct((BLOCK, orders_total), BF16)] * 2,
        in_specs=[VMEM_SPEC] * 3,
        out_specs=[VMEM_SPEC] * 2,
        scratch_shapes=[pltpu.VMEM((RADIX * RADIX, orders_total), F32)] * 2,
        name="table",
    )(cos_rows, sin_rows, active)
    length1 = length.reshape(1)
    grid_scale = (1.0 / jnp.sqrt(order_limit.astype(F32))).reshape(1)
    coef_scale = (gauss_weight[0] * jnp.sqrt(2.0 / length.astype(F32))).reshape(1)

    synth = pl.pallas_call(
        functools.partial(synth_kernel, blocks),
        out_shape=jax.ShapeDtypeStruct((fields * blocks, BLOCK), BF16),
        in_specs=[VMEM_SPEC] * 5 + [SMEM_SPEC] * 2,
        out_specs=VMEM_SPEC,
        name="synth",
    )
    grid_step = pl.pallas_call(
        functools.partial(grid_kernel, fields, blocks, real_blocks),
        out_shape=jax.ShapeDtypeStruct((2 * fields, orders_total), BF16),
        in_specs=[VMEM_SPEC] * 8 + [SMEM_SPEC] * 2,
        out_specs=VMEM_SPEC,
        scratch_shapes=[pltpu.VMEM((fields * blocks, BLOCK), F32)],
        name="grid_step",
    )
    spectral = spectrum.reshape(2 * fields, slot_count, -1)
    fourier = jnp.einsum("vsn,sjn->jvs", spectral, masked, preferred_element_type=F32)
    gram = jnp.einsum("sjn,skn->sjk", masked, masked, preferred_element_type=F32)
    forward = [(i, i + 1) for i in range(count - 1)]
    backward = [(i + 1, i) for i in range(count - 1)]
    for k in range(steps):
        gathered = lax.all_to_all(fourier.astype(BF16), "wave", split_axis=0, concat_axis=2, tiled=True)
        own = synth(
            gathered.reshape(2 * fields, orders_total), cos_rows, sin_rows, fc, fs, length1, grid_scale
        )
        low = lax.ppermute(own, "wave", forward)
        high = lax.ppermute(own, "wave", backward)
        coeffs = grid_step(
            jnp.concatenate([low, own, high], axis=0),
            depart_row[k].reshape(1, stencil, 1, grid_width),
            depart_col[k].reshape(1, stencil, 1, grid_width),
            depart_weight[k].reshape(1, stencil, 1, grid_width),
            cos_rows, sin_rows, fc, fs, length1, coef_scale,
        )
        returned = lax.all_to_all(
            coeffs.reshape(1, 2 * fields, orders_total), "wave", split_axis=2, concat_axis=0, tiled=True
        )
        if k + 1 < steps:
            fourier = jnp.einsum("jvs,sjk->kvs", returned.astype(F32), gram, precision="highest")
    final = jnp.einsum("jvs,sjn->vsn", returned, masked, preferred_element_type=F32).astype(BF16)
    return final.reshape(spectrum.shape)


def solution(mesh):
    placed = (
        P(None, "lev", None, "wave", None),
        P("wave", None, None),
        P(),
        P(),
        P("wave"),
        P(None, "lev", None, "wave", None),
        P(None, "lev", None, "wave", None),
        P(None, "lev", None, "wave", None),
    )
    return jax.shard_map(
        per_device,
        mesh=mesh,
        in_specs=placed,
        out_specs=P(None, "lev", None, "wave", None),
        check_vma=False,
    )
```

```python
import functools
import math

import jax
import jax.numpy as jnp
from jax import lax
from jax.experimental import pallas as pl
from jax.experimental.pallas import tpu as pltpu
from jax.sharding import PartitionSpec as P

BLOCK = 512
RADIX = 8
FULL_TURN = 2.0 * math.pi
F32 = jnp.float32
BF16 = jnp.bfloat16

VMEM_SPEC = pl.BlockSpec(memory_space=pltpu.VMEM)
SMEM_SPEC = pl.BlockSpec(memory_space=pltpu.SMEM)


def padded_blocks(grid_width):
    return -(-(grid_width // BLOCK) // 16) * 16


def phase_rows(length, orders, blocks):
    digits = jnp.arange(RADIX, dtype=jnp.int32)
    steps = [digits, digits * RADIX, digits * RADIX * RADIX]
    steps.append(jnp.arange(blocks, dtype=jnp.int32) * BLOCK)
    steps = jnp.concatenate(steps)
    phases = steps[:, None] * orders[None, :] % length
    angles = phases.astype(F32) * (jnp.float32(FULL_TURN) / length.astype(F32))
    return jnp.cos(angles), jnp.sin(angles)


def build_table(cos_ref, sin_ref, active_ref, fc_ref, fs_ref, ca_ref, sa_ref):
    active = active_ref[...]
    cos_low = cos_ref[0:RADIX, :] * active
    sin_low = sin_ref[0:RADIX, :] * active
    cos_mid = cos_ref[RADIX : 2 * RADIX, :]
    sin_mid = sin_ref[RADIX : 2 * RADIX, :]
    for a in range(RADIX):
        c = cos_ref[2 * RADIX + a : 2 * RADIX + a + 1, :]
        s = sin_ref[2 * RADIX + a : 2 * RADIX + a + 1, :]
        ca_ref[a * RADIX : (a + 1) * RADIX, :] = c * cos_mid - s * sin_mid
        sa_ref[a * RADIX : (a + 1) * RADIX, :] = s * cos_mid + c * sin_mid

    def body(i, carry):
        cos_parts, sin_parts = [], []
        for k in range(2):
            c = ca_ref[pl.ds(2 * i + k, 1), :]
            s = sa_ref[pl.ds(2 * i + k, 1), :]
            cos_parts.append(c * cos_low - s * sin_low)
            sin_parts.append(-(s * cos_low + c * sin_low))
        rows = pl.ds(pl.multiple_of(i * 2 * RADIX, 2 * RADIX), 2 * RADIX)
        fc_ref[rows, :] = jnp.concatenate(cos_parts, axis=0).astype(BF16)
        fs_ref[rows, :] = jnp.concatenate(sin_parts, axis=0).astype(BF16)
        return carry

    lax.fori_loop(0, RADIX * RADIX // 2, body, 0)


def synthesize(coeffs, cos_block, sin_block, fc_ref, fs_ref, length, scale):
    fields = coeffs.shape[0] // 2
    blocks = cos_block.shape[0]
    reals, imags = [], []
    for v in range(fields):
        real = coeffs[2 * v : 2 * v + 1]
        imag = coeffs[2 * v + 1 : 2 * v + 2]
        reals.append((real * cos_block - imag * sin_block).astype(BF16))
        imags.append((real * sin_block + imag * cos_block).astype(BF16))
    dims = (((1,), (1,)), ((), ()))
    out = lax.dot_general(
        jnp.concatenate(reals, axis=0), fc_ref[...], dims, preferred_element_type=F32
    ) + lax.dot_general(
        jnp.concatenate(imags, axis=0), fs_ref[...], dims, preferred_element_type=F32
    )
    row = lax.broadcasted_iota(jnp.int32, out.shape, 0) % blocks
    point = row * BLOCK + lax.broadcasted_iota(jnp.int32, out.shape, 1)
    return jnp.where(point < length, out * scale, 0.0)


def synth_kernel(blocks, coef_ref, cos_ref, sin_ref, fc_ref, fs_ref, len_ref, scale_ref, out_ref):
    out_ref[...] = synthesize(
        coef_ref[...].astype(F32),
        cos_ref[3 * RADIX : 3 * RADIX + blocks, :],
        sin_ref[3 * RADIX : 3 * RADIX + blocks, :],
        fc_ref,
        fs_ref,
        len_ref[0],
        scale_ref[0],
    ).astype(BF16)


def gather_block(b, k, table, row_ref, col_ref, weight_ref, fields, blocks):
    stencil = col_ref.shape[1]
    half = 256
    lanes = pl.ds(pl.multiple_of(b * BLOCK, BLOCK), BLOCK)
    iota_half = lax.broadcasted_iota(jnp.int32, (half, BLOCK), 0).astype(F32).astype(BF16)
    iota_rows = lax.broadcasted_iota(jnp.int32, (3 * blocks, BLOCK), 0)
    one = jnp.ones((), BF16)
    zero = jnp.zeros((), BF16)
    acc = [jnp.zeros((blocks, BLOCK), F32) for _ in range(fields)]
    for p in range(stencil):
        col = col_ref[k, p, :, lanes]
        row = row_ref[k, p, :, lanes]
        weight = weight_ref[k, p, :, lanes]
        point = col % BLOCK
        halves = []
        for h in range(BLOCK // half):
            local = point - h * half
            key = jnp.where((local >= 0) & (local < half), local, -1).astype(F32).astype(BF16)
            halves.append(jnp.where(iota_half == key, one, zero))
        onehot = jnp.concatenate(halves, axis=0)
        found = jnp.dot(table, onehot, preferred_element_type=F32)
        which = (row + 1) * blocks + col // BLOCK
        chosen = jnp.where(iota_rows == which, weight, 0.0)
        for r in range(3):
            sel = chosen[r * blocks : (r + 1) * blocks]
            for v in range(fields):
                start = (r * fields + v) * blocks
                acc[v] = acc[v] + found[start : start + blocks] * sel
    return [jnp.sum(a, axis=0, keepdims=True) for a in acc]


def advance(table, k, row_ref, col_ref, weight_ref, new_ref, length, fields, blocks, real_blocks):
    new_ref[...] = jnp.zeros_like(new_ref)

    def body(b, carry):
        interp = gather_block(b, k, table, row_ref, col_ref, weight_ref, fields, blocks)
        point = b * BLOCK + lax.broadcasted_iota(jnp.int32, (1, BLOCK), 1)
        for v in range(fields):
            value = interp[v] + 0.5 * interp[(v + 1) % fields] * jnp.tanh(interp[(v + 2) % fields])
            new_ref[pl.ds(v * blocks + b, 1), :] = jnp.where(point < length, value, 0.0)
        return carry

    lax.fori_loop(0, real_blocks, body, 0)


def analyse(new_ref, cos_block, sin_block, fc_ref, fs_ref, scale):
    blocks = cos_block.shape[0]
    fields = new_ref.shape[0] // blocks
    newgrid = new_ref[...].astype(BF16)
    part_real = jnp.dot(newgrid, fc_ref[...], preferred_element_type=F32)
    part_imag = jnp.dot(newgrid, fs_ref[...], preferred_element_type=F32)
    out = []
    for v in range(fields):
        pr = part_real[v * blocks : (v + 1) * blocks]
        pi = part_imag[v * blocks : (v + 1) * blocks]
        real = jnp.sum(pr * cos_block + pi * sin_block, axis=0, keepdims=True)
        imag = jnp.sum(pi * cos_block - pr * sin_block, axis=0, keepdims=True)
        out += [real * scale, imag * scale]
    return out


def grid_kernel(
    fields, blocks, real_blocks,
    table_ref, row_ref, col_ref, weight_ref, cos_ref, sin_ref, fc_ref, fs_ref, len_ref, scale_ref,
    out_ref, new_ref,
):
    advance(
        table_ref[...], 0, row_ref, col_ref, weight_ref, new_ref, len_ref[0],
        fields, blocks, real_blocks,
    )
    rows = analyse(
        new_ref,
        cos_ref[3 * RADIX : 3 * RADIX + blocks, :],
        sin_ref[3 * RADIX : 3 * RADIX + blocks, :],
        fc_ref,
        fs_ref,
        scale_ref[0],
    )
    out_ref[...] = jnp.concatenate(rows, axis=0).astype(BF16)


SPAN = 256
WIDE = 6 * SPAN
GROUP = 16
MESH = pl.DeviceIdType.MESH
HBM_SPEC = pl.BlockSpec(memory_space=pltpu.HBM)


def half_rows(lat, stride):
    return (20 + 4 * ((lat + 1) * stride - 1) + SPAN - 1) // SPAN


def unit_turns(steps, orders, length):
    product = steps * orders
    inverse = 1.0 / length
    rest = product - jnp.floor(product * inverse + 0.5) * length
    x = rest * (inverse * (0.25 * FULL_TURN))
    y = x * x
    s = x * (1.0 + y * (-1.0 / 6 + y * (1.0 / 120 + y * (-1.0 / 5040 + y * (1.0 / 362880)))))
    c = 1.0 + y * (-0.5 + y * (1.0 / 24 + y * (-1.0 / 720 + y * (1.0 / 40320))))
    s, c = 2.0 * s * c, 1.0 - 2.0 * s * s
    return 1.0 - 2.0 * s * s, 2.0 * s * c


def tables(p, orders, length, limit, cos_ref, sin_ref, fc_ref, fs_ref, ca_ref, sa_ref):
    shape = (8, orders.shape[1])
    digit = lax.broadcasted_iota(jnp.int32, shape, 0)
    digit_f = digit.astype(F32)
    length_f = jnp.full(shape, length.astype(F32))
    orders_f = jnp.broadcast_to(orders.astype(F32), shape)
    active = jnp.where(orders_f < limit.astype(F32), 1.0, 0.0)
    cos_b, sin_b = unit_turns(digit_f * SPAN, orders_f, length_f)
    mixed = jnp.where(digit < 4, digit_f * 64, (digit_f - 4.0) * (8 * SPAN))
    cos_h, sin_h = unit_turns(mixed, orders_f, length_f)
    cos_ref[p, 0:8, :] = cos_b
    sin_ref[p, 0:8, :] = sin_b
    for t in range(1, cos_ref.shape[1] // 8):
        c, s = cos_h[4 + t : 5 + t], sin_h[4 + t : 5 + t]
        cos_ref[p, 8 * t : 8 * t + 8, :] = c * cos_b - s * sin_b
        sin_ref[p, 8 * t : 8 * t + 8, :] = s * cos_b + c * sin_b
    cos_m, sin_m = unit_turns(digit_f * 8, orders_f, length_f)
    for t in range(SPAN // 64):
        c, s = cos_h[t : t + 1], sin_h[t : t + 1]
        ca_ref[8 * t : 8 * t + 8, :] = c * cos_m - s * sin_m
        sa_ref[8 * t : 8 * t + 8, :] = s * cos_m + c * sin_m
    cos_low, sin_low = unit_turns(digit_f, orders_f, length_f)
    ca_ref[SPAN // 8 : SPAN // 8 + 8, :] = cos_low * active
    sa_ref[SPAN // 8 : SPAN // 8 + 8, :] = sin_low * active

    def body(i, carry):
        cos_l = ca_ref[SPAN // 8 : SPAN // 8 + 8, :]
        sin_l = sa_ref[SPAN // 8 : SPAN // 8 + 8, :]
        cos_parts, sin_parts = [], []
        for k in range(2):
            c = ca_ref[pl.ds(2 * i + k, 1), :]
            s = sa_ref[pl.ds(2 * i + k, 1), :]
            cos_parts.append(c * cos_l - s * sin_l)
            sin_parts.append(-(s * cos_l + c * sin_l))
        rows = pl.ds(pl.multiple_of(i * 16, 16), 16)
        fc_ref[p, rows, :] = jnp.concatenate(cos_parts, axis=0).astype(BF16)
        fs_ref[p, rows, :] = jnp.concatenate(sin_parts, axis=0).astype(BF16)
        return carry

    lax.fori_loop(0, SPAN // 16, body, 0)


def grid_part(coeffs, cos_block, sin_block, fc, fs):
    variables = coeffs.shape[0] // 2
    reals, imags = [], []
    for v in range(variables):
        real = coeffs[2 * v : 2 * v + 1]
        imag = coeffs[2 * v + 1 : 2 * v + 2]
        reals.append((real * cos_block - imag * sin_block).astype(BF16))
        imags.append((real * sin_block + imag * cos_block).astype(BF16))
    dims = (((1,), (1,)), ((), ()))
    return lax.dot_general(
        fc, jnp.concatenate(reals, axis=0), dims, preferred_element_type=F32
    ) + lax.dot_general(
        fs, jnp.concatenate(imags, axis=0), dims, preferred_element_type=F32
    )


def grid_rows(part, blocks, length, scale):
    out = part.T
    row = lax.broadcasted_iota(jnp.int32, out.shape, 0) % blocks
    point = row * SPAN + lax.broadcasted_iota(jnp.int32, out.shape, 1)
    return jnp.where(point < length, out * scale, 0.0)


def pick_wide(b, k, table, most, row_ref, col_ref, weight_ref, variables):
    stencil = col_ref.shape[1]
    lanes = pl.ds(pl.multiple_of(b * WIDE, WIDE), WIDE)
    iota = lax.broadcasted_iota(jnp.int32, (SPAN, WIDE), 0).astype(F32).astype(BF16)
    sub = lax.broadcasted_iota(jnp.int32, (8, WIDE), 0)
    one = jnp.ones((), BF16)
    zero = jnp.zeros((), BF16)
    starts = [sum(most[:r]) if most[r] else 1024 for r in range(3)]
    acc = [None] * variables
    for p in range(stencil):
        col = col_ref[k, p, :, lanes]
        row = row_ref[k, p, :, lanes]
        weight = weight_ref[k, p, :, lanes]
        key = (col & (SPAN - 1)).astype(F32).astype(BF16)
        onehot = jnp.where(iota == key, one, zero)
        found = jnp.dot(table, onehot, preferred_element_type=F32)
        base = jnp.where(row < 0, starts[0], jnp.where(row > 0, starts[2], starts[1]))
        which = base + (col // SPAN)
        got = [jnp.zeros((8, WIDE), F32) for _ in range(variables)]
        for q in range(table.shape[0] // (8 * variables)):
            hit = sub == which - 8 * q
            for v in range(variables):
                start = (q * variables + v) * 8
                got[v] = jnp.where(hit, found[start : start + 8], got[v])
        for v in range(variables):
            term = got[v] * weight
            acc[v] = term if p == 0 else acc[v] + term
    return [jnp.sum(a, axis=0, keepdims=True) for a in acc]


def gather(k, most, turns, own_ref, tab_ref, row_ref, col_ref, weight_ref, new_ref, variables):
    blocks = own_ref.shape[1] // variables
    fill = -sum(most) % 8
    groups = (sum(most) + fill) // 8
    lists = []
    for v in range(variables):
        rows = [own_ref[r, v * blocks : v * blocks + most[r], :] for r in range(3) if most[r]]
        if fill:
            rows.append(jnp.zeros((fill, SPAN), F32))
        lists.append(jnp.concatenate(rows, axis=0))
    parts = [lists[v][8 * t : 8 * t + 8] for t in range(groups) for v in range(variables)]
    size = 8 * len(parts)
    tab_ref[0:size, :] = jnp.concatenate(parts, axis=0).astype(BF16)

    def body(b, carry):
        interp = pick_wide(
            b, k, tab_ref[0:size, :], most, row_ref, col_ref, weight_ref, variables
        )
        for v in range(variables):
            for t in range(WIDE // SPAN):
                new_ref[pl.ds(v * blocks + b * (WIDE // SPAN) + t, 1), :] = interp[v][
                    :, t * SPAN : (t + 1) * SPAN
                ]
        return carry

    lax.fori_loop(0, turns, body, 0)


def new_grid(new_ref, length, variables):
    blocks = new_ref.shape[0] // variables
    interp = [new_ref[v * blocks : (v + 1) * blocks, :] for v in range(variables)]
    shape = interp[0].shape
    point = lax.broadcasted_iota(jnp.int32, shape, 0) * SPAN + lax.broadcasted_iota(jnp.int32, shape, 1)
    inside = point < length
    out = []
    for v in range(variables):
        value = interp[v] + 0.5 * interp[(v + 1) % variables] * jnp.tanh(interp[(v + 2) % variables])
        out.append(jnp.where(inside, value, 0.0))
    return jnp.concatenate(out, axis=0).astype(BF16)


def analyse_rows(newgrid, cos_block, sin_block, fc, fs, scale):
    blocks = cos_block.shape[0]
    part_real = jnp.dot(newgrid, fc, preferred_element_type=F32)
    part_imag = jnp.dot(newgrid, fs, preferred_element_type=F32)
    out = []
    for v in range(newgrid.shape[0] // blocks):
        pr = part_real[v * blocks : (v + 1) * blocks]
        pi = part_imag[v * blocks : (v + 1) * blocks]
        real = jnp.sum(pr * cos_block + pi * sin_block, axis=0, keepdims=True)
        imag = jnp.sum(pi * cos_block - pr * sin_block, axis=0, keepdims=True)
        out += [real * scale, imag * scale]
    return jnp.concatenate(out, axis=0)


def order_rows(first, orders_ref):
    sub = lax.broadcasted_iota(jnp.int32, (8, 128), 0)
    parts = []
    for t in range(GROUP // 8):
        part = jnp.full((8, 128), orders_ref[first + 8 * t], jnp.int32)
        for i in range(1, 8):
            part = jnp.where(sub == i, orders_ref[first + 8 * t + i], part)
        parts.append(part)
    return jnp.concatenate(parts, axis=0)[:, :1]


def own_slots(both, rows_j, width, inner):
    size = GROUP * rows_j
    row = lax.broadcasted_iota(jnp.int32, (size, width), 0) // rows_j
    col = lax.broadcasted_iota(jnp.int32, (size, width), 1)
    col = col % GROUP if inner else col // rows_j
    return jnp.sum(jnp.where(row == col, both, 0.0).reshape(GROUP, rows_j, width), axis=0)


def forward_group(g, first, fields, rows_j, spec_ref, leg_ref, orders_ref, four_ref):
    degrees = spec_ref.shape[3]
    degree = lax.broadcasted_iota(jnp.int32, (GROUP, degrees), 1)
    keep = jnp.where(degree >= order_rows(first + g * GROUP, orders_ref), 1.0, 0.0).astype(BF16)
    state = jnp.concatenate([spec_ref[g, v] * keep for v in range(fields)], axis=0)
    both = lax.dot_general(
        leg_ref[g], state, (((1,), (1,)), ((), ())), preferred_element_type=F32
    )
    four_ref[g] = own_slots(both, rows_j, fields * GROUP, True)


def gram_group(g, first, rows_j, leg_ref, orders_ref, square_ref, masked_ref):
    degrees = leg_ref.shape[2]
    degree = lax.broadcasted_iota(jnp.int32, (2 * rows_j, degrees), 1)
    sub = lax.broadcasted_iota(jnp.int32, (2 * rows_j, 128), 0)
    parts = []
    for pair in range(GROUP // 2):
        slot = first + g * GROUP + 2 * pair
        order = jnp.where(sub < rows_j, orders_ref[slot], orders_ref[slot + 1])[:, :1]
        keep = jnp.where(degree >= order, 1.0, 0.0).astype(BF16)
        parts.append(leg_ref[g, 2 * pair * rows_j : 2 * (pair + 1) * rows_j, :] * keep)
    masked = jnp.concatenate(parts, axis=0)
    masked_ref[g] = masked
    both = lax.dot_general(
        leg_ref[g], masked, (((1,), (1,)), ((), ())), preferred_element_type=F32
    )
    square_ref[g] = own_slots(both, rows_j, GROUP * rows_j, False)


def gram_of(square_ref, gram_ref, rows_j):
    groups, _, size = square_ref.shape
    row = lax.broadcasted_iota(jnp.int32, (size, size), 0)
    col = lax.broadcasted_iota(jnp.int32, (size, size), 1)
    swap = (row // rows_j == col % GROUP) & (row % rows_j == col // GROUP)
    turned = jnp.dot(
        square_ref[...].reshape(groups * rows_j, size), jnp.where(swap, 1.0, 0.0),
        preferred_element_type=F32, precision="highest",
    )
    for h in range(groups):
        rows = turned[h * rows_j : (h + 1) * rows_j]
        for j in range(rows_j):
            gram_ref[j, :, h * GROUP : (h + 1) * GROUP] = rows[:, j * GROUP : (j + 1) * GROUP]


def steps_kernel(
    steps, count, fields, slots, stride,
    spec_hbm, leg_hbm, row_hbm, col_hbm, weight_hbm, order_hbm, len_hbm, gauss_hbm,
    out_ref, masked_ref,
    orders_ref, order_ref, len_ref, gauss_ref, small_sem,
    spec_ref, leg_ref, row_ref, col_ref, weight_ref,
    four_ref, square_ref, vjs_ref, gram_ref, pack_ref,
    cos_ref, sin_ref, fc_ref, fs_ref, ca_ref, sa_ref,
    coef_ref, mine_ref, mix_ref, own_ref, tab_ref, new_ref,
    a_send, a_recv, g_send, g_recv, all_send, all_recv, b_send, b_recv,
    load_sem, point_sem, a_ssem, a_rsem, g_ssem, g_rsem, all_ssem, all_rsem, b_ssem, b_rsem,
):
    rows_j = leg_ref.shape[1] // GROUP
    groups = slots // GROUP
    variables = fields // 2
    total = orders_ref.shape[0]
    blocks = cos_ref.shape[1]
    cut = 3 * slots

    def loads(g):
        slot_rows = pl.ds(pl.multiple_of(g * GROUP, GROUP), GROUP)
        return (
            pltpu.make_async_copy(leg_hbm.at[g], leg_ref.at[g], load_sem.at[0, g]),
            pltpu.make_async_copy(spec_hbm.at[:, slot_rows, :], spec_ref.at[g], load_sem.at[1, g]),
        )

    width = row_hbm.shape[3]
    points = [
        pltpu.make_async_copy(row_hbm, row_ref.at[..., :width], point_sem.at[0]),
        pltpu.make_async_copy(col_hbm, col_ref.at[..., :width], point_sem.at[1]),
        pltpu.make_async_copy(weight_hbm, weight_ref.at[..., :width], point_sem.at[2]),
    ]
    me = lax.axis_index("wave")
    upper = me // (count // 2)
    peers = []
    for i in range(count - 1):
        rising = i + (i - me + count) // count
        falling = count - 1 - i - (i + 1 + me) // count
        peers.append(upper * rising + (1 - upper) * falling)
    core, place, chips = lax.rem(me, 2), me // 2, count // 2
    mate = me + 1 - 2 * core
    others = []
    for i in range(chips - 1):
        rising = i + (i - place + chips) // chips
        falling = chips - 1 - i - (i + 1 + place) // chips
        others.append(upper * rising + (1 - upper) * falling)
    small = [
        pltpu.make_async_copy(order_hbm, orders_ref, small_sem.at[0]),
        pltpu.make_async_copy(order_hbm, order_ref, small_sem.at[1]),
        pltpu.make_async_copy(len_hbm, len_ref, small_sem.at[2]),
        pltpu.make_async_copy(gauss_hbm, gauss_ref, small_sem.at[3]),
    ]
    for copy in small:
        copy.start()
    barrier = pltpu.get_barrier_semaphore()
    for peer in peers:
        pl.semaphore_signal(barrier, inc=1, device_id={"wave": peer}, device_id_type=MESH)
    for copy in small:
        copy.wait()
    for g in range(groups):
        for copy in loads(g):
            copy.start()
    for copy in points:
        copy.start()
    if row_ref.shape[3] > width:
        for ref in (row_ref, col_ref, weight_ref):
            ref[..., width:] = jnp.zeros(ref.shape[:3] + (ref.shape[3] - width,), ref.dtype)
    vjs_ref[...] = jnp.zeros_like(vjs_ref)
    gram_ref[...] = jnp.zeros_like(gram_ref)
    pack_ref[...] = jnp.zeros_like(pack_ref)
    new_ref[...] = jnp.zeros_like(new_ref)
    coef_ref[...] = jnp.zeros_like(coef_ref)
    mine_ref[...] = jnp.zeros_like(mine_ref)
    orders = orders_ref[...].reshape(1, total)
    lats = [jnp.clip(me + r - 1, 0, count - 1) for r in range(3)]
    lengths = [len_ref[lat] for lat in lats]
    limits = [jnp.minimum(total, (length - 1) // 2) for length in lengths]
    first = me * slots

    for r in range(3):
        tables(
            r, orders, lengths[r], limits[r], cos_ref, sin_ref, fc_ref, fs_ref, ca_ref, sa_ref
        )

    for g in range(groups):
        for copy in loads(g):
            copy.wait()
    for g in range(groups):
        forward_group(g, first, fields, rows_j, spec_ref, leg_ref, order_ref, four_ref)
    for h in range(groups):
        for v in range(fields):
            vjs_ref[v, :, h * GROUP : (h + 1) * GROUP] = four_ref[
                h, :, v * GROUP : (v + 1) * GROUP
            ]

    def pack(source, send):
        for p in range(count):
            for r in range(3):
                pack_ref[p, :, r * slots : (r + 1) * slots] = source[
                    min(max(p + r - 1, 0), count - 1)
                ][:, :slots]
        for p in range(count):
            send(p)

    def send_first(p):
        half = pack_ref.shape[2] // 2
        a_send[p] = jnp.concatenate(
            [pack_ref[p, :, :half], pack_ref[p, :, half:]], axis=0
        ).astype(BF16)

    def send_gram(p):
        g_send[p] = pack_ref[p]

    def exchange(send, recv, ssem, rsem):
        copies = []
        for peer in peers:
            d = lax.rem(peer - me + count, count) - 1
            copy = pltpu.make_async_remote_copy(
                src_ref=send(peer), dst_ref=recv.at[me], send_sem=ssem.at[d],
                recv_sem=rsem.at[d], device_id={"wave": peer}, device_id_type=MESH,
            )
            copy.start()
            copies.append(copy)
        return copies

    pack(jnp.swapaxes(vjs_ref[...], 0, 1), send_first)
    pl.semaphore_wait(barrier, count - 1)
    copies = exchange(lambda peer: a_send.at[peer], a_recv, a_ssem, a_rsem)
    a_recv[me] = a_send[me]

    def gram(g, carry):
        gram_group(g, first, rows_j, leg_ref, order_ref, square_ref, masked_ref)
        return carry

    lax.fori_loop(0, groups, gram, 0, unroll=2)
    gram_of(square_ref, gram_ref, rows_j)
    pack(gram_ref[...], send_gram)
    for copy in copies:
        copy.wait()
    gram_copies = exchange(lambda peer: g_send.at[peer], g_recv, g_ssem, g_rsem)
    g_recv[me] = g_send[me]
    for copy in points:
        copy.wait()
    for i in range(count):
        half = a_recv.shape[2]
        both = a_recv[i].astype(F32)
        both = jnp.concatenate([both[:fields], both[fields:]], axis=1)
        for r in range(3):
            coef_ref[r, :, i * slots : (i + 1) * slots] = both[:, r * slots : (r + 1) * slots]

    shape = (1, total)
    coef_scale = gauss_ref[0] * jnp.sqrt(2.0 / jnp.full(shape, lengths[1].astype(F32)))
    inside = [jnp.where(me > 0, 1.0, 0.0), 1.0, jnp.where(me < count - 1, 1.0, 0.0)]
    scales = [
        inside[r] / jnp.sqrt(jnp.full((1, SPAN), limits[r].astype(F32))) for r in range(3)
    ]
    turns = (half_rows(me, stride) + WIDE // SPAN - 1) // (WIDE // SPAN)
    most = [half_rows(count - 4 + r, stride) for r in range(1, 4)]
    def part_of(r, coeffs):
        return grid_part(coeffs, cos_ref[r], sin_ref[r], fc_ref[r], fs_ref[r])

    for r in range(3):
        own_ref[r] = grid_rows(
            part_of(r, coef_ref[r]), blocks, lengths[r], scales[r]
        )
    for k in range(steps):
        args = (own_ref, tab_ref, row_ref, col_ref, weight_ref, new_ref, variables)

        @pl.when(me < count - 1)
        def _():
            gather(k, [most[0], most[1], most[2]], turns, *args)

        @pl.when(me == count - 1)
        def _():
            gather(k, [most[1], most[2], 0], turns, *args)

        fresh = new_grid(new_ref, lengths[1], variables)
        if k + 1 < steps:
            mine = analyse_rows(
                fresh, cos_ref[1], sin_ref[1], fc_ref[1], fs_ref[1], coef_scale
            )
            half = total // 2
            all_send[k] = jnp.concatenate([mine[:, :half], mine[:, half:]], axis=0).astype(BF16)

            def hand(source, lat, slot, peer):
                return pltpu.make_async_remote_copy(
                    src_ref=source, dst_ref=all_recv.at[k, lat], send_sem=all_ssem.at[k, slot],
                    recv_sem=all_rsem.at[k, lat], device_id={"wave": peer}, device_id_type=MESH,
                )

            sent = [
                hand(all_send.at[k], me, i, chip * 2 + core) for i, chip in enumerate(others)
            ]
            sent.append(hand(all_send.at[k], me, len(others), mate))
            for copy in sent:
                copy.start()
            if k == 0:
                for copy in gram_copies:
                    copy.wait()
                for i in range(count):
                    for r in range(3):
                        mix_ref[r, :, i * slots : (i + 1) * slots] = g_recv[
                            i, :, r * slots : (r + 1) * slots
                        ]

            def mixed(lat, both, sums):
                both = both.astype(F32)
                both = jnp.concatenate([both[:fields], both[fields:]], axis=1)
                terms = [mix_ref[r, pl.ds(lat, 1), :] * both for r in range(3)]
                return terms if sums is None else [x + y for x, y in zip(sums, terms)]

            near = [chip * 2 + core for chip in reversed(others)]
            for i, lat in enumerate(near):
                hand(all_send.at[k], lat, 0, mate).wait_recv()
                copy = hand(all_recv.at[k, lat], lat, len(others) + 1 + i, mate)
                copy.start()
                sent.append(copy)
            sums = mixed(me, all_send[k], None)
            for lat in near:
                sums = mixed(lat, all_recv[k, lat], sums)
            for lat in [mate] + [chip * 2 + 1 - core for chip in reversed(others)]:
                hand(all_send.at[k], lat, 0, mate).wait_recv()
                sums = mixed(lat, all_recv[k, lat], sums)
            for r in range(3):
                own_ref[r] = grid_rows(
                    part_of(r, sums[r]), blocks, lengths[r], scales[r]
                )
            for copy in sent:
                copy.wait_send()
        else:
            mine_ref[:, :total] = analyse_rows(
                fresh, cos_ref[1], sin_ref[1], fc_ref[1], fs_ref[1], coef_scale
            )
            for i in range(count):
                b_send[i] = jnp.concatenate(
                    [
                        mine_ref[:, i * slots : i * slots + 128],
                        mine_ref[:, i * slots + 128 : i * slots + 256],
                    ],
                    axis=0,
                ).astype(BF16)
            copies = exchange(lambda peer: b_send.at[peer], b_recv, b_ssem, b_rsem)
            b_recv[me] = b_send[me]
            for copy in copies:
                copy.wait()
    out_ref[...] = b_recv[...]


def inverse_kernel(coef_ref, leg_ref, out_hbm, out_ref, out_sem):
    groups, size, _ = leg_ref.shape
    rows_j = size // GROUP
    fields = coef_ref.shape[1] // 2

    def store(g):
        slot_rows = pl.ds(pl.multiple_of(g * GROUP, GROUP), GROUP)
        return pltpu.make_async_copy(out_ref.at[g], out_hbm.at[:, slot_rows, :], out_sem.at[g])

    last = jnp.swapaxes(coef_ref[...].astype(F32), 0, 1)
    row = lax.broadcasted_iota(jnp.int32, (size, fields * GROUP), 0) // rows_j
    col = lax.broadcasted_iota(jnp.int32, (size, fields * GROUP), 1) % GROUP
    own = row == col
    for g in range(groups):
        half, lane = divmod(g * GROUP, 128)
        coefs = jnp.concatenate(
            [last[half * fields + v, :, lane : lane + GROUP] for v in range(fields)], axis=1
        )
        tiled = jnp.concatenate([coefs] * GROUP, axis=0)
        spread = jnp.where(own, tiled, 0.0).T.astype(BF16)
        out = jnp.dot(spread, leg_ref[g], preferred_element_type=F32).astype(BF16)
        out_ref[g] = out.reshape(out_ref.shape[1:])
        store(g).start()
    for g in range(groups):
        store(g).wait()


def fused(spectrum, legendre, order_of_slot, reduced_length, gauss_weight, row, col, weight, count):
    slots, rows_j, degrees = legendre.shape
    fields = 2 * spectrum.shape[0]
    total = order_of_slot.shape[0]
    steps, stencil, grid_width = row.shape[0], row.shape[2], row.shape[-1]
    blocks = -(-(grid_width // SPAN) // 8) * 8
    stride = total // count
    groups = slots // GROUP
    size = GROUP * rows_j
    lanes = -(-slots // 128) * 128
    packed = -(-3 * slots // 256) * 256
    rows_v = fields // 2 * blocks
    half = total // 2
    points = (steps, stencil, 1, grid_width)
    longest = half_rows(count - 1, stride)
    padded = (steps, stencil, 1, max(grid_width, -(-longest // (WIDE // SPAN)) * WIDE))
    coefs, masked = pl.pallas_call(
        functools.partial(steps_kernel, steps, count, fields, slots, stride),
        out_shape=[
            pltpu.VMEM((count, 2 * fields, 128), BF16),
            pltpu.VMEM((groups, size, degrees), BF16),
        ],
        in_specs=[HBM_SPEC] * 8,
        out_specs=[VMEM_SPEC] * 2,
        scratch_shapes=[
            pltpu.VMEM((total,), jnp.int32),
            pltpu.SMEM((total,), jnp.int32),
            pltpu.SMEM(reduced_length.shape, jnp.int32),
            pltpu.SMEM(gauss_weight.shape, F32),
            pltpu.SemaphoreType.DMA((4,)),
            pltpu.VMEM((groups, fields, GROUP, degrees), BF16),
            pltpu.VMEM((groups, size, degrees), BF16),
            pltpu.VMEM(padded, jnp.int32),
            pltpu.VMEM(padded, jnp.int32),
            pltpu.VMEM(padded, F32),
            pltpu.VMEM((groups, rows_j, fields * GROUP), F32),
            pltpu.VMEM((groups, rows_j, size), F32),
            pltpu.VMEM((fields, rows_j, lanes), F32),
            pltpu.VMEM((rows_j, rows_j, lanes), F32),
            pltpu.VMEM((count, fields, packed), F32),
            pltpu.VMEM((3, blocks, total), F32),
            pltpu.VMEM((3, blocks, total), F32),
            pltpu.VMEM((3, SPAN, total), BF16),
            pltpu.VMEM((3, SPAN, total), BF16),
            pltpu.VMEM((SPAN // 8 + 8, total), F32),
            pltpu.VMEM((SPAN // 8 + 8, total), F32),
            pltpu.VMEM((3, fields, total), F32),
            pltpu.VMEM((fields, total + 128), F32),
            pltpu.VMEM((3, rows_j, total), F32),
            pltpu.VMEM((3, rows_v, SPAN), F32),
            pltpu.VMEM((3 * rows_v, SPAN), BF16),
            pltpu.VMEM((rows_v, SPAN), F32),
            pltpu.VMEM((count, 2 * fields, packed // 2), BF16),
            pltpu.VMEM((count, 2 * fields, packed // 2), BF16),
            pltpu.VMEM((count, rows_j, packed), F32),
            pltpu.VMEM((count, rows_j, packed), F32),
            pltpu.VMEM((steps, 2 * fields, half), BF16),
            pltpu.VMEM((steps, count, 2 * fields, half), BF16),
            pltpu.VMEM((count, 2 * fields, 128), BF16),
            pltpu.VMEM((count, 2 * fields, 128), BF16),
            pltpu.SemaphoreType.DMA((2, groups)),
            pltpu.SemaphoreType.DMA((3,)),
        ]
        + [pltpu.SemaphoreType.DMA((count - 1,))] * 4
        + [pltpu.SemaphoreType.DMA((steps, count))] * 2
        + [pltpu.SemaphoreType.DMA((count - 1,))] * 2,
        compiler_params=pltpu.CompilerParams(
            collective_id=0, has_side_effects=True, vmem_limit_bytes=58 * 2**20
        ),
        name="steps",
    )(
        spectrum.reshape(fields, slots, degrees),
        legendre.reshape(groups, size, degrees),
        row.reshape(points), col.reshape(points), weight.reshape(points),
        order_of_slot, reduced_length, gauss_weight,
    )
    out = pl.pallas_call(
        inverse_kernel,
        out_shape=jax.ShapeDtypeStruct((fields, slots, degrees), BF16),
        in_specs=[VMEM_SPEC, VMEM_SPEC],
        out_specs=pl.BlockSpec(memory_space=pl.ANY),
        scratch_shapes=[
            pltpu.VMEM((groups, fields, GROUP, degrees), BF16),
            pltpu.SemaphoreType.DMA((groups,)),
        ],
        compiler_params=pltpu.CompilerParams(vmem_limit_bytes=24 * 2**20),
        name="inverse",
    )(coefs, masked)
    return out.reshape(spectrum.shape)


def per_device(
    spectrum,
    legendre,
    order_of_slot,
    reduced_length,
    gauss_weight,
    depart_row,
    depart_col,
    depart_weight,
):
    own_index = lax.axis_index("wave")
    count = lax.axis_size("wave")
    slot_count = legendre.shape[0]
    orders_total = order_of_slot.shape[0]
    variables, level_count = spectrum.shape[:2]
    assert level_count == 1
    steps = depart_row.shape[0]
    grid_width = depart_row.shape[-1]
    stencil = depart_row.shape[2]
    fields = variables
    real_blocks = grid_width // BLOCK
    blocks = padded_blocks(grid_width)

    stride = orders_total // count
    longest = half_rows(count - 1, stride)
    fits = (
        slot_count % GROUP == 0 and 128 < slot_count <= 256 and 2 * fields == 8
        and legendre.shape[1] == 8 and count == 8 and stride == slot_count
        and orders_total % 256 == 0 and orders_total * grid_width < 2**24
        and grid_width % SPAN == 0 and grid_width // SPAN <= 24
        and -(-longest // (WIDE // SPAN)) * (WIDE // SPAN) <= -(-(grid_width // SPAN) // 8) * 8
    )
    if fits:
        return fused(
            spectrum, legendre, order_of_slot, reduced_length, gauss_weight,
            depart_row, depart_col, depart_weight, count,
        )

    length = lax.dynamic_index_in_dim(reduced_length, own_index, keepdims=False)
    own_orders = lax.dynamic_slice_in_dim(order_of_slot, own_index * slot_count, slot_count)
    degrees = jnp.arange(legendre.shape[2], dtype=jnp.int32)
    masked = jnp.where(
        degrees[None, None, :] >= own_orders[:, None, None], legendre, jnp.zeros((), BF16)
    )
    order_limit = jnp.minimum(orders_total, (length - 1) // 2)
    cos_rows, sin_rows = phase_rows(length, order_of_slot, blocks)
    active = (order_of_slot < order_limit).astype(F32)[None, :]
    fc, fs = pl.pallas_call(
        build_table,
        out_shape=[jax.ShapeDtypeStruct((BLOCK, orders_total), BF16)] * 2,
        in_specs=[VMEM_SPEC] * 3,
        out_specs=[VMEM_SPEC] * 2,
        scratch_shapes=[pltpu.VMEM((RADIX * RADIX, orders_total), F32)] * 2,
        name="table",
    )(cos_rows, sin_rows, active)
    length1 = length.reshape(1)
    grid_scale = (1.0 / jnp.sqrt(order_limit.astype(F32))).reshape(1)
    coef_scale = (gauss_weight[0] * jnp.sqrt(2.0 / length.astype(F32))).reshape(1)

    synth = pl.pallas_call(
        functools.partial(synth_kernel, blocks),
        out_shape=jax.ShapeDtypeStruct((fields * blocks, BLOCK), BF16),
        in_specs=[VMEM_SPEC] * 5 + [SMEM_SPEC] * 2,
        out_specs=VMEM_SPEC,
        name="synth",
    )
    grid_step = pl.pallas_call(
        functools.partial(grid_kernel, fields, blocks, real_blocks),
        out_shape=jax.ShapeDtypeStruct((2 * fields, orders_total), BF16),
        in_specs=[VMEM_SPEC] * 8 + [SMEM_SPEC] * 2,
        out_specs=VMEM_SPEC,
        scratch_shapes=[pltpu.VMEM((fields * blocks, BLOCK), F32)],
        name="grid_step",
    )
    spectral = spectrum.reshape(2 * fields, slot_count, -1)
    fourier = jnp.einsum("vsn,sjn->jvs", spectral, masked, preferred_element_type=F32)
    gram = jnp.einsum("sjn,skn->sjk", masked, masked, preferred_element_type=F32)
    forward = [(i, i + 1) for i in range(count - 1)]
    backward = [(i + 1, i) for i in range(count - 1)]
    for k in range(steps):
        gathered = lax.all_to_all(fourier.astype(BF16), "wave", split_axis=0, concat_axis=2, tiled=True)
        own = synth(
            gathered.reshape(2 * fields, orders_total), cos_rows, sin_rows, fc, fs, length1, grid_scale
        )
        low = lax.ppermute(own, "wave", forward)
        high = lax.ppermute(own, "wave", backward)
        coeffs = grid_step(
            jnp.concatenate([low, own, high], axis=0),
            depart_row[k].reshape(1, stencil, 1, grid_width),
            depart_col[k].reshape(1, stencil, 1, grid_width),
            depart_weight[k].reshape(1, stencil, 1, grid_width),
            cos_rows, sin_rows, fc, fs, length1, coef_scale,
        )
        returned = lax.all_to_all(
            coeffs.reshape(1, 2 * fields, orders_total), "wave", split_axis=2, concat_axis=0, tiled=True
        )
        if k + 1 < steps:
            fourier = jnp.einsum("jvs,sjk->kvs", returned.astype(F32), gram, precision="highest")
    final = jnp.einsum("jvs,sjn->vsn", returned, masked, preferred_element_type=F32).astype(BF16)
    return final.reshape(spectrum.shape)


def solution(mesh):
    placed = (
        P(None, "lev", None, "wave", None),
        P("wave", None, None),
        P(),
        P(),
        P("wave"),
        P(None, "lev", None, "wave", None),
        P(None, "lev", None, "wave", None),
        P(None, "lev", None, "wave", None),
    )
    return jax.shard_map(
        per_device,
        mesh=mesh,
        in_specs=placed,
        out_specs=P(None, "lev", None, "wave", None),
        check_vma=False,
    )
```

```python
import functools
import math

import jax
import jax.numpy as jnp
from jax import lax
from jax.experimental import pallas as pl
from jax.experimental.pallas import tpu as pltpu
from jax.sharding import PartitionSpec as P

BLOCK = 512
RADIX = 8
FULL_TURN = 2.0 * math.pi
F32 = jnp.float32
BF16 = jnp.bfloat16

VMEM_SPEC = pl.BlockSpec(memory_space=pltpu.VMEM)
SMEM_SPEC = pl.BlockSpec(memory_space=pltpu.SMEM)


def padded_blocks(grid_width):
    return -(-(grid_width // BLOCK) // 16) * 16


def phase_rows(length, orders, blocks):
    digits = jnp.arange(RADIX, dtype=jnp.int32)
    steps = [digits, digits * RADIX, digits * RADIX * RADIX]
    steps.append(jnp.arange(blocks, dtype=jnp.int32) * BLOCK)
    steps = jnp.concatenate(steps)
    phases = steps[:, None] * orders[None, :] % length
    angles = phases.astype(F32) * (jnp.float32(FULL_TURN) / length.astype(F32))
    return jnp.cos(angles), jnp.sin(angles)


def build_table(cos_ref, sin_ref, active_ref, fc_ref, fs_ref, ca_ref, sa_ref):
    active = active_ref[...]
    cos_low = cos_ref[0:RADIX, :] * active
    sin_low = sin_ref[0:RADIX, :] * active
    cos_mid = cos_ref[RADIX : 2 * RADIX, :]
    sin_mid = sin_ref[RADIX : 2 * RADIX, :]
    for a in range(RADIX):
        c = cos_ref[2 * RADIX + a : 2 * RADIX + a + 1, :]
        s = sin_ref[2 * RADIX + a : 2 * RADIX + a + 1, :]
        ca_ref[a * RADIX : (a + 1) * RADIX, :] = c * cos_mid - s * sin_mid
        sa_ref[a * RADIX : (a + 1) * RADIX, :] = s * cos_mid + c * sin_mid

    def body(i, carry):
        cos_parts, sin_parts = [], []
        for k in range(2):
            c = ca_ref[pl.ds(2 * i + k, 1), :]
            s = sa_ref[pl.ds(2 * i + k, 1), :]
            cos_parts.append(c * cos_low - s * sin_low)
            sin_parts.append(-(s * cos_low + c * sin_low))
        rows = pl.ds(pl.multiple_of(i * 2 * RADIX, 2 * RADIX), 2 * RADIX)
        fc_ref[rows, :] = jnp.concatenate(cos_parts, axis=0).astype(BF16)
        fs_ref[rows, :] = jnp.concatenate(sin_parts, axis=0).astype(BF16)
        return carry

    lax.fori_loop(0, RADIX * RADIX // 2, body, 0)


def synthesize(coeffs, cos_block, sin_block, fc_ref, fs_ref, length, scale):
    fields = coeffs.shape[0] // 2
    blocks = cos_block.shape[0]
    reals, imags = [], []
    for v in range(fields):
        real = coeffs[2 * v : 2 * v + 1]
        imag = coeffs[2 * v + 1 : 2 * v + 2]
        reals.append((real * cos_block - imag * sin_block).astype(BF16))
        imags.append((real * sin_block + imag * cos_block).astype(BF16))
    dims = (((1,), (1,)), ((), ()))
    out = lax.dot_general(
        jnp.concatenate(reals, axis=0), fc_ref[...], dims, preferred_element_type=F32
    ) + lax.dot_general(
        jnp.concatenate(imags, axis=0), fs_ref[...], dims, preferred_element_type=F32
    )
    row = lax.broadcasted_iota(jnp.int32, out.shape, 0) % blocks
    point = row * BLOCK + lax.broadcasted_iota(jnp.int32, out.shape, 1)
    return jnp.where(point < length, out * scale, 0.0)


def synth_kernel(blocks, coef_ref, cos_ref, sin_ref, fc_ref, fs_ref, len_ref, scale_ref, out_ref):
    out_ref[...] = synthesize(
        coef_ref[...].astype(F32),
        cos_ref[3 * RADIX : 3 * RADIX + blocks, :],
        sin_ref[3 * RADIX : 3 * RADIX + blocks, :],
        fc_ref,
        fs_ref,
        len_ref[0],
        scale_ref[0],
    ).astype(BF16)


def gather_block(b, k, table, row_ref, col_ref, weight_ref, fields, blocks):
    stencil = col_ref.shape[1]
    half = 256
    lanes = pl.ds(pl.multiple_of(b * BLOCK, BLOCK), BLOCK)
    iota_half = lax.broadcasted_iota(jnp.int32, (half, BLOCK), 0).astype(F32).astype(BF16)
    iota_rows = lax.broadcasted_iota(jnp.int32, (3 * blocks, BLOCK), 0)
    one = jnp.ones((), BF16)
    zero = jnp.zeros((), BF16)
    acc = [jnp.zeros((blocks, BLOCK), F32) for _ in range(fields)]
    for p in range(stencil):
        col = col_ref[k, p, :, lanes]
        row = row_ref[k, p, :, lanes]
        weight = weight_ref[k, p, :, lanes]
        point = col % BLOCK
        halves = []
        for h in range(BLOCK // half):
            local = point - h * half
            key = jnp.where((local >= 0) & (local < half), local, -1).astype(F32).astype(BF16)
            halves.append(jnp.where(iota_half == key, one, zero))
        onehot = jnp.concatenate(halves, axis=0)
        found = jnp.dot(table, onehot, preferred_element_type=F32)
        which = (row + 1) * blocks + col // BLOCK
        chosen = jnp.where(iota_rows == which, weight, 0.0)
        for r in range(3):
            sel = chosen[r * blocks : (r + 1) * blocks]
            for v in range(fields):
                start = (r * fields + v) * blocks
                acc[v] = acc[v] + found[start : start + blocks] * sel
    return [jnp.sum(a, axis=0, keepdims=True) for a in acc]


def advance(table, k, row_ref, col_ref, weight_ref, new_ref, length, fields, blocks, real_blocks):
    new_ref[...] = jnp.zeros_like(new_ref)

    def body(b, carry):
        interp = gather_block(b, k, table, row_ref, col_ref, weight_ref, fields, blocks)
        point = b * BLOCK + lax.broadcasted_iota(jnp.int32, (1, BLOCK), 1)
        for v in range(fields):
            value = interp[v] + 0.5 * interp[(v + 1) % fields] * jnp.tanh(interp[(v + 2) % fields])
            new_ref[pl.ds(v * blocks + b, 1), :] = jnp.where(point < length, value, 0.0)
        return carry

    lax.fori_loop(0, real_blocks, body, 0)


def analyse(new_ref, cos_block, sin_block, fc_ref, fs_ref, scale):
    blocks = cos_block.shape[0]
    fields = new_ref.shape[0] // blocks
    newgrid = new_ref[...].astype(BF16)
    part_real = jnp.dot(newgrid, fc_ref[...], preferred_element_type=F32)
    part_imag = jnp.dot(newgrid, fs_ref[...], preferred_element_type=F32)
    out = []
    for v in range(fields):
        pr = part_real[v * blocks : (v + 1) * blocks]
        pi = part_imag[v * blocks : (v + 1) * blocks]
        real = jnp.sum(pr * cos_block + pi * sin_block, axis=0, keepdims=True)
        imag = jnp.sum(pi * cos_block - pr * sin_block, axis=0, keepdims=True)
        out += [real * scale, imag * scale]
    return out


def grid_kernel(
    fields, blocks, real_blocks,
    table_ref, row_ref, col_ref, weight_ref, cos_ref, sin_ref, fc_ref, fs_ref, len_ref, scale_ref,
    out_ref, new_ref,
):
    advance(
        table_ref[...], 0, row_ref, col_ref, weight_ref, new_ref, len_ref[0],
        fields, blocks, real_blocks,
    )
    rows = analyse(
        new_ref,
        cos_ref[3 * RADIX : 3 * RADIX + blocks, :],
        sin_ref[3 * RADIX : 3 * RADIX + blocks, :],
        fc_ref,
        fs_ref,
        scale_ref[0],
    )
    out_ref[...] = jnp.concatenate(rows, axis=0).astype(BF16)


SPAN = 256
WIDE = 6 * SPAN
GROUP = 16
MESH = pl.DeviceIdType.MESH
HBM_SPEC = pl.BlockSpec(memory_space=pltpu.HBM)


def half_rows(lat, stride):
    return (20 + 4 * ((lat + 1) * stride - 1) + SPAN - 1) // SPAN


def unit_turns(steps, orders, length):
    product = steps * orders
    inverse = 1.0 / length
    rest = product - jnp.floor(product * inverse + 0.5) * length
    x = rest * (inverse * (0.25 * FULL_TURN))
    y = x * x
    s = x * (1.0 + y * (-1.0 / 6 + y * (1.0 / 120 + y * (-1.0 / 5040 + y * (1.0 / 362880)))))
    c = 1.0 + y * (-0.5 + y * (1.0 / 24 + y * (-1.0 / 720 + y * (1.0 / 40320))))
    s, c = 2.0 * s * c, 1.0 - 2.0 * s * s
    return 1.0 - 2.0 * s * s, 2.0 * s * c


def tables(p, orders, length, limit, cos_ref, sin_ref, fc_ref, fs_ref, ca_ref, sa_ref):
    shape = (8, orders.shape[1])
    digit = lax.broadcasted_iota(jnp.int32, shape, 0)
    digit_f = digit.astype(F32)
    length_f = jnp.full(shape, length.astype(F32))
    orders_f = jnp.broadcast_to(orders.astype(F32), shape)
    active = jnp.where(orders_f < limit.astype(F32), 1.0, 0.0)
    cos_b, sin_b = unit_turns(digit_f * SPAN, orders_f, length_f)
    mixed = jnp.where(digit < 4, digit_f * 64, (digit_f - 4.0) * (8 * SPAN))
    cos_h, sin_h = unit_turns(mixed, orders_f, length_f)
    cos_ref[p, 0:8, :] = cos_b
    sin_ref[p, 0:8, :] = sin_b
    for t in range(1, cos_ref.shape[1] // 8):
        c, s = cos_h[4 + t : 5 + t], sin_h[4 + t : 5 + t]
        cos_ref[p, 8 * t : 8 * t + 8, :] = c * cos_b - s * sin_b
        sin_ref[p, 8 * t : 8 * t + 8, :] = s * cos_b + c * sin_b
    cos_m, sin_m = unit_turns(digit_f * 8, orders_f, length_f)
    for t in range(SPAN // 64):
        c, s = cos_h[t : t + 1], sin_h[t : t + 1]
        ca_ref[8 * t : 8 * t + 8, :] = c * cos_m - s * sin_m
        sa_ref[8 * t : 8 * t + 8, :] = s * cos_m + c * sin_m
    cos_low, sin_low = unit_turns(digit_f, orders_f, length_f)
    ca_ref[SPAN // 8 : SPAN // 8 + 8, :] = cos_low * active
    sa_ref[SPAN // 8 : SPAN // 8 + 8, :] = sin_low * active

    def body(i, carry):
        cos_l = ca_ref[SPAN // 8 : SPAN // 8 + 8, :]
        sin_l = sa_ref[SPAN // 8 : SPAN // 8 + 8, :]
        cos_parts, sin_parts = [], []
        for k in range(2):
            c = ca_ref[pl.ds(2 * i + k, 1), :]
            s = sa_ref[pl.ds(2 * i + k, 1), :]
            cos_parts.append(c * cos_l - s * sin_l)
            sin_parts.append(-(s * cos_l + c * sin_l))
        rows = pl.ds(pl.multiple_of(i * 16, 16), 16)
        fc_ref[p, rows, :] = jnp.concatenate(cos_parts, axis=0).astype(BF16)
        fs_ref[p, rows, :] = jnp.concatenate(sin_parts, axis=0).astype(BF16)
        return carry

    lax.fori_loop(0, SPAN // 16, body, 0)


def grid_part(coeffs, cos_block, sin_block, fc, fs):
    variables = coeffs.shape[0] // 2
    reals, imags = [], []
    for v in range(variables):
        real = coeffs[2 * v : 2 * v + 1]
        imag = coeffs[2 * v + 1 : 2 * v + 2]
        reals.append((real * cos_block - imag * sin_block).astype(BF16))
        imags.append((real * sin_block + imag * cos_block).astype(BF16))
    dims = (((1,), (1,)), ((), ()))
    return lax.dot_general(
        fc, jnp.concatenate(reals, axis=0), dims, preferred_element_type=F32
    ) + lax.dot_general(
        fs, jnp.concatenate(imags, axis=0), dims, preferred_element_type=F32
    )


def grid_rows(part, blocks, length, scale):
    out = part.T
    row = lax.broadcasted_iota(jnp.int32, out.shape, 0) % blocks
    point = row * SPAN + lax.broadcasted_iota(jnp.int32, out.shape, 1)
    return jnp.where(point < length, out * scale, 0.0)


def pick_wide(b, k, table, most, row_ref, col_ref, weight_ref, variables):
    stencil = col_ref.shape[1]
    lanes = pl.ds(pl.multiple_of(b * WIDE, WIDE), WIDE)
    iota = lax.broadcasted_iota(jnp.int32, (SPAN, WIDE), 0).astype(F32).astype(BF16)
    sub = lax.broadcasted_iota(jnp.int32, (8, WIDE), 0)
    one = jnp.ones((), BF16)
    zero = jnp.zeros((), BF16)
    starts = [sum(most[:r]) if most[r] else 1024 for r in range(3)]
    acc = [None] * variables
    for p in range(stencil):
        col = col_ref[k, p, :, lanes]
        row = row_ref[k, p, :, lanes]
        weight = weight_ref[k, p, :, lanes]
        key = (col & (SPAN - 1)).astype(F32).astype(BF16)
        onehot = jnp.where(iota == key, one, zero)
        found = jnp.dot(table, onehot, preferred_element_type=F32)
        base = jnp.where(row < 0, starts[0], jnp.where(row > 0, starts[2], starts[1]))
        which = base + (col // SPAN)
        got = [jnp.zeros((8, WIDE), F32) for _ in range(variables)]
        for q in range(table.shape[0] // (8 * variables)):
            hit = sub == which - 8 * q
            for v in range(variables):
                start = (q * variables + v) * 8
                got[v] = jnp.where(hit, found[start : start + 8], got[v])
        for v in range(variables):
            term = got[v] * weight
            acc[v] = term if p == 0 else acc[v] + term
    return [jnp.sum(a, axis=0, keepdims=True) for a in acc]


def gather(k, most, turns, own_ref, tab_ref, row_ref, col_ref, weight_ref, new_ref, variables):
    blocks = own_ref.shape[1] // variables
    fill = -sum(most) % 8
    groups = (sum(most) + fill) // 8
    lists = []
    for v in range(variables):
        rows = [own_ref[r, v * blocks : v * blocks + most[r], :] for r in range(3) if most[r]]
        if fill:
            rows.append(jnp.zeros((fill, SPAN), F32))
        lists.append(jnp.concatenate(rows, axis=0))
    parts = [lists[v][8 * t : 8 * t + 8] for t in range(groups) for v in range(variables)]
    size = 8 * len(parts)
    tab_ref[0:size, :] = jnp.concatenate(parts, axis=0).astype(BF16)

    def body(b, carry):
        interp = pick_wide(
            b, k, tab_ref[0:size, :], most, row_ref, col_ref, weight_ref, variables
        )
        for v in range(variables):
            for t in range(WIDE // SPAN):
                new_ref[pl.ds(v * blocks + b * (WIDE // SPAN) + t, 1), :] = interp[v][
                    :, t * SPAN : (t + 1) * SPAN
                ]
        return carry

    lax.fori_loop(0, turns, body, 0)


def new_grid(new_ref, length, variables):
    blocks = new_ref.shape[0] // variables
    interp = [new_ref[v * blocks : (v + 1) * blocks, :] for v in range(variables)]
    shape = interp[0].shape
    point = lax.broadcasted_iota(jnp.int32, shape, 0) * SPAN + lax.broadcasted_iota(jnp.int32, shape, 1)
    inside = point < length
    out = []
    for v in range(variables):
        value = interp[v] + 0.5 * interp[(v + 1) % variables] * jnp.tanh(interp[(v + 2) % variables])
        out.append(jnp.where(inside, value, 0.0))
    return jnp.concatenate(out, axis=0).astype(BF16)


def analyse_rows(newgrid, cos_block, sin_block, fc, fs, scale):
    blocks = cos_block.shape[0]
    part_real = jnp.dot(newgrid, fc, preferred_element_type=F32)
    part_imag = jnp.dot(newgrid, fs, preferred_element_type=F32)
    out = []
    for v in range(newgrid.shape[0] // blocks):
        pr = part_real[v * blocks : (v + 1) * blocks]
        pi = part_imag[v * blocks : (v + 1) * blocks]
        real = jnp.sum(pr * cos_block + pi * sin_block, axis=0, keepdims=True)
        imag = jnp.sum(pi * cos_block - pr * sin_block, axis=0, keepdims=True)
        out += [real * scale, imag * scale]
    return jnp.concatenate(out, axis=0)


def order_rows(first, orders_ref):
    sub = lax.broadcasted_iota(jnp.int32, (8, 128), 0)
    parts = []
    for t in range(GROUP // 8):
        part = jnp.full((8, 128), orders_ref[first + 8 * t], jnp.int32)
        for i in range(1, 8):
            part = jnp.where(sub == i, orders_ref[first + 8 * t + i], part)
        parts.append(part)
    return jnp.concatenate(parts, axis=0)[:, :1]


def own_slots(both, rows_j, width, inner):
    size = GROUP * rows_j
    row = lax.broadcasted_iota(jnp.int32, (size, width), 0) // rows_j
    col = lax.broadcasted_iota(jnp.int32, (size, width), 1)
    col = col % GROUP if inner else col // rows_j
    return jnp.sum(jnp.where(row == col, both, 0.0).reshape(GROUP, rows_j, width), axis=0)


def forward_group(g, first, fields, rows_j, spec_ref, leg_ref, orders_ref, four_ref):
    degrees = spec_ref.shape[3]
    degree = lax.broadcasted_iota(jnp.int32, (GROUP, degrees), 1)
    keep = jnp.where(degree >= order_rows(first + g * GROUP, orders_ref), 1.0, 0.0).astype(BF16)
    state = jnp.concatenate([spec_ref[g, v] * keep for v in range(fields)], axis=0)
    both = lax.dot_general(
        leg_ref[g], state, (((1,), (1,)), ((), ())), preferred_element_type=F32
    )
    four_ref[g] = own_slots(both, rows_j, fields * GROUP, True)


def gram_group(g, first, rows_j, leg_ref, orders_ref, square_ref, masked_ref):
    degrees = leg_ref.shape[2]
    degree = lax.broadcasted_iota(jnp.int32, (2 * rows_j, degrees), 1)
    sub = lax.broadcasted_iota(jnp.int32, (2 * rows_j, 128), 0)
    parts = []
    for pair in range(GROUP // 2):
        slot = first + g * GROUP + 2 * pair
        order = jnp.where(sub < rows_j, orders_ref[slot], orders_ref[slot + 1])[:, :1]
        keep = jnp.where(degree >= order, 1.0, 0.0).astype(BF16)
        parts.append(leg_ref[g, 2 * pair * rows_j : 2 * (pair + 1) * rows_j, :] * keep)
    masked = jnp.concatenate(parts, axis=0)
    masked_ref[g] = masked
    both = lax.dot_general(
        leg_ref[g], masked, (((1,), (1,)), ((), ())), preferred_element_type=F32
    )
    square_ref[g] = own_slots(both, rows_j, GROUP * rows_j, False)


def gram_of(square_ref, gram_ref, rows_j):
    groups, _, size = square_ref.shape
    row = lax.broadcasted_iota(jnp.int32, (size, size), 0)
    col = lax.broadcasted_iota(jnp.int32, (size, size), 1)
    swap = (row // rows_j == col % GROUP) & (row % rows_j == col // GROUP)
    turned = jnp.dot(
        square_ref[...].reshape(groups * rows_j, size), jnp.where(swap, 1.0, 0.0),
        preferred_element_type=F32, precision="highest",
    )
    for h in range(groups):
        rows = turned[h * rows_j : (h + 1) * rows_j]
        for j in range(rows_j):
            gram_ref[j, :, h * GROUP : (h + 1) * GROUP] = rows[:, j * GROUP : (j + 1) * GROUP]


def steps_kernel(
    steps, count, fields, slots, stride,
    spec_hbm, leg_hbm, row_hbm, col_hbm, weight_hbm, order_hbm, len_hbm, gauss_hbm,
    out_ref, masked_ref,
    orders_ref, order_ref, len_ref, gauss_ref, small_sem,
    spec_ref, leg_ref, row_ref, col_ref, weight_ref,
    four_ref, square_ref, vjs_ref, gram_ref, pack_ref,
    cos_ref, sin_ref, fc_ref, fs_ref, ca_ref, sa_ref,
    coef_ref, mine_ref, mix_ref, own_ref, tab_ref, new_ref,
    a_send, a_recv, g_send, g_recv, all_send, all_recv, b_send, b_recv,
    load_sem, point_sem, a_ssem, a_rsem, g_ssem, g_rsem, all_ssem, all_rsem, b_ssem, b_rsem,
):
    rows_j = leg_ref.shape[1] // GROUP
    groups = slots // GROUP
    variables = fields // 2
    total = orders_ref.shape[0]
    blocks = cos_ref.shape[1]
    cut = 3 * slots

    def loads(g):
        slot_rows = pl.ds(pl.multiple_of(g * GROUP, GROUP), GROUP)
        return (
            pltpu.make_async_copy(leg_hbm.at[g], leg_ref.at[g], load_sem.at[0, g]),
            pltpu.make_async_copy(spec_hbm.at[:, slot_rows, :], spec_ref.at[g], load_sem.at[1, g]),
        )

    width = row_hbm.shape[3]
    points = [
        pltpu.make_async_copy(row_hbm, row_ref.at[..., :width], point_sem.at[0]),
        pltpu.make_async_copy(col_hbm, col_ref.at[..., :width], point_sem.at[1]),
        pltpu.make_async_copy(weight_hbm, weight_ref.at[..., :width], point_sem.at[2]),
    ]
    me = lax.axis_index("wave")
    upper = me // (count // 2)
    peers = []
    for i in range(count - 1):
        rising = i + (i - me + count) // count
        falling = count - 1 - i - (i + 1 + me) // count
        peers.append(upper * rising + (1 - upper) * falling)
    core, place, chips = lax.rem(me, 2), me // 2, count // 2
    mate = me + 1 - 2 * core
    others = []
    for i in range(chips - 1):
        rising = i + (i - place + chips) // chips
        falling = chips - 1 - i - (i + 1 + place) // chips
        others.append(upper * rising + (1 - upper) * falling)
    small = [
        pltpu.make_async_copy(order_hbm, orders_ref, small_sem.at[0]),
        pltpu.make_async_copy(order_hbm, order_ref, small_sem.at[1]),
        pltpu.make_async_copy(len_hbm, len_ref, small_sem.at[2]),
        pltpu.make_async_copy(gauss_hbm, gauss_ref, small_sem.at[3]),
    ]
    for copy in small:
        copy.start()
    barrier = pltpu.get_barrier_semaphore()
    for peer in peers:
        pl.semaphore_signal(barrier, inc=1, device_id={"wave": peer}, device_id_type=MESH)
    for copy in small:
        copy.wait()
    for g in range(groups):
        for copy in loads(g):
            copy.start()
    for copy in points:
        copy.start()
    if row_ref.shape[3] > width:
        for ref in (row_ref, col_ref, weight_ref):
            ref[..., width:] = jnp.zeros(ref.shape[:3] + (ref.shape[3] - width,), ref.dtype)
    vjs_ref[...] = jnp.zeros_like(vjs_ref)
    gram_ref[...] = jnp.zeros_like(gram_ref)
    pack_ref[...] = jnp.zeros_like(pack_ref)
    new_ref[...] = jnp.zeros_like(new_ref)
    coef_ref[...] = jnp.zeros_like(coef_ref)
    mine_ref[...] = jnp.zeros_like(mine_ref)
    orders = orders_ref[...].reshape(1, total)
    lats = [jnp.clip(me + r - 1, 0, count - 1) for r in range(3)]
    lengths = [len_ref[lat] for lat in lats]
    limits = [jnp.minimum(total, (length - 1) // 2) for length in lengths]
    first = me * slots

    for r in range(3):
        tables(
            r, orders, lengths[r], limits[r], cos_ref, sin_ref, fc_ref, fs_ref, ca_ref, sa_ref
        )

    for g in range(groups):
        for copy in loads(g):
            copy.wait()
    for g in range(groups):
        forward_group(g, first, fields, rows_j, spec_ref, leg_ref, order_ref, four_ref)
    for h in range(groups):
        for v in range(fields):
            vjs_ref[v, :, h * GROUP : (h + 1) * GROUP] = four_ref[
                h, :, v * GROUP : (v + 1) * GROUP
            ]

    def pack(source, send):
        for p in range(count):
            for r in range(3):
                pack_ref[p, :, r * slots : (r + 1) * slots] = source[
                    min(max(p + r - 1, 0), count - 1)
                ][:, :slots]
        for p in range(count):
            send(p)

    def send_first(p):
        half = pack_ref.shape[2] // 2
        a_send[p] = jnp.concatenate(
            [pack_ref[p, :, :half], pack_ref[p, :, half:]], axis=0
        ).astype(BF16)

    def send_gram(p):
        g_send[p] = pack_ref[p]

    def exchange(send, recv, ssem, rsem):
        copies = []
        for peer in peers:
            d = lax.rem(peer - me + count, count) - 1
            copy = pltpu.make_async_remote_copy(
                src_ref=send(peer), dst_ref=recv.at[me], send_sem=ssem.at[d],
                recv_sem=rsem.at[d], device_id={"wave": peer}, device_id_type=MESH,
            )
            copy.start()
            copies.append(copy)
        return copies

    pack(jnp.swapaxes(vjs_ref[...], 0, 1), send_first)
    pl.semaphore_wait(barrier, count - 1)
    copies = exchange(lambda peer: a_send.at[peer], a_recv, a_ssem, a_rsem)
    a_recv[me] = a_send[me]

    def gram(g, carry):
        gram_group(g, first, rows_j, leg_ref, order_ref, square_ref, masked_ref)
        return carry

    lax.fori_loop(0, groups, gram, 0, unroll=2)
    gram_of(square_ref, gram_ref, rows_j)
    pack(gram_ref[...], send_gram)
    for copy in copies:
        copy.wait()
    gram_copies = exchange(lambda peer: g_send.at[peer], g_recv, g_ssem, g_rsem)
    g_recv[me] = g_send[me]
    for copy in points:
        copy.wait()
    for i in range(count):
        half = a_recv.shape[2]
        both = a_recv[i].astype(F32)
        both = jnp.concatenate([both[:fields], both[fields:]], axis=1)
        for r in range(3):
            coef_ref[r, :, i * slots : (i + 1) * slots] = both[:, r * slots : (r + 1) * slots]

    shape = (1, total)
    coef_scale = gauss_ref[0] * jnp.sqrt(2.0 / jnp.full(shape, lengths[1].astype(F32)))
    inside = [jnp.where(me > 0, 1.0, 0.0), 1.0, jnp.where(me < count - 1, 1.0, 0.0)]
    scales = [
        inside[r] / jnp.sqrt(jnp.full((1, SPAN), limits[r].astype(F32))) for r in range(3)
    ]
    turns = (half_rows(me, stride) + WIDE // SPAN - 1) // (WIDE // SPAN)
    most = [half_rows(count - 4 + r, stride) for r in range(1, 4)]
    def part_of(r, coeffs):
        return grid_part(coeffs, cos_ref[r], sin_ref[r], fc_ref[r], fs_ref[r])

    for r in range(3):
        own_ref[r] = grid_rows(
            part_of(r, coef_ref[r]), blocks, lengths[r], scales[r]
        )
    for k in range(steps):
        args = (own_ref, tab_ref, row_ref, col_ref, weight_ref, new_ref, variables)

        @pl.when(me < count - 2)
        def _():
            gather(k, [half_rows(count - 4, stride), most[0], most[1]], turns, *args)

        @pl.when(me == count - 2)
        def _():
            gather(k, [most[0], most[1], most[2]], turns, *args)

        @pl.when(me == count - 1)
        def _():
            gather(k, [most[1], most[2], 0], turns, *args)

        fresh = new_grid(new_ref, lengths[1], variables)
        if k + 1 < steps:
            mine = analyse_rows(
                fresh, cos_ref[1], sin_ref[1], fc_ref[1], fs_ref[1], coef_scale
            )
            half = total // 2
            all_send[k] = jnp.concatenate([mine[:, :half], mine[:, half:]], axis=0).astype(BF16)

            def hand(source, lat, slot, peer):
                return pltpu.make_async_remote_copy(
                    src_ref=source, dst_ref=all_recv.at[k, lat], send_sem=all_ssem.at[k, slot],
                    recv_sem=all_rsem.at[k, lat], device_id={"wave": peer}, device_id_type=MESH,
                )

            sent = [
                hand(all_send.at[k], me, i, chip * 2 + core) for i, chip in enumerate(others)
            ]
            sent.append(hand(all_send.at[k], me, len(others), mate))
            for copy in sent:
                copy.start()
            if k == 0:
                for copy in gram_copies:
                    copy.wait()
                for i in range(count):
                    for r in range(3):
                        mix_ref[r, :, i * slots : (i + 1) * slots] = g_recv[
                            i, :, r * slots : (r + 1) * slots
                        ]

            def mixed(lat, both, sums):
                both = both.astype(F32)
                both = jnp.concatenate([both[:fields], both[fields:]], axis=1)
                terms = [mix_ref[r, pl.ds(lat, 1), :] * both for r in range(3)]
                return terms if sums is None else [x + y for x, y in zip(sums, terms)]

            near = [chip * 2 + core for chip in reversed(others)]
            for i, lat in enumerate(near):
                hand(all_send.at[k], lat, 0, mate).wait_recv()
                copy = hand(all_recv.at[k, lat], lat, len(others) + 1 + i, mate)
                copy.start()
                sent.append(copy)
            sums = mixed(me, all_send[k], None)
            for lat in near:
                sums = mixed(lat, all_recv[k, lat], sums)
            for lat in [mate] + [chip * 2 + 1 - core for chip in reversed(others)]:
                hand(all_send.at[k], lat, 0, mate).wait_recv()
                sums = mixed(lat, all_recv[k, lat], sums)
            for r in range(3):
                own_ref[r] = grid_rows(
                    part_of(r, sums[r]), blocks, lengths[r], scales[r]
                )
            for copy in sent:
                copy.wait_send()
        else:
            mine_ref[:, :total] = analyse_rows(
                fresh, cos_ref[1], sin_ref[1], fc_ref[1], fs_ref[1], coef_scale
            )
            for i in range(count):
                b_send[i] = jnp.concatenate(
                    [
                        mine_ref[:, i * slots : i * slots + 128],
                        mine_ref[:, i * slots + 128 : i * slots + 256],
                    ],
                    axis=0,
                ).astype(BF16)
            copies = exchange(lambda peer: b_send.at[peer], b_recv, b_ssem, b_rsem)
            b_recv[me] = b_send[me]
            for copy in copies:
                copy.wait()
    out_ref[...] = b_recv[...]


def inverse_kernel(coef_ref, leg_ref, out_hbm, out_ref, out_sem):
    groups, size, _ = leg_ref.shape
    rows_j = size // GROUP
    fields = coef_ref.shape[1] // 2

    def store(g):
        slot_rows = pl.ds(pl.multiple_of(g * GROUP, GROUP), GROUP)
        return pltpu.make_async_copy(out_ref.at[g], out_hbm.at[:, slot_rows, :], out_sem.at[g])

    last = jnp.swapaxes(coef_ref[...].astype(F32), 0, 1)
    row = lax.broadcasted_iota(jnp.int32, (size, fields * GROUP), 0) // rows_j
    col = lax.broadcasted_iota(jnp.int32, (size, fields * GROUP), 1) % GROUP
    own = row == col
    for g in range(groups):
        half, lane = divmod(g * GROUP, 128)
        coefs = jnp.concatenate(
            [last[half * fields + v, :, lane : lane + GROUP] for v in range(fields)], axis=1
        )
        tiled = jnp.concatenate([coefs] * GROUP, axis=0)
        spread = jnp.where(own, tiled, 0.0).T.astype(BF16)
        out = jnp.dot(spread, leg_ref[g], preferred_element_type=F32).astype(BF16)
        out_ref[g] = out.reshape(out_ref.shape[1:])
        store(g).start()
    for g in range(groups):
        store(g).wait()


def fused(spectrum, legendre, order_of_slot, reduced_length, gauss_weight, row, col, weight, count):
    slots, rows_j, degrees = legendre.shape
    fields = 2 * spectrum.shape[0]
    total = order_of_slot.shape[0]
    steps, stencil, grid_width = row.shape[0], row.shape[2], row.shape[-1]
    blocks = -(-(grid_width // SPAN) // 8) * 8
    stride = total // count
    groups = slots // GROUP
    size = GROUP * rows_j
    lanes = -(-slots // 128) * 128
    packed = -(-3 * slots // 256) * 256
    rows_v = fields // 2 * blocks
    half = total // 2
    points = (steps, stencil, 1, grid_width)
    longest = half_rows(count - 1, stride)
    padded = (steps, stencil, 1, max(grid_width, -(-longest // (WIDE // SPAN)) * WIDE))
    coefs, masked = pl.pallas_call(
        functools.partial(steps_kernel, steps, count, fields, slots, stride),
        out_shape=[
            pltpu.VMEM((count, 2 * fields, 128), BF16),
            pltpu.VMEM((groups, size, degrees), BF16),
        ],
        in_specs=[HBM_SPEC] * 8,
        out_specs=[VMEM_SPEC] * 2,
        scratch_shapes=[
            pltpu.VMEM((total,), jnp.int32),
            pltpu.SMEM((total,), jnp.int32),
            pltpu.SMEM(reduced_length.shape, jnp.int32),
            pltpu.SMEM(gauss_weight.shape, F32),
            pltpu.SemaphoreType.DMA((4,)),
            pltpu.VMEM((groups, fields, GROUP, degrees), BF16),
            pltpu.VMEM((groups, size, degrees), BF16),
            pltpu.VMEM(padded, jnp.int32),
            pltpu.VMEM(padded, jnp.int32),
            pltpu.VMEM(padded, F32),
            pltpu.VMEM((groups, rows_j, fields * GROUP), F32),
            pltpu.VMEM((groups, rows_j, size), F32),
            pltpu.VMEM((fields, rows_j, lanes), F32),
            pltpu.VMEM((rows_j, rows_j, lanes), F32),
            pltpu.VMEM((count, fields, packed), F32),
            pltpu.VMEM((3, blocks, total), F32),
            pltpu.VMEM((3, blocks, total), F32),
            pltpu.VMEM((3, SPAN, total), BF16),
            pltpu.VMEM((3, SPAN, total), BF16),
            pltpu.VMEM((SPAN // 8 + 8, total), F32),
            pltpu.VMEM((SPAN // 8 + 8, total), F32),
            pltpu.VMEM((3, fields, total), F32),
            pltpu.VMEM((fields, total + 128), F32),
            pltpu.VMEM((3, rows_j, total), F32),
            pltpu.VMEM((3, rows_v, SPAN), F32),
            pltpu.VMEM((3 * rows_v, SPAN), BF16),
            pltpu.VMEM((rows_v, SPAN), F32),
            pltpu.VMEM((count, 2 * fields, packed // 2), BF16),
            pltpu.VMEM((count, 2 * fields, packed // 2), BF16),
            pltpu.VMEM((count, rows_j, packed), F32),
            pltpu.VMEM((count, rows_j, packed), F32),
            pltpu.VMEM((steps, 2 * fields, half), BF16),
            pltpu.VMEM((steps, count, 2 * fields, half), BF16),
            pltpu.VMEM((count, 2 * fields, 128), BF16),
            pltpu.VMEM((count, 2 * fields, 128), BF16),
            pltpu.SemaphoreType.DMA((2, groups)),
            pltpu.SemaphoreType.DMA((3,)),
        ]
        + [pltpu.SemaphoreType.DMA((count - 1,))] * 4
        + [pltpu.SemaphoreType.DMA((steps, count))] * 2
        + [pltpu.SemaphoreType.DMA((count - 1,))] * 2,
        compiler_params=pltpu.CompilerParams(
            collective_id=0, has_side_effects=True, vmem_limit_bytes=58 * 2**20
        ),
        name="steps",
    )(
        spectrum.reshape(fields, slots, degrees),
        legendre.reshape(groups, size, degrees),
        row.reshape(points), col.reshape(points), weight.reshape(points),
        order_of_slot, reduced_length, gauss_weight,
    )
    out = pl.pallas_call(
        inverse_kernel,
        out_shape=jax.ShapeDtypeStruct((fields, slots, degrees), BF16),
        in_specs=[VMEM_SPEC, VMEM_SPEC],
        out_specs=pl.BlockSpec(memory_space=pl.ANY),
        scratch_shapes=[
            pltpu.VMEM((groups, fields, GROUP, degrees), BF16),
            pltpu.SemaphoreType.DMA((groups,)),
        ],
        compiler_params=pltpu.CompilerParams(vmem_limit_bytes=24 * 2**20),
        name="inverse",
    )(coefs, masked)
    return out.reshape(spectrum.shape)


def per_device(
    spectrum,
    legendre,
    order_of_slot,
    reduced_length,
    gauss_weight,
    depart_row,
    depart_col,
    depart_weight,
):
    own_index = lax.axis_index("wave")
    count = lax.axis_size("wave")
    slot_count = legendre.shape[0]
    orders_total = order_of_slot.shape[0]
    variables, level_count = spectrum.shape[:2]
    assert level_count == 1
    steps = depart_row.shape[0]
    grid_width = depart_row.shape[-1]
    stencil = depart_row.shape[2]
    fields = variables
    real_blocks = grid_width // BLOCK
    blocks = padded_blocks(grid_width)

    stride = orders_total // count
    longest = half_rows(count - 1, stride)
    fits = (
        slot_count % GROUP == 0 and 128 < slot_count <= 256 and 2 * fields == 8
        and legendre.shape[1] == 8 and count == 8 and stride == slot_count
        and orders_total % 256 == 0 and orders_total * grid_width < 2**24
        and grid_width % SPAN == 0 and grid_width // SPAN <= 24
        and -(-longest // (WIDE // SPAN)) * (WIDE // SPAN) <= -(-(grid_width // SPAN) // 8) * 8
    )
    if fits:
        return fused(
            spectrum, legendre, order_of_slot, reduced_length, gauss_weight,
            depart_row, depart_col, depart_weight, count,
        )

    length = lax.dynamic_index_in_dim(reduced_length, own_index, keepdims=False)
    own_orders = lax.dynamic_slice_in_dim(order_of_slot, own_index * slot_count, slot_count)
    degrees = jnp.arange(legendre.shape[2], dtype=jnp.int32)
    masked = jnp.where(
        degrees[None, None, :] >= own_orders[:, None, None], legendre, jnp.zeros((), BF16)
    )
    order_limit = jnp.minimum(orders_total, (length - 1) // 2)
    cos_rows, sin_rows = phase_rows(length, order_of_slot, blocks)
    active = (order_of_slot < order_limit).astype(F32)[None, :]
    fc, fs = pl.pallas_call(
        build_table,
        out_shape=[jax.ShapeDtypeStruct((BLOCK, orders_total), BF16)] * 2,
        in_specs=[VMEM_SPEC] * 3,
        out_specs=[VMEM_SPEC] * 2,
        scratch_shapes=[pltpu.VMEM((RADIX * RADIX, orders_total), F32)] * 2,
        name="table",
    )(cos_rows, sin_rows, active)
    length1 = length.reshape(1)
    grid_scale = (1.0 / jnp.sqrt(order_limit.astype(F32))).reshape(1)
    coef_scale = (gauss_weight[0] * jnp.sqrt(2.0 / length.astype(F32))).reshape(1)

    synth = pl.pallas_call(
        functools.partial(synth_kernel, blocks),
        out_shape=jax.ShapeDtypeStruct((fields * blocks, BLOCK), BF16),
        in_specs=[VMEM_SPEC] * 5 + [SMEM_SPEC] * 2,
        out_specs=VMEM_SPEC,
        name="synth",
    )
    grid_step = pl.pallas_call(
        functools.partial(grid_kernel, fields, blocks, real_blocks),
        out_shape=jax.ShapeDtypeStruct((2 * fields, orders_total), BF16),
        in_specs=[VMEM_SPEC] * 8 + [SMEM_SPEC] * 2,
        out_specs=VMEM_SPEC,
        scratch_shapes=[pltpu.VMEM((fields * blocks, BLOCK), F32)],
        name="grid_step",
    )
    spectral = spectrum.reshape(2 * fields, slot_count, -1)
    fourier = jnp.einsum("vsn,sjn->jvs", spectral, masked, preferred_element_type=F32)
    gram = jnp.einsum("sjn,skn->sjk", masked, masked, preferred_element_type=F32)
    forward = [(i, i + 1) for i in range(count - 1)]
    backward = [(i + 1, i) for i in range(count - 1)]
    for k in range(steps):
        gathered = lax.all_to_all(fourier.astype(BF16), "wave", split_axis=0, concat_axis=2, tiled=True)
        own = synth(
            gathered.reshape(2 * fields, orders_total), cos_rows, sin_rows, fc, fs, length1, grid_scale
        )
        low = lax.ppermute(own, "wave", forward)
        high = lax.ppermute(own, "wave", backward)
        coeffs = grid_step(
            jnp.concatenate([low, own, high], axis=0),
            depart_row[k].reshape(1, stencil, 1, grid_width),
            depart_col[k].reshape(1, stencil, 1, grid_width),
            depart_weight[k].reshape(1, stencil, 1, grid_width),
            cos_rows, sin_rows, fc, fs, length1, coef_scale,
        )
        returned = lax.all_to_all(
            coeffs.reshape(1, 2 * fields, orders_total), "wave", split_axis=2, concat_axis=0, tiled=True
        )
        if k + 1 < steps:
            fourier = jnp.einsum("jvs,sjk->kvs", returned.astype(F32), gram, precision="highest")
    final = jnp.einsum("jvs,sjn->vsn", returned, masked, preferred_element_type=F32).astype(BF16)
    return final.reshape(spectrum.shape)


def solution(mesh):
    placed = (
        P(None, "lev", None, "wave", None),
        P("wave", None, None),
        P(),
        P(),
        P("wave"),
        P(None, "lev", None, "wave", None),
        P(None, "lev", None, "wave", None),
        P(None, "lev", None, "wave", None),
    )
    return jax.shard_map(
        per_device,
        mesh=mesh,
        in_specs=placed,
        out_specs=P(None, "lev", None, "wave", None),
        check_vma=False,
    )
```
